32 devices in a mesh: fsdp: 16 (over z, y, x), tensor: 2 (over core).
Axes of the slice: x: 2, y: 2, z: 4, core: 2. Of those that a mesh axis runs over, the one named last changes fastest.
Arguments:
- tokens: bfloat16 [64, 577, 1024], P(('fsdp', 'tensor')), may hold values from -6 to 6
- cotangent: bfloat16 [64, 577, 1024], P(('fsdp', 'tensor')), may hold values from -6 to 6
- adapter_index: int32 [64], P('fsdp'), may hold values from 0 to 7
- filled: int32 [64], P('fsdp'), may hold values 0 or 1
- ln1_gain: bfloat16 [1024], replicated, may hold values from 0.5 to 1.5
- ln1_shift: bfloat16 [1024], replicated, may hold values from -2 to 2
- qkv_weight: bfloat16 [1024, 3, 1024], P('fsdp', None, 'tensor'), may hold values from -0.1875 to 0.1875
- qv_bias: bfloat16 [2, 1024], replicated, may hold values from -3 to 3
- out_weight: bfloat16 [1024, 1024], P('tensor', 'fsdp'), may hold values from -0.75 to 0.75
- out_bias: bfloat16 [1024], replicated, may hold values from -3 to 3
- ln2_gain: bfloat16 [1024], replicated, may hold values from 0.5 to 1.5
- ln2_shift: bfloat16 [1024], replicated, may hold values from -2 to 2
- fc1_weight: bfloat16 [1024, 4096], P('fsdp', 'tensor'), may hold values from -0.1875 to 0.1875
- fc1_bias: bfloat16 [4096], replicated, may hold values from -3 to 3
- fc2_weight: bfloat16 [4096, 1024], P('tensor', 'fsdp'), may hold values from -0.09375 to 0.09375
- fc2_bias: bfloat16 [1024], replicated, may hold values from -3 to 3
- qkv_down: bfloat16 [8, 16, 1024], P(None, None, ('fsdp', 'tensor')), may hold values from -0.1875 to 0.1875
- qkv_up: bfloat16 [8, 16, 3072], P(None, None, ('fsdp', 'tensor')), may hold values from -0.75 to 0.75
- out_down: bfloat16 [8, 16, 1024], P(None, None, ('fsdp', 'tensor')), may hold values from -0.75 to 0.75
- out_up: bfloat16 [8, 16, 1024], P(None, None, ('fsdp', 'tensor')), may hold values from -0.75 to 0.75
- fc1_down: bfloat16 [8, 16, 1024], P(None, None, ('fsdp', 'tensor')), may hold values from -0.1875 to 0.1875
- fc1_up: bfloat16 [8, 16, 4096], P(None, None, ('fsdp', 'tensor')), may hold values from -0.75 to 0.75
- fc2_down: bfloat16 [8, 16, 4096], P(None, None, ('fsdp', 'tensor')), may hold values from -0.1875 to 0.1875
- fc2_up: bfloat16 [8, 16, 1024], P(None, None, ('fsdp', 'tensor')), may hold values from -0.75 to 0.75
Outputs:
- outputs: bfloat16 [64, 577, 1024], P(('fsdp', 'tensor'))
- input_grad: float32 [64, 577, 1024], P(('fsdp', 'tensor'))
- grad_qkv_down: float32 [8, 16, 1024], P(None, None, ('fsdp', 'tensor'))
- grad_qkv_up: float32 [8, 16, 3072], P(None, None, ('fsdp', 'tensor'))
- grad_out_down: float32 [8, 16, 1024], P(None, None, ('fsdp', 'tensor'))
- grad_out_up: float32 [8, 16, 1024], P(None, None, ('fsdp', 'tensor'))
- grad_fc1_down: float32 [8, 16, 1024], P(None, None, ('fsdp', 'tensor'))
- grad_fc1_up: float32 [8, 16, 4096], P(None, None, ('fsdp', 'tensor'))
- grad_fc2_down: float32 [8, 16, 4096], P(None, None, ('fsdp', 'tensor'))
- grad_fc2_up: float32 [8, 16, 1024], P(None, None, ('fsdp', 'tensor'))
The draws below stay inside these ranges and needn't reach their ends.
All inputs are finite; a program needn't handle non-finite values. No bound on the sum of `filled` on one device may be relied on, other than what follows from the above.
Results may differ from the reference program's by a relative error of at most 0.014.
Values may be sent and summed in bfloat16 or wider, within the bound.
No kernel may reach another device: no remote copies, remote signals or barrier semaphores. Data moves between devices by JAX's collectives and lax.ppermute only.
A program may use at most 256 MiB of HBM per device.

```python
import jax
import jax.numpy as jnp
from jax import lax

D = 1024
HEADS = 16
HEAD_DIM = 64
FF = 4096
SEQ = 577
RANK = 16
ADAPTERS = 8
IMAGES = 64


def set_ends(entries, key, smallest, high):
    shape = entries.shape
    spot = [jax.random.randint(jax.random.fold_in(key, axis), (), 0, shape[axis]) for axis in range(len(shape))]
    entries = entries.at[tuple(spot)].set(smallest)
    longest = shape.index(max(shape))
    spot[longest] = (spot[longest] + 1) % shape[longest]
    return entries.at[tuple(spot)].set(high)


def levels(key, extent, pieces, low, high):
    gain, own = 1.0, jax.random.fold_in(key, 6)
    for axis_at, shards_of in pieces:
        steps = jnp.exp(jax.random.uniform(jax.random.fold_in(own, axis_at), (shards_of,), jnp.float32, low / len(pieces), high / len(pieces)))
        gain = gain * jnp.repeat(steps, extent[axis_at] // shards_of).reshape([-1 if axis == axis_at else 1 for axis in range(len(extent))])
    return gain


def gaussian(key, shape, width, reach, split=(), kind=jnp.bfloat16):
    gain = levels(key, shape, split, -0.22, 0.18) if split else 1.0
    entries = jax.random.normal(key, shape, jnp.float32) * width * gain
    return jnp.minimum(jnp.maximum(entries, -reach), reach).astype(kind)


def setup_inputs(seed: int = 0) -> dict:
    arg_keys = jax.random.split(jax.random.key(seed), 25)
    return {
        "tokens": gaussian(arg_keys[0], (IMAGES, SEQ, D), 1.0, 6.0, ((0, 32),)),
        "cotangent": gaussian(arg_keys[1], (IMAGES, SEQ, D), 1.0, 6.0, ((0, 32),)),
        "adapter_index": set_ends(jax.random.randint(arg_keys[2], (IMAGES,), 0, ADAPTERS), jax.random.fold_in(arg_keys[2], 1), 0, ADAPTERS - 1).astype(jnp.int32),
        "filled": set_ends((jax.random.randint(arg_keys[3], (IMAGES,), 0, 8) < 7).astype(jnp.int32), jax.random.fold_in(arg_keys[3], 1), 0, 1),
        "ln1_gain": jnp.clip(1.0 + 0.1 * jax.random.normal(arg_keys[4], (D,), jnp.float32), 0.5, 1.5).astype(jnp.bfloat16),
        "ln1_shift": gaussian(arg_keys[5], (D,), 0.3, 2.0),
        "qkv_weight": gaussian(arg_keys[6], (D, 3, D), D ** -0.5, 0.1875, ((0, 16), (2, 2))),
        "qv_bias": gaussian(arg_keys[7], (2, D), 0.5, 3.0),
        "out_weight": gaussian(arg_keys[8], (D, D), (D // 16) ** -0.5, 0.75, ((0, 2), (1, 16))),
        "out_bias": gaussian(arg_keys[9], (D,), 0.5, 3.0),
        "ln2_gain": jnp.clip(1.0 + 0.1 * jax.random.normal(arg_keys[10], (D,), jnp.float32), 0.5, 1.5).astype(jnp.bfloat16),
        "ln2_shift": gaussian(arg_keys[11], (D,), 0.3, 2.0),
        "fc1_weight": gaussian(arg_keys[12], (D, FF), D ** -0.5, 0.1875, ((0, 16), (1, 2))),
        "fc1_bias": gaussian(arg_keys[13], (FF,), 0.5, 3.0),
        "fc2_weight": gaussian(arg_keys[14], (FF, D), FF ** -0.5, 0.09375, ((0, 2), (1, 16))),
        "fc2_bias": gaussian(arg_keys[15], (D,), 0.5, 3.0),
        "qkv_down": gaussian(arg_keys[16], (ADAPTERS, RANK, D), D ** -0.5, 0.1875, ((2, 32),)),
        "qkv_up": gaussian(arg_keys[17], (ADAPTERS, RANK, 3 * D), (RANK * 4) ** -0.5, 0.75, ((2, 32),)),
        "out_down": gaussian(arg_keys[18], (ADAPTERS, RANK, D), (D // 16) ** -0.5, 0.75, ((2, 32),)),
        "out_up": gaussian(arg_keys[19], (ADAPTERS, RANK, D), (RANK * 4) ** -0.5, 0.75, ((2, 32),)),
        "fc1_down": gaussian(arg_keys[20], (ADAPTERS, RANK, D), D ** -0.5, 0.1875, ((2, 32),)),
        "fc1_up": gaussian(arg_keys[21], (ADAPTERS, RANK, FF), (RANK * 4) ** -0.5, 0.75, ((2, 32),)),
        "fc2_down": gaussian(arg_keys[22], (ADAPTERS, RANK, FF), (FF // 4) ** -0.5, 0.1875, ((2, 32),)),
        "fc2_up": gaussian(arg_keys[23], (ADAPTERS, RANK, D), (RANK * 4) ** -0.5, 0.75, ((2, 32),)),
    }


@jax.custom_vjp
def low(v):
    return lax.optimization_barrier(v.astype(jnp.bfloat16)).astype(jnp.float32)

@jax.custom_vjp
def low_back(v):
    return v

def low_keep(v):
    return (low(v), None)

def low_pass(kept, grad):
    return (grad,)

def back_keep(v):
    return (v, None)

def back_low(kept, grad):
    return (low(grad),)
low.defvjp(low_keep, low_pass)
low_back.defvjp(back_keep, back_low)
epsilon = 1e-05
highest = lax.Precision.HIGHEST

def layer_norm(values, gain_row, shift_row):
    center = values - lax.optimization_barrier(jnp.mean(values, axis=-1, keepdims=True))
    inverse = lax.rsqrt(lax.optimization_barrier(jnp.mean(center * center, axis=-1, keepdims=True)) + epsilon)
    return center * inverse * gain_row + shift_row

def matmul(left, right):
    return jnp.dot(left, right, precision=highest, preferred_element_type=jnp.float32)

def low_rank_map(inputs, down_sel, up_sel):
    middle = low_back(low(jnp.einsum('isw,irw->isr', inputs, down_sel, precision=highest)))
    return jnp.einsum('isr,irw->isw', middle, up_sel, precision=highest)

def attend(blocks):
    queries, key_rows, value_rows = blocks
    score_scale = HEAD_DIM ** (-0.5)
    scores = low_back(jnp.einsum('qhd,khd->hqk', queries, key_rows, precision=highest) * score_scale)
    prob_rows = jax.nn.softmax(scores, axis=-1)
    return jnp.einsum('hqk,khd->qhd', low(prob_rows), value_rows, precision=highest)

def reference(tokens, cotangent, adapter_index, filled, ln1_gain, ln1_shift, qkv_weight, qv_bias, out_weight, out_bias, ln2_gain, ln2_shift, fc1_weight, fc1_bias, fc2_weight, fc2_bias, qkv_down, qkv_up, out_down, out_up, fc1_down, fc1_up, fc2_down, fc2_up):
    choose = (adapter_index[:, None] == jnp.arange(ADAPTERS, dtype=jnp.int32)[None, :]).astype(jnp.float32)
    mask_rows = filled.astype(jnp.float32)[:, None, None]
    gain_one = ln1_gain.astype(jnp.float32)
    shift_one = ln1_shift.astype(jnp.float32)
    gain_two = ln2_gain.astype(jnp.float32)
    shift_two = ln2_shift.astype(jnp.float32)
    qkv_full = qkv_weight.astype(jnp.float32).reshape(D, 3 * D)
    bias_pair = qv_bias.astype(jnp.float32)
    bias_full = jnp.concatenate([bias_pair[0], jnp.zeros((D,), jnp.float32), bias_pair[1]])
    out_full = out_weight.astype(jnp.float32)
    out_shift = out_bias.astype(jnp.float32)
    first_full = fc1_weight.astype(jnp.float32)
    first_shift = fc1_bias.astype(jnp.float32)
    second_full = fc2_weight.astype(jnp.float32)
    second_shift = fc2_bias.astype(jnp.float32)

    def forward(inputs, adapters):
        chosen = [jnp.einsum('ie,erw->irw', choose, stacked, precision=highest) for stacked in adapters]
        normed_low = low(layer_norm(inputs, gain_one, shift_one))
        projected = matmul(normed_low.reshape(IMAGES * SEQ, D), qkv_full).reshape(IMAGES, SEQ, 3 * D)
        projected = projected + low_rank_map(normed_low, chosen[0], chosen[1]) + bias_full
        projected = projected.reshape(IMAGES, SEQ, 3, HEADS, HEAD_DIM)
        queries = low_back(low(projected[:, :, 0]))
        key_rows = low_back(low(projected[:, :, 1]))
        value_rows = low_back(low(projected[:, :, 2]))
        mixed_rows = lax.map(jax.checkpoint(attend), (queries, key_rows, value_rows)).reshape(IMAGES, SEQ, D)
        mixed_rows = low_back(low(mixed_rows))
        branch_one = matmul(mixed_rows.reshape(IMAGES * SEQ, D), out_full).reshape(IMAGES, SEQ, D)
        branch_one = low_back(branch_one + out_shift + low_rank_map(mixed_rows, chosen[2], chosen[3]))
        middle = inputs + mask_rows * branch_one
        normed_two = low(layer_norm(middle, gain_two, shift_two))
        before = matmul(normed_two.reshape(IMAGES * SEQ, D), first_full).reshape(IMAGES, SEQ, FF)
        before = low_back(before + first_shift + low_rank_map(normed_two, chosen[4], chosen[5]))
        activated = low(jax.nn.gelu(before, approximate=False))
        branch_two = matmul(activated.reshape(IMAGES * SEQ, FF), second_full).reshape(IMAGES, SEQ, D)
        branch_two = low_back(branch_two + second_shift + low_rank_map(activated, chosen[6], chosen[7]))
        return middle + mask_rows * branch_two
    adapter_list = tuple((stacked.astype(jnp.float32) for stacked in (qkv_down, qkv_up, out_down, out_up, fc1_down, fc1_up, fc2_down, fc2_up)))
    outputs, pullback = jax.vjp(forward, tokens.astype(jnp.float32), adapter_list)
    input_grad, adapter_grads = pullback(cotangent.astype(jnp.float32))
    return (outputs.astype(jnp.bfloat16), input_grad, adapter_grads[0], adapter_grads[1], adapter_grads[2], adapter_grads[3], adapter_grads[4], adapter_grads[5], adapter_grads[6], adapter_grads[7])
```

```python
from functools import partial

import jax
import jax.numpy as jnp
from jax import lax
from jax.sharding import PartitionSpec as P

D = 1024
HEADS = 16
HEAD_DIM = 64
FF = 4096
SEQ = 577
RANK = 16
ADAPTERS = 8


epsilon = 1e-05
highest = lax.Precision.HIGHEST


def layer_norm(values, gain_row, shift_row):
    center = values - jnp.mean(values, axis=-1, keepdims=True)
    inverse = lax.rsqrt(jnp.mean(center * center, axis=-1, keepdims=True) + epsilon)
    normed = center * inverse
    return (normed * gain_row + shift_row, normed, inverse)


def norm_back(upstream, normed, inverse, gain_row):
    scaled = upstream * gain_row
    return inverse * (
        scaled
        - jnp.mean(scaled, axis=-1, keepdims=True)
        - normed * jnp.mean(scaled * normed, axis=-1, keepdims=True)
    )


def down_map(inputs, chosen):
    return jnp.einsum("isw,irw->isr", inputs, chosen, preferred_element_type=jnp.float32).astype(
        jnp.bfloat16
    )


def up_map(low_rank, chosen):
    return jnp.einsum("isr,irw->isw", low_rank, chosen, preferred_element_type=jnp.float32)


def outer_grad(low_rank, other_side):
    return jnp.einsum("isr,isw->irw", low_rank, other_side, preferred_element_type=jnp.float32)


def attend(blocks):
    queries, key_rows, value_rows = blocks
    score_scale = HEAD_DIM ** (-0.5)
    scores = (
        jnp.einsum("qhd,khd->hqk", queries, key_rows, preferred_element_type=jnp.float32)
        * score_scale
    )
    log_total = jax.nn.logsumexp(scores, axis=-1)
    prob_rows = jnp.exp(scores - log_total[:, :, None]).astype(jnp.bfloat16)
    mixed_rows = jnp.einsum(
        "hqk,khd->qhd", prob_rows, value_rows, preferred_element_type=jnp.float32
    )
    return (mixed_rows.astype(jnp.bfloat16), log_total)


def attend_back(blocks):
    queries, key_rows, value_rows, log_total, mixed_grad = blocks
    score_scale = HEAD_DIM ** (-0.5)
    scores = (
        jnp.einsum("qhd,khd->hqk", queries, key_rows, preferred_element_type=jnp.float32)
        * score_scale
    )
    prob_rows = jnp.exp(scores - log_total[:, :, None])
    prob_grad = jnp.einsum(
        "qhd,khd->hqk", mixed_grad, value_rows, preferred_element_type=jnp.float32
    )
    value_grad = jnp.einsum(
        "hqk,qhd->khd",
        prob_rows.astype(jnp.bfloat16),
        mixed_grad,
        preferred_element_type=jnp.float32,
    )
    score_grad = (
        prob_rows * (prob_grad - jnp.sum(prob_rows * prob_grad, axis=-1, keepdims=True))
    ).astype(jnp.bfloat16)
    query_grad = (
        jnp.einsum("hqk,khd->qhd", score_grad, key_rows, preferred_element_type=jnp.float32)
        * score_scale
    )
    key_grad = (
        jnp.einsum("hqk,qhd->khd", score_grad, queries, preferred_element_type=jnp.float32)
        * score_scale
    )
    return jnp.stack([query_grad, key_grad, value_grad], axis=1).astype(jnp.bfloat16)


def on_device(
    tokens,
    cotangent,
    adapter_index,
    filled,
    ln1_gain,
    ln1_shift,
    qkv_weight,
    qv_bias,
    out_weight,
    out_bias,
    ln2_gain,
    ln2_shift,
    fc1_weight,
    fc1_bias,
    fc2_weight,
    fc2_bias,
    qkv_down,
    qkv_up,
    out_down,
    out_up,
    fc1_down,
    fc1_up,
    fc2_down,
    fc2_up,
):
    own_images = tokens.shape[0]
    own_start = lax.axis_index("tensor") * own_images
    own_mask = lax.dynamic_slice_in_dim(filled, own_start, own_images, 0).astype(jnp.float32)[
        :, None, None
    ]
    stack_list = (qkv_down, qkv_up, out_down, out_up, fc1_down, fc1_up, fc2_down, fc2_up)
    widths = [stacked.shape[2] for stacked in stack_list]
    packed = lax.all_gather(jnp.concatenate(stack_list, axis=2), ("fsdp", "tensor"), axis=0)
    members = packed.shape[0]
    stacks = []
    offset = 0
    for width in widths:
        part = packed[:, :, :, offset : offset + width]
        stacks.append(part.transpose(1, 2, 0, 3).reshape(ADAPTERS, RANK, members * width))
        offset += width
    rows = qkv_weight.shape[0]
    group = fc1_weight.shape[1]
    column = qkv_weight.shape[2]
    weights = jnp.concatenate(
        [qkv_weight.reshape(rows, 3 * column), out_weight.T, fc1_weight, fc2_weight.T], axis=1
    )
    weights = lax.all_gather(weights, "fsdp", axis=0, tiled=True)
    weights = lax.all_gather(weights, "tensor", axis=0)
    qkv_local = (
        weights[:, :, : 3 * column]
        .reshape(-1, D, 3, column)
        .transpose(1, 2, 0, 3)
        .reshape(D, 3, D)
    )
    out_local = weights[:, :, 3 * column : 4 * column].transpose(0, 2, 1).reshape(D, D)
    first_local = (
        weights[:, :, 4 * column : 4 * column + group].transpose(1, 0, 2).reshape(D, FF)
    )
    second_local = weights[:, :, 4 * column + group :].transpose(0, 2, 1).reshape(FF, D)
    split_count = 1
    member = 0
    work_index = lax.dynamic_slice_in_dim(adapter_index, own_start, own_images, 0)
    local_heads = HEADS // split_count
    local_width = D // split_count
    hidden_width = FF // split_count
    hidden_start = member * hidden_width
    choose = (work_index[:, None] == jnp.arange(ADAPTERS, dtype=jnp.int32)[None, :]).astype(
        jnp.bfloat16
    )

    def select(stacked):
        return jnp.einsum(
            "ie,erw->irw", choose, stacked, preferred_element_type=jnp.float32
        ).astype(jnp.bfloat16)

    def gather_back(per_image):
        return jnp.einsum("ie,irw->erw", choose.astype(jnp.float32), per_image, precision=highest)

    qkv_up_local = stacks[1].reshape(ADAPTERS, RANK, 3, D).reshape(ADAPTERS, RANK, 3 * local_width)
    out_down_local = stacks[2]
    fc1_up_local = stacks[5]
    fc2_down_local = stacks[6]
    sel_qkv_down = select(stacks[0])
    sel_qkv_up = select(qkv_up_local)
    sel_out_down = select(out_down_local)
    sel_out_up = select(stacks[3])
    sel_fc1_down = select(stacks[4])
    sel_fc1_up = select(fc1_up_local)
    sel_fc2_down = select(fc2_down_local)
    sel_fc2_up = select(stacks[7])
    gain_one = ln1_gain.astype(jnp.float32)
    gain_two = ln2_gain.astype(jnp.float32)
    inputs = tokens.astype(jnp.float32)
    normed_one, unit_one, inverse_one = layer_norm(inputs, gain_one, ln1_shift.astype(jnp.float32))
    normed_low = normed_one.astype(jnp.bfloat16)
    images = normed_low.shape[0]
    qkv_flat = qkv_local.reshape(D, 3 * local_width)
    projected = jnp.dot(
        normed_low.reshape(images * SEQ, D), qkv_flat, preferred_element_type=jnp.float32
    ).reshape(images, SEQ, 3 * local_width)
    rank_one = down_map(normed_low, sel_qkv_down)
    bias_rows = qv_bias.astype(jnp.float32)
    bias_full = jnp.concatenate([bias_rows[0], jnp.zeros_like(bias_rows[0]), bias_rows[1]])
    projected = (projected + up_map(rank_one, sel_qkv_up) + bias_full).astype(jnp.bfloat16)
    projected = projected.reshape(images, SEQ, 3, local_heads, HEAD_DIM)
    queries = projected[:, :, 0]
    key_rows = projected[:, :, 1]
    value_rows = projected[:, :, 2]
    heads_out, log_total = lax.map(attend, (queries, key_rows, value_rows))
    mixed_low = heads_out.reshape(images, SEQ, local_width)
    attn_part = jnp.dot(
        mixed_low.reshape(images * SEQ, local_width), out_local, preferred_element_type=jnp.float32
    ).reshape(images, SEQ, D)
    rank_out = down_map(mixed_low, sel_out_down)
    attn_part = attn_part + up_map(rank_out, sel_out_up)
    middle = inputs + own_mask * (attn_part + out_bias.astype(jnp.float32))
    normed_two, unit_two, inverse_two = layer_norm(middle, gain_two, ln2_shift.astype(jnp.float32))
    normed_low_two = normed_two.astype(jnp.bfloat16)
    first_shift = fc1_bias.astype(jnp.float32)
    before = jnp.dot(
        normed_low_two.reshape(images * SEQ, D), first_local, preferred_element_type=jnp.float32
    ).reshape(images, SEQ, hidden_width)
    rank_three = down_map(normed_low_two, sel_fc1_down)
    before = before + up_map(rank_three, sel_fc1_up) + first_shift
    exact_gelu = partial(jax.nn.gelu, approximate=False)
    activated, gelu_back = jax.vjp(exact_gelu, before)
    activated = activated.astype(jnp.bfloat16)
    mlp_part = jnp.dot(
        activated.reshape(images * SEQ, hidden_width),
        second_local,
        preferred_element_type=jnp.float32,
    ).reshape(images, SEQ, D)
    rank_four = down_map(activated, sel_fc2_down)
    mlp_part = mlp_part + up_map(rank_four, sel_fc2_up)
    outputs = (middle + own_mask * (mlp_part + fc2_bias.astype(jnp.float32))).astype(jnp.bfloat16)
    upstream = cotangent.astype(jnp.float32)
    branch_grad_two = (own_mask * upstream).astype(jnp.bfloat16)
    grad_fc2_up_sel = outer_grad(rank_four, branch_grad_two)
    rank_four_grad = down_map(branch_grad_two, sel_fc2_up)
    grad_fc2_down_sel = outer_grad(rank_four_grad, activated)
    act_grad = jnp.dot(
        branch_grad_two.reshape(images * SEQ, D), second_local.T, preferred_element_type=jnp.float32
    ).reshape(images, SEQ, hidden_width)
    act_grad = act_grad + up_map(rank_four_grad, sel_fc2_down)
    pre_grad = gelu_back(act_grad)[0].astype(jnp.bfloat16)
    grad_fc1_up_sel = outer_grad(rank_three, pre_grad)
    rank_three_grad = down_map(pre_grad, sel_fc1_up)
    grad_fc1_down_sel = outer_grad(rank_three_grad, normed_low_two)
    norm_part_two = jnp.dot(
        pre_grad.reshape(images * SEQ, hidden_width),
        first_local.T,
        preferred_element_type=jnp.float32,
    ).reshape(images, SEQ, D)
    norm_part_two = norm_part_two + up_map(rank_three_grad, sel_fc1_down)
    middle_grad = upstream + norm_back(norm_part_two, unit_two, inverse_two, gain_two)
    branch_grad_one = (own_mask * middle_grad).astype(jnp.bfloat16)
    grad_out_up_sel = outer_grad(rank_out, branch_grad_one)
    rank_out_grad = down_map(branch_grad_one, sel_out_up)
    grad_out_down_sel = outer_grad(rank_out_grad, mixed_low)
    mixed_grad = jnp.dot(
        branch_grad_one.reshape(images * SEQ, D), out_local.T, preferred_element_type=jnp.float32
    ).reshape(images, SEQ, local_width)
    mixed_grad = (
        (mixed_grad + up_map(rank_out_grad, sel_out_down))
        .astype(jnp.bfloat16)
        .reshape(images, SEQ, local_heads, HEAD_DIM)
    )
    qkv_grad = lax.map(attend_back, (queries, key_rows, value_rows, log_total, mixed_grad)).reshape(
        images, SEQ, 3 * local_width
    )
    grad_qkv_up_sel = outer_grad(rank_one, qkv_grad)
    rank_one_grad = down_map(qkv_grad, sel_qkv_up)
    grad_qkv_down_sel = outer_grad(rank_one_grad, normed_low)
    norm_part_one = jnp.dot(
        qkv_grad.reshape(images * SEQ, 3 * local_width),
        qkv_flat.T,
        preferred_element_type=jnp.float32,
    ).reshape(images, SEQ, D)
    norm_part_one = norm_part_one + up_map(rank_one_grad, sel_qkv_down)
    input_grad = middle_grad + norm_back(norm_part_one, unit_one, inverse_one, gain_one)
    qkv_up_term = gather_back(grad_qkv_up_sel).reshape(ADAPTERS, RANK, 3, local_width)
    qkv_up_term = qkv_up_term.reshape(ADAPTERS, RANK, 3 * D)
    out_down_term = gather_back(grad_out_down_sel)
    fc1_up_term = gather_back(grad_fc1_up_sel)
    fc2_down_term = lax.dynamic_update_slice_in_dim(
        jnp.zeros((ADAPTERS, RANK, FF), jnp.float32),
        gather_back(grad_fc2_down_sel),
        hidden_start,
        2,
    )
    terms = (
        gather_back(grad_qkv_down_sel),
        qkv_up_term,
        out_down_term,
        gather_back(grad_out_up_sel),
        gather_back(grad_fc1_down_sel),
        fc1_up_term,
        fc2_down_term,
        gather_back(grad_fc2_up_sel),
    )
    packed_terms = jnp.concatenate(
        [
            term.reshape(ADAPTERS, RANK, members, width).transpose(2, 0, 1, 3)
            for term, width in zip(terms, widths)
        ],
        axis=3,
    )
    scattered = lax.psum_scatter(
        packed_terms, ("fsdp", "tensor"), scatter_dimension=0, tiled=False
    )
    summed = []
    offset = 0
    for width in widths:
        summed.append(scattered[:, :, offset : offset + width])
        offset += width
    return (
        outputs,
        input_grad,
        summed[0],
        summed[1],
        summed[2],
        summed[3],
        summed[4],
        summed[5],
        summed[6],
        summed[7],
    )


def solution(mesh):
    in_specs = (
        P(("fsdp", "tensor"), None, None),
        P(("fsdp", "tensor"), None, None),
        P("fsdp"),
        P("fsdp"),
        P(),
        P(),
        P("fsdp", None, "tensor"),
        P(),
        P("tensor", "fsdp"),
        P(),
        P(),
        P(),
        P("fsdp", "tensor"),
        P(),
        P("tensor", "fsdp"),
        P(),
        P(None, None, ("fsdp", "tensor")),
        P(None, None, ("fsdp", "tensor")),
        P(None, None, ("fsdp", "tensor")),
        P(None, None, ("fsdp", "tensor")),
        P(None, None, ("fsdp", "tensor")),
        P(None, None, ("fsdp", "tensor")),
        P(None, None, ("fsdp", "tensor")),
        P(None, None, ("fsdp", "tensor")),
    )
    out_specs = (
        P(("fsdp", "tensor"), None, None),
        P(("fsdp", "tensor"), None, None),
        P(None, None, ("fsdp", "tensor")),
        P(None, None, ("fsdp", "tensor")),
        P(None, None, ("fsdp", "tensor")),
        P(None, None, ("fsdp", "tensor")),
        P(None, None, ("fsdp", "tensor")),
        P(None, None, ("fsdp", "tensor")),
        P(None, None, ("fsdp", "tensor")),
        P(None, None, ("fsdp", "tensor")),
    )
    return jax.shard_map(
        on_device, mesh=mesh, in_specs=in_specs, out_specs=out_specs, check_vma=False
    )
```

```python
from functools import partial

import jax
import jax.numpy as jnp
from jax import lax
from jax.experimental import pallas as pl
from jax.experimental.pallas import tpu as pltpu
from jax.sharding import PartitionSpec as P

D = 1024
HEADS = 16
HEAD_DIM = 64
FF = 4096
SEQ = 577
RANK = 16
ADAPTERS = 8
STACK = ADAPTERS * RANK
TILE = 512

epsilon = 1e-05
bf16 = jnp.bfloat16
f32 = jnp.float32
NN = (((1,), (0,)), ((), ()))
NT = (((1,), (1,)), ((), ()))
TN = (((0,), (0,)), ((), ()))
BOTH = ("fsdp", "tensor")


def dot(left, right, dims):
    return lax.dot_general(left, right, dims, preferred_element_type=f32)


def params():
    return pltpu.CompilerParams(vmem_limit_bytes=60 << 20)


def cost(flops, moved, exps=0):
    return pl.CostEstimate(flops=flops, bytes_accessed=moved, transcendentals=exps)


def smem():
    return pl.BlockSpec(memory_space=pltpu.SMEM)


def whole(shape):
    return pl.BlockSpec(shape, lambda *_: (0,) * len(shape), pipeline_mode=pl.Buffered(1))


def image_rows(width=D):
    return pl.BlockSpec((pl.Squeezed(), SEQ, width), lambda i: (i, 0, 0))


def normalize(values):
    center = values - jnp.mean(values, axis=-1, keepdims=True)
    inverse = lax.rsqrt(jnp.mean(center * center, axis=-1, keepdims=True) + epsilon)
    return center * inverse, inverse


def norm_back(upstream, normed, inverse, gain_row):
    scaled = upstream * gain_row
    return inverse * (
        scaled
        - jnp.mean(scaled, axis=-1, keepdims=True)
        - normed * jnp.mean(scaled * normed, axis=-1, keepdims=True)
    )


def chosen_lanes(adapter):
    lanes = lax.broadcasted_iota(jnp.int32, (1, STACK), 1)
    return (lanes // RANK) == adapter


def keep(product, adapter):
    return jnp.where(chosen_lanes(adapter), product, 0.0).astype(bf16)


def add_to(ref, value, first):
    @pl.when(first)
    def _():
        ref[...] = value

    @pl.when(jnp.logical_not(first))
    def _():
        ref[...] += value


def flat(block):
    return block.reshape(D, block.shape[-1])


def qkv_kernel(
    index_ref, tokens_ref, weight_ref, down_ref, up_ref, bias_ref, gain_ref, shift_ref,
    q_ref, k_ref, v_ref, low_ref, a_s, low_s,
):
    group = pl.program_id(0)
    image = pl.program_id(1)

    @pl.when(group == 0)
    def _():
        normed, _ = normalize(tokens_ref[...].astype(f32))
        a = (normed * gain_ref[...] + shift_ref[...]).astype(bf16)
        a_s[image] = a
        low_s[image] = keep(dot(a, down_ref[...], NN), index_ref[image])

    a = a_s[image]
    low = low_s[image]
    low_ref[...] = low
    width = q_ref.shape[-1]
    weight = flat(weight_ref[...])
    start = pl.multiple_of(group * width, width)
    bias = bias_ref[...].astype(f32)
    for part, out_ref in enumerate((q_ref, k_ref, v_ref)):
        value = dot(a, weight[:, part * width : (part + 1) * width], NN)
        value += dot(low, up_ref[pl.ds(part * D + start, width), :], NT)
        if part != 1:
            value += bias[part // 2 : part // 2 + 1]
        out_ref[...] = value.astype(bf16)


def qkv_project(tokens, weights, down, up, index, bias, gain, shift):
    images = tokens.shape[0]
    members, groups, rows, columns = weights.shape
    width = D // groups
    sq = pl.Squeezed()
    out = pl.BlockSpec((sq, SEQ, width), lambda g, i: (i, 0, g))
    vector = whole((1, D))
    return pl.pallas_call(
        qkv_kernel,
        grid=(groups, images),
        in_specs=[
            smem(),
            pl.BlockSpec((sq, SEQ, D), lambda g, i: (i, 0, 0)),
            pl.BlockSpec((members, sq, rows, 3 * width), lambda g, i: (0, g, 0, 0)),
            whole((D, STACK)),
            whole((3 * D, STACK)),
            pl.BlockSpec((2, width), lambda g, i: (0, g)),
            vector,
            vector,
        ],
        out_specs=[out, out, out, pl.BlockSpec((sq, SEQ, STACK), lambda g, i: (i, 0, 0))],
        out_shape=[jax.ShapeDtypeStruct((images, SEQ, D), bf16)] * 3
        + [jax.ShapeDtypeStruct((images, SEQ, STACK), bf16)],
        scratch_shapes=[
            pltpu.VMEM((images, SEQ, D), bf16),
            pltpu.VMEM((images, SEQ, STACK), bf16),
        ],
        compiler_params=params(),
        cost_estimate=cost(6 * images * SEQ * D * D, 20 << 20),
        name="qkv_project",
    )(index, tokens, weights, down, up, bias, gain, shift)


def attend_kernel(q_ref, k_ref, v_ref, o_ref, w_ref):
    q = q_ref[...]
    k = k_ref[...]
    v = v_ref[...]
    low = lax.broadcasted_iota(jnp.int32, q.shape, 1) < HEAD_DIM
    outs = []
    for head in range(2):
        own = low if head == 0 else jnp.logical_not(low)
        queries = jnp.where(own, q * HEAD_DIM**-0.5, jnp.zeros_like(q)).astype(bf16)
        scores = dot(queries, k, NT)
        top = jnp.max(scores, axis=-1, keepdims=True)
        raised = jnp.exp(scores - top)
        total = jnp.sum(raised, axis=-1, keepdims=True)
        prob = (raised * (1.0 / total)).astype(bf16)
        w_ref[head] = prob
        outs.append(dot(prob, v, NN))
    o_ref[...] = jnp.where(low, outs[0], outs[1]).astype(bf16)


def pair_rows():
    return pl.BlockSpec((pl.Squeezed(), SEQ, 2 * HEAD_DIM), lambda i, h: (i, 0, h))


def pair_weights():
    return pl.BlockSpec((2, SEQ, SEQ), lambda i, h: (i * (HEADS // 2) + h, 0, 0))


def attend(q, k, v):
    images = q.shape[0]
    return pl.pallas_call(
        attend_kernel,
        grid=(images, HEADS // 2),
        in_specs=[pair_rows()] * 3,
        out_specs=[pair_rows(), pair_weights()],
        out_shape=[
            jax.ShapeDtypeStruct((images, SEQ, D), bf16),
            jax.ShapeDtypeStruct((images * HEADS, SEQ, SEQ), bf16),
        ],
        compiler_params=params(),
        cost_estimate=cost(16 * images * SEQ * SEQ * D, 40 << 20, images * HEADS * SEQ * SEQ),
        name="attend",
    )(q, k, v)


def attend_back_kernel(q_ref, k_ref, v_ref, do_ref, w_ref, dq_ref, dk_ref, dv_ref):
    q = q_ref[...]
    k = k_ref[...]
    v = v_ref[...]
    do = do_ref[...]
    low = lax.broadcasted_iota(jnp.int32, q.shape, 1) < HEAD_DIM
    grads = []
    for head in range(2):
        own = low if head == 0 else jnp.logical_not(low)
        mixed_grad = jnp.where(own, do, jnp.zeros_like(do))
        prob_grad = dot(mixed_grad, v, NT)
        prob_low = w_ref[head]
        prob = prob_low.astype(f32)
        inner = jnp.sum(prob * prob_grad, axis=-1, keepdims=True)
        score_grad = (prob * (prob_grad - inner)).astype(bf16)
        grads.append((dot(score_grad, k, NN), dot(score_grad, q, TN), dot(prob_low, do, TN)))
    scale = HEAD_DIM**-0.5
    dq_ref[...] = (jnp.where(low, grads[0][0], grads[1][0]) * scale).astype(bf16)
    dk_ref[...] = (jnp.where(low, grads[0][1], grads[1][1]) * scale).astype(bf16)
    dv_ref[...] = jnp.where(low, grads[0][2], grads[1][2]).astype(bf16)


def attend_back(q, k, v, do, prob):
    images = q.shape[0]
    return pl.pallas_call(
        attend_back_kernel,
        grid=(images, HEADS // 2),
        in_specs=[pair_rows()] * 4 + [pair_weights()],
        out_specs=[pair_rows()] * 3,
        out_shape=[jax.ShapeDtypeStruct((images, SEQ, D), bf16)] * 3,
        compiler_params=params(),
        cost_estimate=cost(32 * images * SEQ * SEQ * D, 48 << 20),
        name="attend_back",
    )(q, k, v, do, prob)


def out_kernel(
    index_ref, filled_ref, tokens_ref, o_ref, weight_ref, down_ref, up_ref, bias_ref,
    h_ref, low_ref,
):
    image = pl.program_id(0)
    o = o_ref[...]
    low = keep(dot(o, down_ref[...], NN), index_ref[image])
    low_ref[...] = low
    value = dot(low, up_ref[...], NT) + bias_ref[...]
    width = weight_ref.shape[-1]
    for group in range(weight_ref.shape[1]):
        weight = flat(weight_ref[:, group])
        value += dot(o[:, group * width : (group + 1) * width], weight, NT)
    h_ref[...] = tokens_ref[...].astype(f32) + filled_ref[image].astype(f32) * value


def out_project(tokens, o, weights, down, up, index, filled, bias):
    images = tokens.shape[0]
    members, groups, rows, width = weights.shape
    return pl.pallas_call(
        out_kernel,
        grid=(images,),
        in_specs=[
            smem(),
            smem(),
            image_rows(),
            image_rows(),
            whole((members, groups, rows, width)),
            whole((D, STACK)),
            whole((D, STACK)),
            whole((1, D)),
        ],
        out_specs=[image_rows(), image_rows(STACK)],
        out_shape=[
            jax.ShapeDtypeStruct((images, SEQ, D), f32),
            jax.ShapeDtypeStruct((images, SEQ, STACK), bf16),
        ],
        compiler_params=params(),
        cost_estimate=cost(2 * images * SEQ * D * D, 12 << 20),
        name="out_project",
    )(index, filled, tokens, o, weights, down, up, bias)


def out_back_kernel(
    index_ref, filled_ref, dh_ref, o_ref, low_ref, weight_ref, down_ref, up_ref,
    do_ref, grad_up_ref, grad_down_ref,
):
    image = pl.program_id(0)
    branch = (dh_ref[...] * filled_ref[image].astype(f32)).astype(bf16)
    low_grad = keep(dot(branch, up_ref[...], NN), index_ref[image])
    width = weight_ref.shape[-1]
    for group in range(weight_ref.shape[1]):
        span = slice(group * width, (group + 1) * width)
        value = dot(branch, flat(weight_ref[:, group]), NN)
        value += dot(low_grad, down_ref[span, :], NT)
        do_ref[:, span] = value.astype(bf16)
    add_to(grad_up_ref, dot(low_ref[...], branch, TN).T, image == 0)
    add_to(grad_down_ref, dot(low_grad, o_ref[...], TN).T, image == 0)


def out_back(dh, o, low, weights, down, up, index, filled):
    images = dh.shape[0]
    members, groups, rows, width = weights.shape
    grad = pl.BlockSpec((D, STACK), lambda i: (0, 0))
    return pl.pallas_call(
        out_back_kernel,
        grid=(images,),
        in_specs=[
            smem(),
            smem(),
            image_rows(),
            image_rows(),
            image_rows(STACK),
            whole((members, groups, rows, width)),
            whole((D, STACK)),
            whole((D, STACK)),
        ],
        out_specs=[image_rows(), grad, grad],
        out_shape=[jax.ShapeDtypeStruct((images, SEQ, D), bf16)]
        + [jax.ShapeDtypeStruct((D, STACK), f32)] * 2,
        compiler_params=params(),
        cost_estimate=cost(2 * images * SEQ * D * D, 12 << 20),
        name="out_back",
    )(index, filled, dh, o, low, weights, down, up)


def mlp_kernel(
    index_ref, filled_ref, h_ref, cot_ref, first_ref, second_ref, down1_ref, up1_ref, down2_ref,
    up2_ref, bias1_ref, bias2_ref, gain_ref, shift_ref,
    out_ref, dh_ref, grad_up2_ref, grad_down2_ref, grad_up1_ref, grad_down1_ref,
    a_s, dz_s, low3_s, dlow4_s, z_s, da_s, low4_s, dlow3_s,
):
    tile = pl.program_id(0)
    image = pl.program_id(1)
    last = tile == pl.num_programs(0) - 1
    adapter = index_ref[image]
    mask = filled_ref[image].astype(f32)

    @pl.when(tile == 0)
    def _():
        normed, _ = normalize(h_ref[image])
        a = (normed * gain_ref[...] + shift_ref[...]).astype(bf16)
        a_s[image] = a
        dz = (cot_ref[image].astype(f32) * mask).astype(bf16)
        dz_s[image] = dz
        low3_s[image] = keep(dot(a, down1_ref[...], NN), adapter)
        dlow4_s[image] = keep(dot(dz, up2_ref[...], NN), adapter)

    a = a_s[image]
    dz = dz_s[image]
    low3 = low3_s[image]
    dlow4 = dlow4_s[image]
    first = flat(first_ref[...])
    second = flat(second_ref[...])
    before = dot(a, first, NN) + dot(low3, up1_ref[...], NT) + bias1_ref[...]
    density = jnp.exp(before * before * -0.5) * 0.3989422804014327
    below = 0.5 * lax.erf(before * 0.7071067811865476) + 0.5
    g = (before * below).astype(bf16)
    slope = below + before * density
    dg = dot(dz, second, NN) + dot(dlow4, down2_ref[...], NT)
    df = (dg * slope).astype(bf16)
    z_part = dot(g, second, NT)
    da_part = dot(df, first, NT)
    low4_part = dot(g, down2_ref[...], NN)
    dlow3_part = dot(df, up1_ref[...], NN)

    @pl.when(tile == 0)
    def _():
        z_s[image] = z_part
        da_s[image] = da_part
        low4_s[image] = low4_part
        dlow3_s[image] = dlow3_part

    @pl.when(tile > 0)
    def _():
        z_s[image] += z_part
        da_s[image] += da_part
        low4_s[image] += low4_part
        dlow3_s[image] += dlow3_part

    add_to(grad_down2_ref, dot(dlow4, g, TN).T, image == 0)
    add_to(grad_up1_ref, dot(low3, df, TN).T, image == 0)

    @pl.when(last)
    def _():
        low4 = keep(low4_s[image], adapter)
        h = h_ref[image]
        z = z_s[image] + dot(low4, up2_ref[...], NT) + bias2_ref[...]
        out_ref[...] = (h + mask * z).astype(bf16)
        add_to(grad_up2_ref, dot(low4, dz, TN).T, image == 0)
        dlow3 = keep(dlow3_s[image], adapter)
        da = da_s[image] + dot(dlow3, down1_ref[...], NT)
        add_to(grad_down1_ref, dot(dlow3, a, TN).T, image == 0)
        normed, inverse = normalize(h)
        dh_ref[...] = cot_ref[image].astype(f32) + norm_back(
            da, normed, inverse, gain_ref[...]
        )


def mlp(h, cot, first, second, down1, up1, down2, up2, index, filled, bias1, bias2, gain, shift):
    images = h.shape[0]
    members, groups, rows, columns = first.shape
    tiles = FF // TILE
    per_group = columns // TILE
    sq = pl.Squeezed()
    weight = pl.BlockSpec(
        (members, sq, rows, TILE), lambda j, i: (0, j // per_group, 0, j % per_group)
    )
    tall = pl.BlockSpec((TILE, STACK), lambda j, i: (j, 0))
    short = pl.BlockSpec((D, STACK), lambda j, i: (0, 0))
    late = pl.BlockSpec((sq, SEQ, D), lambda j, i: (jnp.where(j == tiles - 1, i, 0), 0, 0))
    return pl.pallas_call(
        mlp_kernel,
        grid=(tiles, images),
        in_specs=[
            smem(),
            smem(),
            whole((images, SEQ, D)),
            whole((images, SEQ, D)),
            weight,
            weight,
            whole((D, STACK)),
            tall,
            tall,
            whole((D, STACK)),
            pl.BlockSpec((1, TILE), lambda j, i: (0, j)),
            whole((1, D)),
            whole((1, D)),
            whole((1, D)),
        ],
        out_specs=[late, late, short, tall, tall, short],
        out_shape=[
            jax.ShapeDtypeStruct((images, SEQ, D), bf16),
            jax.ShapeDtypeStruct((images, SEQ, D), f32),
            jax.ShapeDtypeStruct((D, STACK), f32),
            jax.ShapeDtypeStruct((FF, STACK), f32),
            jax.ShapeDtypeStruct((FF, STACK), f32),
            jax.ShapeDtypeStruct((D, STACK), f32),
        ],
        scratch_shapes=[
            pltpu.VMEM((images, SEQ, D), bf16),
            pltpu.VMEM((images, SEQ, D), bf16),
            pltpu.VMEM((images, SEQ, STACK), bf16),
            pltpu.VMEM((images, SEQ, STACK), bf16),
            pltpu.VMEM((images, SEQ, D), f32),
            pltpu.VMEM((images, SEQ, D), f32),
            pltpu.VMEM((images, SEQ, STACK), f32),
            pltpu.VMEM((images, SEQ, STACK), f32),
        ],
        compiler_params=params(),
        cost_estimate=cost(8 * images * SEQ * D * FF, 40 << 20, 2 * images * SEQ * FF),
        name="mlp",
    )(index, filled, h, cot, first, second, down1, up1, down2, up2, bias1, bias2, gain, shift)


def qkv_back_kernel(
    index_ref, tokens_ref, dh_ref, dq_ref, dk_ref, dv_ref, low_ref, weight_ref, down_ref, up_ref,
    gain_ref, shift_ref, grad_ref, grad_up_ref, grad_down_ref,
):
    image = pl.program_id(0)
    normed, inverse = normalize(tokens_ref[...].astype(f32))
    gain = gain_ref[...]
    a = (normed * gain + shift_ref[...]).astype(bf16)
    parts = (dq_ref[...], dk_ref[...], dv_ref[...])
    low_grad = dot(parts[0], up_ref[0:D, :], NN)
    for part in (1, 2):
        low_grad += dot(parts[part], up_ref[part * D : (part + 1) * D, :], NN)
    low_grad = keep(low_grad, index_ref[image])
    da = dot(low_grad, down_ref[...], NT)
    width = weight_ref.shape[-1] // 3
    for group in range(weight_ref.shape[1]):
        weight = flat(weight_ref[:, group])
        for part in range(3):
            da += dot(
                parts[part][:, group * width : (group + 1) * width],
                weight[:, part * width : (part + 1) * width],
                NT,
            )
    low = low_ref[...]
    for part in range(3):
        add_to(
            grad_up_ref.at[part * D : (part + 1) * D, :],
            dot(low, parts[part], TN).T,
            image == 0,
        )
    add_to(grad_down_ref, dot(low_grad, a, TN).T, image == 0)
    grad_ref[...] = dh_ref[...] + norm_back(da, normed, inverse, gain)


def qkv_back(tokens, dh, dq, dk, dv, low, weights, down, up, index, gain, shift):
    images = tokens.shape[0]
    members, groups, rows, columns = weights.shape
    return pl.pallas_call(
        qkv_back_kernel,
        grid=(images,),
        in_specs=[
            smem(),
            image_rows(),
            image_rows(),
            image_rows(),
            image_rows(),
            image_rows(),
            image_rows(STACK),
            whole((members, groups, rows, columns)),
            whole((D, STACK)),
            whole((3 * D, STACK)),
            whole((1, D)),
            whole((1, D)),
        ],
        out_specs=[
            image_rows(),
            pl.BlockSpec((3 * D, STACK), lambda i: (0, 0)),
            pl.BlockSpec((D, STACK), lambda i: (0, 0)),
        ],
        out_shape=[
            jax.ShapeDtypeStruct((images, SEQ, D), f32),
            jax.ShapeDtypeStruct((3 * D, STACK), f32),
            jax.ShapeDtypeStruct((D, STACK), f32),
        ],
        compiler_params=params(),
        cost_estimate=cost(6 * images * SEQ * D * D, 28 << 20),
        name="qkv_back",
    )(index, tokens, dh, dq, dk, dv, low, weights, down, up, gain, shift)


def on_device(
    tokens,
    cotangent,
    adapter_index,
    filled,
    ln1_gain,
    ln1_shift,
    qkv_weight,
    qv_bias,
    out_weight,
    out_bias,
    ln2_gain,
    ln2_shift,
    fc1_weight,
    fc1_bias,
    fc2_weight,
    fc2_bias,
    qkv_down,
    qkv_up,
    out_down,
    out_up,
    fc1_down,
    fc1_up,
    fc2_down,
    fc2_up,
):
    images = tokens.shape[0]
    own_start = lax.axis_index("tensor") * images
    index = lax.dynamic_slice_in_dim(adapter_index, own_start, images, 0)
    mask = lax.dynamic_slice_in_dim(filled, own_start, images, 0)
    stack_list = (qkv_down, qkv_up, out_down, out_up, fc1_down, fc1_up, fc2_down, fc2_up)
    widths = [stacked.shape[2] for stacked in stack_list]
    spans = []
    offset = 0
    for width in widths:
        spans.append(slice(offset, offset + width))
        offset += width
    packed = jnp.concatenate([stacked.reshape(STACK, -1) for stacked in stack_list], axis=1).T
    rows = qkv_weight.shape[0]
    column = qkv_weight.shape[2]
    hidden = fc1_weight.shape[1]
    packed = lax.all_gather(packed, BOTH, axis=0)
    gather = lambda shard: lax.all_gather(shard, BOTH, axis=0).reshape(
        D // rows, D // column, rows, -1
    )
    qkv_all = gather(qkv_weight.reshape(rows, 3 * column))
    rest = gather(jnp.concatenate([out_weight.T, fc1_weight, fc2_weight.T], axis=1))
    out_all = rest[..., :column]
    first_all = rest[..., column : column + hidden]
    second_all = rest[..., column + hidden :]
    full = [packed[:, span, :].reshape(-1, STACK) for span in spans]
    row = lambda vector: vector.astype(f32)[None, :]
    q, k, v, low_one = qkv_project(
        tokens, qkv_all, full[0], full[1], index, qv_bias, row(ln1_gain), row(ln1_shift)
    )
    o, prob = attend(q, k, v)
    h, low_out = out_project(tokens, o, out_all, full[2], full[3], index, mask, row(out_bias))
    outputs, dh, grad_up2, grad_down2, grad_up1, grad_down1 = mlp(
        h, cotangent, first_all, second_all, full[4], full[5], full[6], full[7], index, mask,
        row(fc1_bias), row(fc2_bias), row(ln2_gain), row(ln2_shift),
    )
    do, grad_out_up, grad_out_down = out_back(
        dh, o, low_out, out_all, full[2], full[3], index, mask
    )
    dq, dk, dv = attend_back(q, k, v, do, prob)
    input_grad, grad_qkv_up, grad_qkv_down = qkv_back(
        tokens, dh, dq, dk, dv, low_one, qkv_all, full[0], full[1], index,
        row(ln1_gain), row(ln1_shift),
    )
    terms = (
        grad_qkv_down, grad_qkv_up, grad_out_down, grad_out_up,
        grad_down1, grad_up1, grad_down2, grad_up2,
    )
    members = packed.shape[0]
    summed = lax.psum_scatter(
        jnp.concatenate([term.reshape(members, -1, STACK) for term in terms], axis=1),
        BOTH,
        scatter_dimension=0,
        tiled=False,
    ).T
    grads = [summed[:, span].reshape(ADAPTERS, RANK, -1) for span in spans]
    return (outputs, input_grad, *grads)


def solution(mesh):
    images = P(BOTH, None, None)
    stacked = P(None, None, BOTH)
    in_specs = (
        images, images, P("fsdp"), P("fsdp"), P(), P(), P("fsdp", None, "tensor"), P(),
        P("tensor", "fsdp"), P(), P(), P(), P("fsdp", "tensor"), P(), P("tensor", "fsdp"), P(),
    ) + (stacked,) * 8
    out_specs = (images, images) + (stacked,) * 8
    return jax.shard_map(
        on_device, mesh=mesh, in_specs=in_specs, out_specs=out_specs, check_vma=False
    )
```

```python
import math
from functools import partial

import jax
import jax.numpy as jnp
from jax import lax
from jax.experimental import pallas as pl
from jax.experimental.pallas import tpu as pltpu
from jax.sharding import PartitionSpec as P

D = 1024
HEADS = 16
HEAD_DIM = 64
FF = 4096
SEQ = 577
RANK = 16
ADAPTERS = 8
STACK = ADAPTERS * RANK
TILE = 512

epsilon = 1e-05
bf16 = jnp.bfloat16
f32 = jnp.float32
NN = (((1,), (0,)), ((), ()))
NT = (((1,), (1,)), ((), ()))
TN = (((0,), (0,)), ((), ()))
BOTH = ("fsdp", "tensor")


def dot(left, right, dims):
    return lax.dot_general(left, right, dims, preferred_element_type=f32)


def params():
    return pltpu.CompilerParams(vmem_limit_bytes=60 << 20)


def cost(flops, moved, exps=0):
    return pl.CostEstimate(flops=flops, bytes_accessed=moved, transcendentals=exps)


def smem():
    return pl.BlockSpec(memory_space=pltpu.SMEM)


def whole(shape):
    return pl.BlockSpec(shape, lambda *_: (0,) * len(shape), pipeline_mode=pl.Buffered(1))


def image_rows(width=D):
    return pl.BlockSpec((pl.Squeezed(), SEQ, width), lambda i: (i, 0, 0))


def normalize(values):
    center = values - jnp.mean(values, axis=-1, keepdims=True)
    inverse = lax.rsqrt(jnp.mean(center * center, axis=-1, keepdims=True) + epsilon)
    return center * inverse, inverse


def norm_back(upstream, normed, inverse, gain_row):
    scaled = upstream * gain_row
    return inverse * (
        scaled
        - jnp.mean(scaled, axis=-1, keepdims=True)
        - normed * jnp.mean(scaled * normed, axis=-1, keepdims=True)
    )


def chosen_lanes(adapter):
    lanes = lax.broadcasted_iota(jnp.int32, (1, STACK), 1)
    return (lanes // RANK) == adapter


def keep(product, adapter):
    return jnp.where(chosen_lanes(adapter), product, 0.0).astype(bf16)


def add_to(ref, value, first):
    @pl.when(first)
    def _():
        ref[...] = value

    @pl.when(jnp.logical_not(first))
    def _():
        ref[...] += value


def flat(block):
    return block.reshape(D, block.shape[-1])


def any_space():
    return pl.BlockSpec(memory_space=pl.ANY)


class Stream:
    def __init__(self, sources, lane, width, slots, sems):
        self.sources, self.lane, self.width = sources, lane, width
        self.slots, self.sems = slots, sems

    def copy(self, source, inner, slot):
        lanes = pl.ds(self.lane, self.width)
        return pltpu.make_async_copy(
            source.at[inner, :, :, lanes], self.slots.at[slot], self.sems.at[slot]
        )

    def start(self, group, slot):
        offset = 0
        for source in self.sources:
            count = source.shape[0]

            @pl.when(jnp.logical_and(group >= offset, group < offset + count))
            def _(source=source, offset=offset):
                self.copy(source, group - offset, slot).start()

            offset += count

    def start_all(self):
        group = 0
        for source in self.sources:
            for inner in range(source.shape[0]):
                self.copy(source, inner, group).start()
                group += 1

    def wait(self, slot):
        self.copy(self.sources[0], 0, slot).wait()


def qkv_kernel(count, *refs):
    table_ref, index_ref, tokens_ref = refs[:3]
    sources = refs[3 : 3 + count]
    down_ref, up_ref, bias_ref, gain_ref, shift_ref = refs[3 + count : 8 + count]
    q_ref, k_ref, v_ref, low_ref, a_s, low_s, slots, sems = refs[8 + count :]
    group = pl.program_id(0)
    image = pl.program_id(1)
    width = q_ref.shape[-1]
    stream = Stream(sources, 0, 3 * width, slots, sems)
    slot = group % 2

    @pl.when(jnp.logical_and(group == 0, image == 0))
    def _():
        stream.start(group, 0)

    @pl.when(group == 0)
    def _():
        normed, _ = normalize(tokens_ref[...].astype(f32))
        a = (normed * gain_ref[...] + shift_ref[...]).astype(bf16)
        a_s[image] = a
        low_s[image] = keep(dot(a, down_ref[...], NN), index_ref[image])

    @pl.when(image == 0)
    def _():
        stream.wait(slot)

        @pl.when(group + 1 < pl.num_programs(0))
        def _():
            stream.start(group + 1, 1 - slot)

    a = a_s[image]
    low = low_s[image]
    low_ref[...] = low
    weight = flat(slots[slot])
    start = pl.multiple_of(table_ref[group] * width, width)
    bias = bias_ref[...].astype(f32)
    for part, out_ref in enumerate((q_ref, k_ref, v_ref)):
        value = dot(a, weight[:, part * width : (part + 1) * width], NN)
        value += dot(low, up_ref[pl.ds(part * D + start, width), :], NT)
        if part != 1:
            value += bias[part // 2 : part // 2 + 1]
        out_ref[...] = value.astype(bf16)


def group_count(sources):
    return sum(source.shape[0] for source in sources)


def qkv_project(tokens, sources, table, down, up, index, bias, gain, shift):
    images = tokens.shape[0]
    members, rows = sources[0].shape[1:3]
    groups = group_count(sources)
    width = D // groups
    sq = pl.Squeezed()
    out = pl.BlockSpec((sq, SEQ, width), lambda g, i, t: (i, 0, t[g]))
    vector = whole((1, D))
    grid_spec = pltpu.PrefetchScalarGridSpec(
        num_scalar_prefetch=1,
        grid=(groups, images),
        in_specs=[smem(), pl.BlockSpec((sq, SEQ, D), lambda g, i, t: (i, 0, 0))]
        + [any_space()] * len(sources)
        + [
            whole((D, STACK)),
            whole((3 * D, STACK)),
            pl.BlockSpec((2, width), lambda g, i, t: (0, t[g])),
            vector,
            vector,
        ],
        out_specs=[out, out, out, pl.BlockSpec((sq, SEQ, STACK), lambda g, i, t: (i, 0, 0))],
        scratch_shapes=[
            pltpu.VMEM((images, SEQ, D), bf16),
            pltpu.VMEM((images, SEQ, STACK), bf16),
            pltpu.VMEM((2, members, rows, 3 * width), bf16),
            pltpu.SemaphoreType.DMA((2,)),
        ],
    )
    return pl.pallas_call(
        partial(qkv_kernel, len(sources)),
        grid_spec=grid_spec,
        out_shape=[jax.ShapeDtypeStruct((images, SEQ, D), bf16)] * 3
        + [jax.ShapeDtypeStruct((images, SEQ, STACK), bf16)],
        compiler_params=params(),
        cost_estimate=cost(6 * images * SEQ * D * D, 20 << 20),
        name="qkv_project",
    )(table, index, tokens, *sources, down, up, bias, gain, shift)


def attend_kernel(q_ref, k_ref, v_ref, o_ref, w_ref):
    q = q_ref[...]
    k = k_ref[...]
    v = v_ref[...]
    low = lax.broadcasted_iota(jnp.int32, q.shape, 1) < HEAD_DIM
    outs = []
    for head in range(2):
        own = low if head == 0 else jnp.logical_not(low)
        queries = jnp.where(own, q * HEAD_DIM**-0.5, jnp.zeros_like(q)).astype(bf16)
        scores = dot(queries, k, NT)
        top = jnp.max(scores, axis=-1, keepdims=True)
        raised = jnp.exp(scores - top)
        total = jnp.sum(raised, axis=-1, keepdims=True)
        prob = (raised * (1.0 / total)).astype(bf16)
        w_ref[head] = prob
        outs.append(dot(prob, v, NN))
    o_ref[...] = jnp.where(low, outs[0], outs[1]).astype(bf16)


def pair_rows(image):
    return pl.BlockSpec((pl.Squeezed(), SEQ, 2 * HEAD_DIM), lambda h: (image, 0, h))


def pair_weights(image):
    return pl.BlockSpec((2, SEQ, SEQ), lambda h: (image * (HEADS // 2) + h, 0, 0))


def into(kernel, inputs):
    def body(*refs):
        kernel(*refs[:inputs], *refs[len(refs) - (len(refs) - inputs) // 2 :])

    return body


def per_image(kernel, name, image, inputs, in_specs, outs, out_specs, filled, flops, moved, exps):
    count = len(inputs)
    if filled is None:
        return pl.pallas_call(
            kernel, grid=(HEADS // 2,), in_specs=in_specs, out_specs=out_specs, out_shape=outs,
            compiler_params=params(), cost_estimate=cost(flops, moved, exps), name=name,
        )(*inputs)
    return pl.pallas_call(
        into(kernel, count), grid=(HEADS // 2,), in_specs=in_specs + [any_space()] * len(outs),
        out_specs=out_specs, out_shape=outs,
        input_output_aliases={count + n: n for n in range(len(outs))},
        compiler_params=params(), cost_estimate=cost(flops, moved, exps), name=name,
    )(*inputs, *filled)


def attend(q, k, v, image, filled):
    images = q.shape[0]
    outs = [
        jax.ShapeDtypeStruct((images, SEQ, D), bf16),
        jax.ShapeDtypeStruct((images * HEADS, SEQ, SEQ), bf16),
    ]
    return per_image(
        attend_kernel, "attend", image, (q, k, v), [pair_rows(image)] * 3, outs,
        [pair_rows(image), pair_weights(image)], filled,
        16 * SEQ * SEQ * D, 20 << 20, HEADS * SEQ * SEQ,
    )


def attend_back_kernel(q_ref, k_ref, v_ref, do_ref, w_ref, dq_ref, dk_ref, dv_ref):
    q = q_ref[...]
    k = k_ref[...]
    v = v_ref[...]
    do = do_ref[...]
    low = lax.broadcasted_iota(jnp.int32, q.shape, 1) < HEAD_DIM
    grads = []
    for head in range(2):
        own = low if head == 0 else jnp.logical_not(low)
        mixed_grad = jnp.where(own, do, jnp.zeros_like(do))
        prob_grad = dot(mixed_grad, v, NT)
        prob_low = w_ref[head]
        prob = prob_low.astype(f32)
        inner = jnp.sum(prob * prob_grad, axis=-1, keepdims=True)
        score_grad = (prob * (prob_grad - inner)).astype(bf16)
        grads.append((dot(score_grad, k, NN), dot(score_grad, q, TN), dot(prob_low, do, TN)))
    scale = HEAD_DIM**-0.5
    dq_ref[...] = (jnp.where(low, grads[0][0], grads[1][0]) * scale).astype(bf16)
    dk_ref[...] = (jnp.where(low, grads[0][1], grads[1][1]) * scale).astype(bf16)
    dv_ref[...] = jnp.where(low, grads[0][2], grads[1][2]).astype(bf16)


def attend_back(q, k, v, do, prob, image, filled):
    outs = [jax.ShapeDtypeStruct(q.shape, bf16)] * 3
    return per_image(
        attend_back_kernel, "attend_back", image, (q, k, v, do, prob),
        [pair_rows(image)] * 4 + [pair_weights(image)], outs, [pair_rows(image)] * 3, filled,
        32 * SEQ * SEQ * D, 24 << 20, 0,
    )


def out_kernel(count, lane, *refs):
    table_ref, index_ref, filled_ref, tokens_ref, o_ref = refs[:5]
    sources = refs[5 : 5 + count]
    down_ref, up_ref, bias_ref, h_ref, low_ref, slots, sems = refs[5 + count :]
    image = pl.program_id(0)
    groups = slots.shape[0]
    width = slots.shape[-1]
    stream = Stream(sources, lane, width, slots, sems)

    @pl.when(image == 0)
    def _():
        stream.start_all()

    low = keep(dot(o_ref[...], down_ref[...], NN), index_ref[image])
    low_ref[...] = low
    value = dot(low, up_ref[...], NT) + bias_ref[...]
    for group in range(groups):
        @pl.when(image == 0)
        def _(group=group):
            stream.wait(group)

        start = pl.multiple_of(table_ref[group] * width, width)
        value += dot(o_ref[:, pl.ds(start, width)], flat(slots[group]), NT)
    h_ref[...] = tokens_ref[...].astype(f32) + filled_ref[image].astype(f32) * value


def out_slots(sources):
    members, rows = sources[0].shape[1:3]
    groups = group_count(sources)
    return [
        pltpu.VMEM((groups, members, rows, D // groups), bf16),
        pltpu.SemaphoreType.DMA((groups,)),
    ]


def out_project(tokens, o, sources, lane, table, down, up, index, filled, bias):
    images = tokens.shape[0]
    return pl.pallas_call(
        partial(out_kernel, len(sources), lane),
        grid=(images,),
        in_specs=[smem(), smem(), smem(), image_rows(), image_rows()]
        + [any_space()] * len(sources)
        + [whole((D, STACK)), whole((D, STACK)), whole((1, D))],
        out_specs=[image_rows(), image_rows(STACK)],
        out_shape=[
            jax.ShapeDtypeStruct((images, SEQ, D), f32),
            jax.ShapeDtypeStruct((images, SEQ, STACK), bf16),
        ],
        scratch_shapes=out_slots(sources),
        compiler_params=params(),
        cost_estimate=cost(2 * images * SEQ * D * D, 12 << 20),
        name="out_project",
    )(table, index, filled, tokens, o, *sources, down, up, bias)


def out_back_kernel(count, lane, *refs):
    table_ref, index_ref, filled_ref, dh_ref, o_ref, low_ref = refs[:6]
    sources = refs[6 : 6 + count]
    down_ref, up_ref, do_ref, grad_up_ref, grad_down_ref = refs[6 + count : 11 + count]
    grad_up_s, grad_down_s, slots, sems = refs[11 + count :]
    image = pl.program_id(0)
    last = image == pl.num_programs(0) - 1
    width = slots.shape[-1]
    stream = Stream(sources, lane, width, slots, sems)

    @pl.when(image == 0)
    def _():
        stream.start_all()

    branch = (dh_ref[...] * filled_ref[image].astype(f32)).astype(bf16)
    low_grad = keep(dot(branch, up_ref[...], NN), index_ref[image])
    add_to(grad_up_s, dot(low_ref[...], branch, TN), image == 0)
    add_to(grad_down_s, dot(low_grad, o_ref[...], TN), image == 0)
    for group in range(slots.shape[0]):
        @pl.when(image == 0)
        def _(group=group):
            stream.wait(group)

        start = pl.multiple_of(table_ref[group] * width, width)
        value = dot(branch, flat(slots[group]), NN)
        value += dot(low_grad, down_ref[pl.ds(start, width), :], NT)
        do_ref[:, pl.ds(start, width)] = value.astype(bf16)

    @pl.when(last)
    def _():
        grad_up_ref[...] = grad_up_s[...].T.astype(bf16)
        grad_down_ref[...] = grad_down_s[...].T.astype(bf16)


def out_back(dh, o, low, sources, lane, table, down, up, index, filled):
    images = dh.shape[0]
    grad = pl.BlockSpec((D, STACK), lambda i: (0, 0))
    return pl.pallas_call(
        partial(out_back_kernel, len(sources), lane),
        grid=(images,),
        in_specs=[smem(), smem(), smem(), image_rows(), image_rows(), image_rows(STACK)]
        + [any_space()] * len(sources)
        + [whole((D, STACK)), whole((D, STACK))],
        out_specs=[image_rows(), grad, grad],
        out_shape=[jax.ShapeDtypeStruct((images, SEQ, D), bf16)]
        + [jax.ShapeDtypeStruct((D, STACK), bf16)] * 2,
        scratch_shapes=[pltpu.VMEM((STACK, D), f32)] * 2 + out_slots(sources),
        compiler_params=params(),
        cost_estimate=cost(2 * images * SEQ * D * D, 12 << 20),
        name="out_back",
    )(table, index, filled, dh, o, low, *sources, down, up)


def mlp_kernel(
    index_ref, filled_ref, h_ref, cot_ref, first_ref, second_ref, down1_ref, up1_ref, down2_ref,
    up2_ref, bias1_ref, bias2_ref, gain_ref, shift_ref,
    out_ref, dh_ref, grad_up2_ref, grad_down2_ref, grad_up1_ref, grad_down1_ref,
    a_s, dz_s, low3_s, dlow4_s, z_s, da_s, low4_s, dlow3_s,
    grad_up2_s, grad_down2_s, grad_up1_s, grad_down1_s,
):
    tile = pl.program_id(0)
    image = pl.program_id(1)
    last = tile == pl.num_programs(0) - 1
    final = image == pl.num_programs(1) - 1
    adapter = index_ref[image]
    mask = filled_ref[image].astype(f32)

    @pl.when(tile == 0)
    def _():
        normed, _ = normalize(h_ref[image])
        a = (normed * gain_ref[...] + shift_ref[...]).astype(bf16)
        a_s[image] = a
        dz = (cot_ref[image].astype(f32) * mask).astype(bf16)
        dz_s[image] = dz
        low3_s[image] = keep(dot(a, down1_ref[...], NN), adapter)
        dlow4_s[image] = keep(dot(dz, up2_ref[...], NN), adapter)

    a = a_s[image]
    dz = dz_s[image]
    low3 = low3_s[image]
    dlow4 = dlow4_s[image]
    first = flat(first_ref[...])
    second = flat(second_ref[...])
    before = dot(a, first, NN) + dot(low3, up1_ref[...], NT) + bias1_ref[...]
    density = jnp.exp(before * before * -0.5) * 0.3989422804014327
    below = 0.5 * lax.erf(before * 0.7071067811865476) + 0.5
    g = (before * below).astype(bf16)
    slope = below + before * density
    dg = dot(dz, second, NN) + dot(dlow4, down2_ref[...], NT)
    df = (dg * slope).astype(bf16)
    z_part = dot(g, second, NT)
    da_part = dot(df, first, NT)
    low4_part = dot(g, down2_ref[...], NN)
    dlow3_part = dot(df, up1_ref[...], NN)

    @pl.when(tile == 0)
    def _():
        z_s[image] = z_part
        da_s[image] = da_part
        low4_s[image] = low4_part
        dlow3_s[image] = dlow3_part

    @pl.when(tile > 0)
    def _():
        z_s[image] += z_part
        da_s[image] += da_part
        low4_s[image] += low4_part
        dlow3_s[image] += dlow3_part

    add_to(grad_down2_s, dot(dlow4, g, TN), image == 0)
    add_to(grad_up1_s, dot(low3, df, TN), image == 0)

    @pl.when(final)
    def _():
        grad_down2_ref[...] = grad_down2_s[...].T.astype(bf16)
        grad_up1_ref[...] = grad_up1_s[...].T.astype(bf16)

    @pl.when(last)
    def _():
        low4 = keep(low4_s[image], adapter)
        h = h_ref[image]
        z = z_s[image] + dot(low4, up2_ref[...], NT) + bias2_ref[...]
        out_ref[...] = (h + mask * z).astype(bf16)
        add_to(grad_up2_s, dot(low4, dz, TN), image == 0)
        dlow3 = keep(dlow3_s[image], adapter)
        da = da_s[image] + dot(dlow3, down1_ref[...], NT)
        add_to(grad_down1_s, dot(dlow3, a, TN), image == 0)
        normed, inverse = normalize(h)
        dh_ref[...] = cot_ref[image].astype(f32) + norm_back(
            da, normed, inverse, gain_ref[...]
        )

    @pl.when(jnp.logical_and(last, final))
    def _():
        grad_up2_ref[...] = grad_up2_s[...].T.astype(bf16)
        grad_down1_ref[...] = grad_down1_s[...].T.astype(bf16)


def mlp(h, cot, weights, down1, up1, down2, up2, index, filled, bias1, bias2, gain, shift):
    images = h.shape[0]
    members, groups, rows, _ = weights.shape
    hidden = FF // groups
    width = min(TILE, hidden)
    per_group = hidden // width
    tiles = FF // width
    sq = pl.Squeezed()

    def weight(base):
        return pl.BlockSpec(
            (members, sq, rows, width),
            lambda j, i: (0, j // per_group, 0, base * per_group + j % per_group),
        )

    tall = pl.BlockSpec((width, STACK), lambda j, i: (j, 0))
    short = pl.BlockSpec((D, STACK), lambda j, i: (0, 0))
    late = pl.BlockSpec((sq, SEQ, D), lambda j, i: (jnp.where(j == tiles - 1, i, 0), 0, 0))
    return pl.pallas_call(
        mlp_kernel,
        grid=(tiles, images),
        in_specs=[
            smem(),
            smem(),
            whole((images, SEQ, D)),
            whole((images, SEQ, D)),
            weight(0),
            weight(1),
            whole((D, STACK)),
            tall,
            tall,
            whole((D, STACK)),
            pl.BlockSpec((1, width), lambda j, i: (0, j)),
            whole((1, D)),
            whole((1, D)),
            whole((1, D)),
        ],
        out_specs=[late, late, short, tall, tall, short],
        out_shape=[
            jax.ShapeDtypeStruct((images, SEQ, D), bf16),
            jax.ShapeDtypeStruct((images, SEQ, D), f32),
            jax.ShapeDtypeStruct((D, STACK), bf16),
            jax.ShapeDtypeStruct((FF, STACK), bf16),
            jax.ShapeDtypeStruct((FF, STACK), bf16),
            jax.ShapeDtypeStruct((D, STACK), bf16),
        ],
        scratch_shapes=[
            pltpu.VMEM((images, SEQ, D), bf16),
            pltpu.VMEM((images, SEQ, D), bf16),
            pltpu.VMEM((images, SEQ, STACK), bf16),
            pltpu.VMEM((images, SEQ, STACK), bf16),
            pltpu.VMEM((images, SEQ, D), f32),
            pltpu.VMEM((images, SEQ, D), f32),
            pltpu.VMEM((images, SEQ, STACK), f32),
            pltpu.VMEM((images, SEQ, STACK), f32),
            pltpu.VMEM((STACK, D), f32),
            pltpu.VMEM((STACK, width), f32),
            pltpu.VMEM((STACK, width), f32),
            pltpu.VMEM((STACK, D), f32),
        ],
        compiler_params=params(),
        cost_estimate=cost(8 * images * SEQ * D * FF, 40 << 20, 2 * images * SEQ * FF),
        name="mlp",
    )(index, filled, h, cot, weights, weights, down1, up1, down2, up2, bias1, bias2, gain, shift)


def qkv_grads_kernel(
    index_ref, tokens_ref, dq_ref, dk_ref, dv_ref, low_ref, up_ref, gain_ref, shift_ref,
    low_grad_ref, grad_up_ref, grad_down_ref, grad_up_s, grad_down_s,
):
    image = pl.program_id(0)
    parts = (dq_ref, dk_ref, dv_ref)
    low = low_ref[...]
    low_grad = dot(parts[0][...], up_ref[0:D, :], NN)
    for part in (1, 2):
        low_grad += dot(parts[part][...], up_ref[part * D : (part + 1) * D, :], NN)
    low_grad = keep(low_grad, index_ref[image])
    low_grad_ref[...] = low_grad
    for part in range(3):
        add_to(grad_up_s.at[part], dot(low, parts[part][...], TN), image == 0)
    normed, _ = normalize(tokens_ref[...].astype(f32))
    a = (normed * gain_ref[...] + shift_ref[...]).astype(bf16)
    add_to(grad_down_s, dot(low_grad, a, TN), image == 0)

    @pl.when(image == pl.num_programs(0) - 1)
    def _():
        for part in range(3):
            grad_up_ref[part * D : (part + 1) * D, :] = grad_up_s[part].T.astype(bf16)
        grad_down_ref[...] = grad_down_s[...].T.astype(bf16)


def qkv_grads(tokens, dq, dk, dv, low, up, index, gain, shift):
    images = tokens.shape[0]
    return pl.pallas_call(
        qkv_grads_kernel,
        grid=(images,),
        in_specs=[smem()]
        + [image_rows()] * 4
        + [image_rows(STACK), whole((3 * D, STACK)), whole((1, D)), whole((1, D))],
        out_specs=[
            image_rows(STACK),
            pl.BlockSpec((3 * D, STACK), lambda i: (0, 0)),
            pl.BlockSpec((D, STACK), lambda i: (0, 0)),
        ],
        out_shape=[
            jax.ShapeDtypeStruct((images, SEQ, STACK), bf16),
            jax.ShapeDtypeStruct((3 * D, STACK), bf16),
            jax.ShapeDtypeStruct((D, STACK), bf16),
        ],
        scratch_shapes=[pltpu.VMEM((3, STACK, D), f32), pltpu.VMEM((STACK, D), f32)],
        compiler_params=params(),
        cost_estimate=cost(2 * images * SEQ * D * D, 12 << 20),
        name="qkv_grads",
    )(index, tokens, dq, dk, dv, low, up, gain, shift)


def qkv_back_kernel(count, *refs):
    table_ref, tokens_ref, dh_ref, dq_ref, dk_ref, dv_ref, low_grad_ref = refs[:7]
    sources = refs[7 : 7 + count]
    down_ref, gain_ref = refs[7 + count : 9 + count]
    grad_ref, slots, sems = refs[-3:]
    width = slots.shape[-1] // 3
    stream = Stream(sources, 0, 3 * width, slots, sems)
    stream.start_all()
    parts = (dq_ref, dk_ref, dv_ref)
    da = dot(low_grad_ref[...], down_ref[...], NT)
    normed, inverse = normalize(tokens_ref[...].astype(f32))
    for group in range(slots.shape[0]):
        stream.wait(group)
        start = pl.multiple_of(table_ref[group] * width, width)
        weight = flat(slots[group])
        for part in range(3):
            da += dot(
                parts[part][:, pl.ds(start, width)],
                weight[:, part * width : (part + 1) * width],
                NT,
            )
    grad_ref[...] = dh_ref[...] + norm_back(da, normed, inverse, gain_ref[...])


def qkv_back(tokens, dh, dq, dk, dv, low_grad, sources, table, down, gain, image, filled):
    images = tokens.shape[0]
    members, rows = sources[0].shape[1:3]
    groups = group_count(sources)
    at_image = lambda width=D: pl.BlockSpec((pl.Squeezed(), SEQ, width), lambda i: (image, 0, 0))
    extra = [] if filled is None else [filled]
    inputs = (table, tokens, dh, dq, dk, dv, low_grad, *sources, down, gain, *extra)
    return pl.pallas_call(
        partial(qkv_back_kernel, len(sources)),
        grid=(1,),
        in_specs=[smem()]
        + [at_image()] * 5
        + [at_image(STACK)]
        + [any_space()] * len(sources)
        + [whole((D, STACK)), whole((1, D))]
        + [any_space()] * len(extra),
        out_specs=at_image(),
        out_shape=jax.ShapeDtypeStruct((images, SEQ, D), f32),
        scratch_shapes=[
            pltpu.VMEM((groups, members, rows, 3 * D // groups), bf16),
            pltpu.SemaphoreType.DMA((groups,)),
        ],
        input_output_aliases={len(inputs) - 1: 0} if extra else {},
        compiler_params=params(),
        cost_estimate=cost(6 * SEQ * D * D, 18 << 20),
        name="qkv_back",
    )(*inputs)


STEPS = (16, 2, 2)


def along_x(array):
    return lax.ppermute(array, "fsdp", [(f, f ^ 1) for f in range(16)])


def along_y(array):
    return lax.ppermute(array, "fsdp", [(f, f ^ 2) for f in range(16)])


def along_z(array, shift):
    pairs = [(f, (f // 4 + shift) % 4 * 4 + f % 4) for f in range(16)]
    return lax.ppermute(array, "fsdp", pairs)


def other_core(array):
    return lax.ppermute(array, "tensor", [(0, 1), (1, 0)])


def positions():
    f = lax.axis_index("fsdp")
    t = lax.axis_index("tensor")
    z, y, x = f // 4, f // 2 % 2, f % 2
    places = [z, (z + 3) % 4, (z + 2) % 4, (z + 1) % 4, y, 1 - y, x, 1 - x, t, 1 - t]
    return jnp.stack(places).astype(jnp.int32)


def move(name, places, parts, outs, moves, room=None):
    room = room or (4 << 20) + sum(2 * math.prod(shape) for shape in outs)

    def kernel(places_ref, *refs):
        sems = refs[-1]
        copies = []
        for number, (part, out, source, target) in enumerate(moves):
            copies.append(
                pltpu.make_async_copy(
                    source(refs[part], places_ref),
                    target(refs[len(parts) + out], places_ref),
                    sems.at[number],
                )
            )
            copies[-1].start()
        for copy in copies:
            copy.wait()

    return pl.pallas_call(
        kernel,
        in_specs=[smem()] + [any_space()] * len(parts),
        out_specs=[pl.BlockSpec(memory_space=pltpu.VMEM)] * len(outs),
        out_shape=[jax.ShapeDtypeStruct(shape, bf16) for shape in outs],
        scratch_shapes=[pltpu.SemaphoreType.DMA((len(moves),))],
        compiler_params=pltpu.CompilerParams(vmem_limit_bytes=room),
        name=name,
    )(places, *parts)


def everything(ref, places):
    return ref


def after(value, *others):
    return lax.optimization_barrier((value, *others))[0]


class Piece:
    def __init__(self, shard, places, tag):
        self.shard, self.places, self.tag = shard, places, tag
        self.rows, self.half = shard.shape[0], shard.shape[1] // 2

    def send_z(self):
        self.parts = [self.shard] + [along_z(self.shard, shift) for shift in (1, 2, 3)]

    def wait_for(self, other):
        self.parts[0] = after(self.parts[0], other)

    def join_z(self):
        half = self.half
        self.a, self.b = move(
            "gather_z" + self.tag, self.places, self.parts, [(4, self.rows, half)] * 2,
            [
                (
                    shift, side,
                    lambda ref, p, side=side: ref.at[:, pl.ds(side * half, half)],
                    lambda ref, p, shift=shift: ref.at[p[shift]],
                )
                for shift in range(4)
                for side in range(2)
            ],
        )

    def send_half(self):
        self.parts = [self.a, along_y(self.a), self.b, along_x(self.b)]

    def join_half(self):
        self.a, self.b = move(
            "gather_yx" + self.tag, self.places, self.parts, [(4, 2, self.rows, self.half)] * 2,
            [
                (0, 0, everything, lambda ref, p: ref.at[:, p[4]]),
                (1, 0, everything, lambda ref, p: ref.at[:, p[5]]),
                (2, 1, everything, lambda ref, p: ref.at[:, p[6]]),
                (3, 1, everything, lambda ref, p: ref.at[:, p[7]]),
            ],
        )

    def send_rest(self):
        self.parts = [self.a, along_x(self.a), self.b, along_y(self.b)]

    def join_rest(self):
        (joined,) = move(
            "gather_xy" + self.tag, self.places, self.parts,
            [(2, 4, 2, 2, self.rows, self.half)],
            [
                (0, 0, everything, lambda ref, p: ref.at[0, :, :, p[6]]),
                (1, 0, everything, lambda ref, p: ref.at[0, :, :, p[7]]),
                (2, 0, everything, lambda ref, p: ref.at[1, :, p[4]]),
                (3, 0, everything, lambda ref, p: ref.at[1, :, p[5]]),
            ],
        )
        self.own = joined.reshape(2, 16, self.rows, self.half)
        self.sources = (self.own, other_core(self.own))


class SmallPiece(Piece):
    def join_z(self):
        (self.a,) = move(
            "gather_z" + self.tag, self.places, self.parts, [(4, self.rows, 2 * self.half)],
            [
                (shift, 0, everything, lambda ref, p, shift=shift: ref.at[p[shift]])
                for shift in range(4)
            ],
        )

    def send_layer(self):
        diagonal = lax.ppermute(self.a, "fsdp", [(f, f ^ 3) for f in range(16)])
        self.parts = [self.a, along_x(self.a), along_y(self.a), diagonal]

    def join_layer(self):
        half = self.half
        (joined,) = move(
            "gather_layer" + self.tag, self.places, self.parts,
            [(2, 4, 2, 2, self.rows, half)],
            [
                (
                    part, 0,
                    lambda ref, p, side=side: ref.at[:, :, pl.ds(side * half, half)],
                    lambda ref, p, side=side, y=y, x=x: ref.at[side, :, p[y], p[x]],
                )
                for part, (y, x) in enumerate(((4, 6), (4, 7), (5, 6), (5, 7)))
                for side in range(2)
            ],
        )
        self.own = joined.reshape(2, 16, self.rows, half)
        self.sources = (self.own, other_core(self.own))


def transposed(stacked):
    return stacked.reshape(STACK, -1).T


def halves(rows_by_lanes, pieces):
    rows = rows_by_lanes.shape[0]
    split = rows_by_lanes.reshape(rows, pieces, 2, -1)
    return [split[:, :, side].reshape(rows, -1) for side in range(2)]


class StepGather:
    def __init__(self, qkv_weight, out_weight, fc1_weight, fc2_weight, shards):
        rows, _, column = qkv_weight.shape
        qd, qu, od, ou, f1d, f1u, f2d, f2u = shards
        places = positions()
        t = lax.axis_index("tensor")
        qkv_a, qkv_b = halves(qkv_weight.reshape(rows, 3 * column), 3)
        out_a, out_b = halves(out_weight.T, 1)
        low1 = jnp.concatenate([qd, qu], axis=0)
        low2 = jnp.concatenate([od, ou], axis=0)
        low3 = jnp.concatenate([f1d, f2u], axis=0)
        self.piece1 = Piece(
            jnp.concatenate([qkv_a, low1[:64], qkv_b, low1[64:]], axis=1), places, "1"
        )
        self.piece2 = SmallPiece(jnp.concatenate([out_a, low2, out_b, low3], axis=1), places, "2")
        hidden = jnp.concatenate(
            [fc1_weight, fc2_weight.T, f1u[:64], f1u[64:], f2d[:64], f2d[64:]], axis=1
        )
        self.hidden = hidden
        self.places, self.column = places, column
        self.width = fc1_weight.shape[1]
        self.groups = jnp.stack([2 * t, 2 * t + 1, 2 - 2 * t, 3 - 2 * t]).astype(jnp.int32)
        self.lane = 0

    def first(self):
        one, two = self.piece1, self.piece2
        one.send_z()
        one.join_z()
        two.shard = after(two.shard, one.a)
        hidden = after(self.hidden, one.a)
        self.hidden = lax.all_gather(hidden, BOTH, axis=0).reshape(16, 2, *hidden.shape)
        one.send_half()
        one.join_half()
        one.send_rest()
        two.send_z()
        one.join_rest()
        lanes = pl.ds(3 * self.column // 2, STACK)
        qd, qu = move(
            "stacks1", self.places, one.sources, [(16, 2, 32, STACK), (16, 2, 96, STACK)],
            [
                m
                for source, core in ((0, 8), (1, 9))
                for m in (
                    (source, 0, lambda ref, p: ref.at[0, :, pl.ds(0, 32), lanes],
                     lambda ref, p, core=core: ref.at[:, p[core]]),
                    (source, 1, lambda ref, p: ref.at[0, :, pl.ds(32, 32), lanes],
                     lambda ref, p, core=core: ref.at[:, p[core], pl.ds(0, 32)]),
                    (source, 1, lambda ref, p: ref.at[1, :, :, lanes],
                     lambda ref, p, core=core: ref.at[:, p[core], pl.ds(32, 64)]),
                )
            ],
        )
        return one.sources, qd.reshape(-1, STACK), qu.reshape(-1, STACK)

    def after_qkv(self, q):
        two = self.piece2
        two.wait_for(q)
        two.join_z()
        two.send_layer()
        return after(q, two.a)

    def second(self, o):
        self.piece2.wait_for(o)
        self.piece2.join_layer()
        lanes = pl.ds(self.column // 2, STACK)
        stacks = move(
            "stacks2", self.places, self.piece2.sources, [(16, 2, 32, STACK)] * 4,
            [
                (source, out,
                 lambda ref, p, out=out: ref.at[out // 2, :, pl.ds(out % 2 * 32, 32), lanes],
                 lambda ref, p, core=core: ref.at[:, p[core]])
                for source, core in ((0, 8), (1, 9))
                for out in range(4)
            ],
        )
        od, ou, f1d, f2u = [stack.reshape(-1, STACK) for stack in stacks]
        self.stacks = (f1d, f2u)
        return self.piece2.sources, od, ou

    def third(self):
        base = 2 * self.width
        f1u, f2d = move(
            "stacks3", self.places, [self.hidden], [(16, 2, 128, STACK)] * 2,
            [
                (0, out,
                 lambda ref, p, out=out, side=side: ref.at[
                     :, :, :, pl.ds(base + (2 * out + side) * STACK, STACK)],
                 lambda ref, p, side=side: ref.at[:, :, pl.ds(side * 64, 64)])
                for out in range(2)
                for side in range(2)
            ],
            room=60 << 20,
        )
        f1d, f2u = self.stacks
        return self.hidden, (f1d, f1u.reshape(-1, STACK), f2d.reshape(-1, STACK), f2u)


class WholeGather:
    def __init__(self, qkv_weight, out_weight, fc1_weight, fc2_weight, shards):
        rows, _, column = qkv_weight.shape
        piece = jnp.concatenate(
            [fc1_weight, fc2_weight.T, qkv_weight.reshape(rows, 3 * column), out_weight.T],
            axis=1,
        )
        groups = lax.axis_size("tensor")
        self.joined = lax.all_gather(piece, BOTH, axis=0).reshape(-1, groups, *piece.shape)
        stacked = lax.all_gather(jnp.concatenate(shards, axis=0), BOTH, axis=0)
        self.full = []
        offset = 0
        for shard in shards:
            part = stacked[:, offset : offset + shard.shape[0]]
            self.full.append(part.reshape(-1, STACK))
            offset += shard.shape[0]
        start = 2 * fc1_weight.shape[1]
        by_group = self.joined[..., start:].transpose(1, 0, 2, 3)
        self.qkv, self.out = by_group[..., : 3 * column], by_group[..., 3 * column :]
        self.groups = jnp.arange(groups, dtype=jnp.int32)
        self.lane = 0

    def first(self):
        return (self.qkv,), self.full[0], self.full[1]

    def after_qkv(self, q):
        return q

    def second(self, o):
        return (self.out,), self.full[2], self.full[3]

    def third(self):
        return self.joined, self.full[4:]


def small_call(name, kernel, places, parts, outs):
    vmem = pl.BlockSpec(memory_space=pltpu.VMEM)
    return pl.pallas_call(
        kernel,
        in_specs=[smem()] + [vmem] * len(parts),
        out_specs=[vmem] * len(outs),
        out_shape=[jax.ShapeDtypeStruct(shape, dtype) for shape, dtype in outs],
        compiler_params=pltpu.CompilerParams(vmem_limit_bytes=24 << 20),
        name=name,
    )(places, *parts)


def add(*values):
    total = values[0].astype(f32)
    for value in values[1:]:
        total += value.astype(f32)
    return total


class StepScatter:
    def __init__(self, terms, tag):
        self.places, self.tag = positions(), tag
        self.widths = [term.shape[0] // 32 for term in terms]
        self.total = sum(self.widths)
        moves = []
        offset = 0
        for number, width in enumerate(self.widths):
            for out, core in enumerate((8, 9)):
                moves.append(
                    (number, out,
                     lambda ref, p, core=core: ref.at[:, :, :, p[core]],
                     lambda ref, p, offset=offset, width=width: ref.at[
                         :, :, :, pl.ds(offset, width)])
                )
            offset += width
        split = [
            term.reshape(4, 2, 2, 2, width, STACK) for term, width in zip(terms, self.widths)
        ]
        kept, sent = move(
            "scatter_core" + tag, self.places, split, [(4, 2, 2, self.total, STACK)] * 2, moves
        )
        self.parts = [kept, other_core(sent)]
        self.mark = kept

    def wait_for(self, other):
        self.parts[0] = after(self.parts[0], other)

    def layer(self):
        def kernel(p, kept, came, *outs):
            for out, y, x in zip(outs, (4, 4, 5, 5), (6, 7, 6, 7)):
                out[...] = add(kept[:, p[y], p[x]], came[:, p[y], p[x]]).astype(bf16)

        shape = ((4, self.total, STACK), bf16)
        own, to_x, to_y, to_both = small_call(
            "scatter_layer" + self.tag, kernel, self.places, self.parts, [shape] * 4
        )
        diagonal = lax.ppermute(to_both, "fsdp", [(f, f ^ 3) for f in range(16)])
        self.parts = [own, along_x(to_x), along_y(to_y), diagonal]
        self.mark = own

    def layers(self):
        def kernel(p, one, two, three, four, *outs):
            for shift, out in enumerate(outs):
                z = (p[0] + shift) % 4
                out[...] = add(one[z], two[z], three[z], four[z]).astype(out.dtype)

        own, *sends = small_call(
            "scatter_layers" + self.tag, kernel, self.places, self.parts,
            [((self.total, STACK), f32)] + [((self.total, STACK), bf16)] * 3,
        )
        self.parts = [own] + [along_z(send, shift + 1) for shift, send in enumerate(sends)]
        self.mark = own

    def finish(self):
        def kernel(p, own, first, second, third, *outs):
            value = add(own[...], first[...], second[...], third[...])
            offset = 0
            for width, out in zip(self.widths, outs):
                out[...] = value[offset : offset + width].T
                offset += width

        return small_call(
            "scatter_sum" + self.tag, kernel, self.places, self.parts,
            [((STACK, width), f32) for width in self.widths],
        )


class WholeScatter:
    def __init__(self, terms, tag):
        members = lax.axis_size(BOTH)
        packed = jnp.concatenate(
            [term.reshape(members, -1, STACK).astype(f32) for term in terms], axis=1
        )
        self.widths = [term.shape[0] // members for term in terms]
        self.summed = lax.psum_scatter(packed, BOTH, scatter_dimension=0, tiled=False)
        self.mark = terms[0]

    def wait_for(self, other):
        pass

    def layer(self):
        pass

    def layers(self):
        pass

    def finish(self):
        grads = []
        offset = 0
        for width in self.widths:
            grads.append(self.summed[offset : offset + width].T)
            offset += width
        return grads


def on_device(
    tokens,
    cotangent,
    adapter_index,
    filled,
    ln1_gain,
    ln1_shift,
    qkv_weight,
    qv_bias,
    out_weight,
    out_bias,
    ln2_gain,
    ln2_shift,
    fc1_weight,
    fc1_bias,
    fc2_weight,
    fc2_bias,
    qkv_down,
    qkv_up,
    out_down,
    out_up,
    fc1_down,
    fc1_up,
    fc2_down,
    fc2_up,
):
    images = tokens.shape[0]
    own_start = lax.axis_index("tensor") * images
    index = lax.dynamic_slice_in_dim(adapter_index, own_start, images, 0)
    mask = lax.dynamic_slice_in_dim(filled, own_start, images, 0)
    stack_list = (qkv_down, qkv_up, out_down, out_up, fc1_down, fc1_up, fc2_down, fc2_up)
    steps = (lax.axis_size("fsdp"), lax.axis_size("tensor"), images) == STEPS
    shards = [transposed(stacked) for stacked in stack_list]
    gather = (StepGather if steps else WholeGather)(
        qkv_weight, out_weight, fc1_weight, fc2_weight, shards
    )
    scatter = StepScatter if steps else WholeScatter
    groups = gather.groups
    row = lambda vector: vector.astype(f32)[None, :]
    qkv_sources, qkv_down_full, qkv_up_full = gather.first()
    q, k, v, low_one = qkv_project(
        tokens, qkv_sources, groups, qkv_down_full, qkv_up_full, index, qv_bias, row(ln1_gain),
        row(ln1_shift),
    )
    q = gather.after_qkv(q)
    mixed = None
    for image in range(images):
        mixed = attend(q, k, v, image, mixed)
    o, prob = mixed
    out_sources, out_down_full, out_up_full = gather.second(o)
    h, low_out = out_project(
        tokens, o, out_sources, gather.lane, groups, out_down_full, out_up_full, index, mask,
        row(out_bias),
    )
    mlp_weights, stacks = gather.third()
    outputs, dh, grad_up2, grad_down2, grad_up1, grad_down1 = mlp(
        h, cotangent, mlp_weights, *stacks, index, mask,
        row(fc1_bias), row(fc2_bias), row(ln2_gain), row(ln2_shift),
    )
    do, grad_out_up, grad_out_down = out_back(
        dh, o, low_out, out_sources, gather.lane, groups, out_down_full, out_up_full, index, mask
    )
    early = scatter(
        [grad_out_down, grad_out_up, grad_down1, grad_up1, grad_down2, grad_up2], "1"
    )
    do = after(do, early.mark)
    grads = None
    for image in range(images):
        grads = attend_back(q, k, v, do, prob, image, grads)
        if image == 0:
            early.wait_for(grads[0])
            early.layer()
            grads = (after(grads[0], early.mark), *grads[1:])
    dq, dk, dv = grads
    early.wait_for(dq)
    early.layers()
    dq = after(dq, early.mark)
    low_grad, grad_qkv_up, grad_qkv_down = qkv_grads(
        tokens, dq, dk, dv, low_one, qkv_up_full, index, row(ln1_gain), row(ln1_shift)
    )
    late = scatter([grad_qkv_down, grad_qkv_up], "2")
    low_grad = after(low_grad, late.mark)
    input_grad = None
    for image in range(images):
        input_grad = qkv_back(
            tokens, dh, dq, dk, dv, low_grad, qkv_sources, groups, qkv_down_full,
            row(ln1_gain), image, input_grad,
        )
        if image == 0:
            late.wait_for(input_grad)
            late.layer()
            input_grad = after(input_grad, late.mark)
    late.layers()
    grads = [grad.reshape(ADAPTERS, RANK, -1) for grad in (*late.finish(), *early.finish())]
    return (outputs, input_grad, *grads)


def solution(mesh):
    images = P(BOTH, None, None)
    stacked = P(None, None, BOTH)
    in_specs = (
        images, images, P("fsdp"), P("fsdp"), P(), P(), P("fsdp", None, "tensor"), P(),
        P("tensor", "fsdp"), P(), P(), P(), P("fsdp", "tensor"), P(), P("tensor", "fsdp"), P(),
    ) + (stacked,) * 8
    out_specs = (images, images) + (stacked,) * 8
    return jax.shard_map(
        on_device, mesh=mesh, in_specs=in_specs, out_specs=out_specs, check_vma=False
    )
```

```python
import math
from functools import partial

import jax
import jax.numpy as jnp
from jax import lax
from jax.experimental import pallas as pl
from jax.experimental.pallas import tpu as pltpu
from jax.sharding import PartitionSpec as P

D = 1024
HEADS = 16
HEAD_DIM = 64
FF = 4096
SEQ = 577
RANK = 16
ADAPTERS = 8
STACK = ADAPTERS * RANK
TILE = 1024

epsilon = 1e-05
bf16 = jnp.bfloat16
f32 = jnp.float32
NN = (((1,), (0,)), ((), ()))
NT = (((1,), (1,)), ((), ()))
TN = (((0,), (0,)), ((), ()))
BOTH = ("fsdp", "tensor")


def dot(left, right, dims):
    return lax.dot_general(left, right, dims, preferred_element_type=f32)


def params():
    return pltpu.CompilerParams(vmem_limit_bytes=60 << 20)


def cost(flops, moved, exps=0):
    return pl.CostEstimate(flops=flops, bytes_accessed=moved, transcendentals=exps)


def smem():
    return pl.BlockSpec(memory_space=pltpu.SMEM)


def whole(shape):
    return pl.BlockSpec(shape, lambda *_: (0,) * len(shape), pipeline_mode=pl.Buffered(1))


def image_rows(width=D):
    return pl.BlockSpec((pl.Squeezed(), SEQ, width), lambda i: (i, 0, 0))


def normalize(values):
    center = values - jnp.mean(values, axis=-1, keepdims=True)
    inverse = lax.rsqrt(jnp.mean(center * center, axis=-1, keepdims=True) + epsilon)
    return center * inverse, inverse


def norm_back(upstream, normed, inverse, gain_row):
    scaled = upstream * gain_row
    return inverse * (
        scaled
        - jnp.mean(scaled, axis=-1, keepdims=True)
        - normed * jnp.mean(scaled * normed, axis=-1, keepdims=True)
    )


def chosen_lanes(adapter):
    lanes = lax.broadcasted_iota(jnp.int32, (1, STACK), 1)
    return (lanes // RANK) == adapter


def keep(product, adapter):
    return jnp.where(chosen_lanes(adapter), product, 0.0).astype(bf16)


def add_to(ref, value, first):
    @pl.when(first)
    def _():
        ref[...] = value

    @pl.when(jnp.logical_not(first))
    def _():
        ref[...] += value


def flat(block):
    return block.reshape(D, block.shape[-1])


def any_space():
    return pl.BlockSpec(memory_space=pl.ANY)


def untangle_kernel(mixed_ref, out_ref):
    for image in range(out_ref.shape[0]):
        out_ref[image] = mixed_ref[:, image, :]


def untangle(array):
    images = array.shape[0]
    return pl.pallas_call(
        untangle_kernel,
        grid=(1,),
        in_specs=[whole((SEQ, images, D))],
        out_specs=whole((images, SEQ, D)),
        out_shape=jax.ShapeDtypeStruct((images, SEQ, D), array.dtype),
        compiler_params=pltpu.CompilerParams(vmem_limit_bytes=32 << 20),
        name="untangle",
    )(array.transpose(1, 0, 2))


class Stream:
    def __init__(self, sources, lane, width, slots, sems):
        self.sources, self.lane, self.width = sources, lane, width
        self.slots, self.sems = slots, sems

    def copy(self, source, inner, slot):
        lanes = pl.ds(self.lane, self.width)
        return pltpu.make_async_copy(
            source.at[inner, :, :, lanes], self.slots.at[slot], self.sems.at[slot]
        )

    def start(self, group, slot):
        offset = 0
        for source in self.sources:
            count = source.shape[0]

            @pl.when(jnp.logical_and(group >= offset, group < offset + count))
            def _(source=source, offset=offset):
                self.copy(source, group - offset, slot).start()

            offset += count

    def wait(self, slot):
        self.copy(self.sources[0], 0, slot).wait()


def spread_copies(sources, lane, parts, table_ref, weight_ref, sem):
    members, rows, total = weight_ref.shape
    groups = group_count(sources)
    width = total // parts // groups
    group = 0
    for source in sources:
        for inner in range(source.shape[0]):
            start = pl.multiple_of(table_ref[group] * width, width)
            for part in range(parts):
                yield pltpu.make_async_copy(
                    source.at[inner, :, :, pl.ds(lane + part * width, width)],
                    weight_ref.at[:, :, pl.ds(part * width * groups + start, width)],
                    sem.at[group * parts + part],
                )
            group += 1


def spread_scratch(sources, parts):
    members, rows = sources[0].shape[1:3]
    return [
        pltpu.VMEM((members, rows, parts * D), bf16),
        pltpu.SemaphoreType.DMA((group_count(sources) * parts,)),
    ]


def qkv_kernel(count, *refs):
    table_ref, index_ref, tokens_ref = refs[:3]
    sources = refs[3 : 3 + count]
    down_ref, up_ref, bias_ref, gain_ref, shift_ref = refs[3 + count : 8 + count]
    q_ref, k_ref, v_ref, low_ref, a_s, low_s, slots, sems = refs[8 + count :]
    group = pl.program_id(0)
    image = pl.program_id(1)
    width = q_ref.shape[-1]
    stream = Stream(sources, 0, 3 * width, slots, sems)
    slot = group % 2

    @pl.when(jnp.logical_and(group == 0, image == 0))
    def _():
        stream.start(group, 0)

    @pl.when(group == 0)
    def _():
        normed, _ = normalize(tokens_ref[...].astype(f32))
        a = (normed * gain_ref[...] + shift_ref[...]).astype(bf16)
        a_s[image] = a
        low_s[image] = keep(dot(a, down_ref[...], NN), index_ref[image])

    @pl.when(image == 0)
    def _():
        stream.wait(slot)

        @pl.when(group + 1 < pl.num_programs(0))
        def _():
            stream.start(group + 1, 1 - slot)

    a = a_s[image]
    low = low_s[image]
    low_ref[...] = low
    weight = flat(slots[slot])
    start = pl.multiple_of(table_ref[group] * width, width)
    bias = bias_ref[...].astype(f32)
    for part, out_ref in enumerate((q_ref, k_ref, v_ref)):
        value = dot(a, weight[:, part * width : (part + 1) * width], NN)
        value += dot(low, up_ref[pl.ds(part * D + start, width), :], NT)
        if part != 1:
            value += bias[part // 2 : part // 2 + 1]
        out_ref[...] = value.astype(bf16)


def group_count(sources):
    return sum(source.shape[0] for source in sources)


def qkv_project(tokens, sources, table, down, up, index, bias, gain, shift):
    images = tokens.shape[0]
    members, rows = sources[0].shape[1:3]
    groups = group_count(sources)
    width = D // groups
    sq = pl.Squeezed()
    out = pl.BlockSpec((sq, SEQ, width), lambda g, i, t: (i, 0, t[g]))
    vector = whole((1, D))
    grid_spec = pltpu.PrefetchScalarGridSpec(
        num_scalar_prefetch=1,
        grid=(groups, images),
        in_specs=[smem(), pl.BlockSpec((sq, SEQ, D), lambda g, i, t: (i, 0, 0))]
        + [any_space()] * len(sources)
        + [
            whole((D, STACK)),
            whole((3 * D, STACK)),
            pl.BlockSpec((2, width), lambda g, i, t: (0, t[g])),
            vector,
            vector,
        ],
        out_specs=[out, out, out, pl.BlockSpec((sq, SEQ, STACK), lambda g, i, t: (i, 0, 0))],
        scratch_shapes=[
            pltpu.VMEM((images, SEQ, D), bf16),
            pltpu.VMEM((images, SEQ, STACK), bf16),
            pltpu.VMEM((2, members, rows, 3 * width), bf16),
            pltpu.SemaphoreType.DMA((2,)),
        ],
    )
    return pl.pallas_call(
        partial(qkv_kernel, len(sources)),
        grid_spec=grid_spec,
        out_shape=[jax.ShapeDtypeStruct((images, SEQ, D), bf16)] * 3
        + [jax.ShapeDtypeStruct((images, SEQ, STACK), bf16)],
        compiler_params=params(),
        cost_estimate=cost(6 * images * SEQ * D * D, 20 << 20),
        name="qkv_project",
    )(table, index, tokens, *sources, down, up, bias, gain, shift)


def attend_kernel(q_ref, k_ref, v_ref, o_ref, w_ref, scale_ref):
    q = q_ref[...]
    k = k_ref[...]
    v = v_ref[...]
    low = lax.broadcasted_iota(jnp.int32, q.shape, 1) < HEAD_DIM
    both = jnp.concatenate([v, jnp.ones_like(v)], axis=1)
    outs = []
    for head in range(2):
        own = low if head == 0 else jnp.logical_not(low)
        queries = jnp.where(own, q * HEAD_DIM**-0.5, jnp.zeros_like(q)).astype(bf16)
        scores = dot(queries, k, NT)
        raised = jnp.exp(scores - jnp.max(scores, axis=-1, keepdims=True)).astype(bf16)
        w_ref[head] = raised
        outs.append(dot(raised, both, NN))
    width = v.shape[-1]
    scale = 1.0 / jnp.where(low, outs[0][:, width:], outs[1][:, width:])
    scale_ref[...] = scale
    o_ref[...] = (jnp.where(low, outs[0][:, :width], outs[1][:, :width]) * scale).astype(bf16)


def pair_rows(image):
    return pl.BlockSpec((pl.Squeezed(), SEQ, 2 * HEAD_DIM), lambda h: (image, 0, h))


def pair_weights(image):
    return pl.BlockSpec((2, SEQ, SEQ), lambda h: (image * (HEADS // 2) + h, 0, 0))


def into(kernel, inputs):
    def body(*refs):
        kernel(*refs[:inputs], *refs[len(refs) - (len(refs) - inputs) // 2 :])

    return body


def per_image(kernel, name, image, inputs, in_specs, outs, out_specs, filled, flops, moved, exps):
    count = len(inputs)
    if filled is None:
        return pl.pallas_call(
            kernel, grid=(HEADS // 2,), in_specs=in_specs, out_specs=out_specs, out_shape=outs,
            compiler_params=params(), cost_estimate=cost(flops, moved, exps), name=name,
        )(*inputs)
    return pl.pallas_call(
        into(kernel, count), grid=(HEADS // 2,), in_specs=in_specs + [any_space()] * len(outs),
        out_specs=out_specs, out_shape=outs,
        input_output_aliases={count + n: n for n in range(len(outs))},
        compiler_params=params(), cost_estimate=cost(flops, moved, exps), name=name,
    )(*inputs, *filled)


def attend(q, k, v, image, filled):
    images = q.shape[0]
    outs = [
        jax.ShapeDtypeStruct((images, SEQ, D), bf16),
        jax.ShapeDtypeStruct((images * HEADS, SEQ, SEQ), bf16),
        jax.ShapeDtypeStruct((images, SEQ, D), f32),
    ]
    return per_image(
        attend_kernel, "attend", image, (q, k, v), [pair_rows(image)] * 3, outs,
        [pair_rows(image), pair_weights(image), pair_rows(image)], filled,
        16 * SEQ * SEQ * D, 20 << 20, HEADS * SEQ * SEQ,
    )


def attend_back_kernel(
    q_ref, k_ref, v_ref, do_ref, o_ref, w_ref, scale_ref, dq_ref, dk_ref, dv_ref
):
    q = q_ref[...]
    k = k_ref[...]
    v = v_ref[...]
    do = (do_ref[...].astype(f32) * scale_ref[...]).astype(bf16)
    products = do.astype(f32) * o_ref[...].astype(f32)
    low = lax.broadcasted_iota(jnp.int32, q.shape, 1) < HEAD_DIM
    grads = []
    for head in range(2):
        own = low if head == 0 else jnp.logical_not(low)
        mixed_grad = jnp.where(own, do, jnp.zeros_like(do))
        inner = jnp.sum(jnp.where(own, products, 0.0), axis=-1, keepdims=True)
        raised = w_ref[head]
        prob_grad = dot(mixed_grad, v, NT)
        score_grad = (raised.astype(f32) * (prob_grad - inner)).astype(bf16)
        grads.append((dot(score_grad, k, NN), dot(score_grad, q, TN), dot(raised, do, TN)))
    scale = HEAD_DIM**-0.5
    dq_ref[...] = (jnp.where(low, grads[0][0], grads[1][0]) * scale).astype(bf16)
    dk_ref[...] = (jnp.where(low, grads[0][1], grads[1][1]) * scale).astype(bf16)
    dv_ref[...] = jnp.where(low, grads[0][2], grads[1][2]).astype(bf16)


def attend_back(q, k, v, do, o, kept, image, filled):
    outs = [jax.ShapeDtypeStruct(q.shape, bf16)] * 3
    return per_image(
        attend_back_kernel, "attend_back", image, (q, k, v, do, o, *kept),
        [pair_rows(image)] * 5 + [pair_weights(image), pair_rows(image)], outs,
        [pair_rows(image)] * 3, filled, 32 * SEQ * SEQ * D, 24 << 20, 0,
    )


def out_kernel(count, lane, *refs):
    table_ref, index_ref, filled_ref, tokens_ref, o_ref = refs[:5]
    sources = refs[5 : 5 + count]
    down_ref, up_ref, bias_ref, h_ref, low_ref, weight_s, sems = refs[5 + count :]
    image = pl.program_id(0)

    @pl.when(image == 0)
    def _():
        for copy in spread_copies(sources, lane, 1, table_ref, weight_s, sems):
            copy.start()

    low = keep(dot(o_ref[...], down_ref[...], NN), index_ref[image])
    low_ref[...] = low

    @pl.when(image == 0)
    def _():
        for copy in spread_copies(sources, lane, 1, table_ref, weight_s, sems):
            copy.wait()

    value = dot(o_ref[...], flat(weight_s[...]), NT) + dot(low, up_ref[...], NT) + bias_ref[...]
    h_ref[...] = tokens_ref[...].astype(f32) + filled_ref[image].astype(f32) * value


def out_project(tokens, o, sources, lane, table, down, up, index, filled, bias):
    images = tokens.shape[0]
    return pl.pallas_call(
        partial(out_kernel, len(sources), lane),
        grid=(images,),
        in_specs=[smem(), smem(), smem(), image_rows(), image_rows()]
        + [any_space()] * len(sources)
        + [whole((D, STACK)), whole((D, STACK)), whole((1, D))],
        out_specs=[image_rows(), image_rows(STACK)],
        out_shape=[
            jax.ShapeDtypeStruct((images, SEQ, D), f32),
            jax.ShapeDtypeStruct((images, SEQ, STACK), bf16),
        ],
        scratch_shapes=spread_scratch(sources, 1),
        compiler_params=params(),
        cost_estimate=cost(2 * images * SEQ * D * D, 12 << 20),
        name="out_project",
    )(table, index, filled, tokens, o, *sources, down, up, bias)


def out_back_kernel(count, lane, *refs):
    table_ref, index_ref, filled_ref, dh_ref, o_ref, low_ref = refs[:6]
    sources = refs[6 : 6 + count]
    down_ref, up_ref, do_ref, grad_up_ref, grad_down_ref = refs[6 + count : 11 + count]
    grad_up_s, grad_down_s, weight_s, sems = refs[11 + count :]
    image = pl.program_id(0)
    last = image == pl.num_programs(0) - 1

    @pl.when(image == 0)
    def _():
        for copy in spread_copies(sources, lane, 1, table_ref, weight_s, sems):
            copy.start()
        grad_up_s[...] = jnp.zeros_like(grad_up_s)
        grad_down_s[...] = jnp.zeros_like(grad_down_s)

    branch = (dh_ref[...] * filled_ref[image].astype(f32)).astype(bf16)
    low_grad = keep(dot(branch, up_ref[...], NN), index_ref[image])
    grad_up_s[...] += dot(low_ref[...], branch, TN)
    grad_down_s[...] += dot(low_grad, o_ref[...], TN)

    @pl.when(image == 0)
    def _():
        for copy in spread_copies(sources, lane, 1, table_ref, weight_s, sems):
            copy.wait()

    value = dot(branch, flat(weight_s[...]), NN) + dot(low_grad, down_ref[...], NT)
    do_ref[...] = value.astype(bf16)

    @pl.when(last)
    def _():
        grad_up_ref[...] = grad_up_s[...].T.astype(bf16)
        grad_down_ref[...] = grad_down_s[...].T.astype(bf16)


def out_back(dh, o, low, sources, lane, table, down, up, index, filled):
    images = dh.shape[0]
    grad = pl.BlockSpec((D, STACK), lambda i: (0, 0))
    return pl.pallas_call(
        partial(out_back_kernel, len(sources), lane),
        grid=(images,),
        in_specs=[smem(), smem(), smem(), image_rows(), image_rows(), image_rows(STACK)]
        + [any_space()] * len(sources)
        + [whole((D, STACK)), whole((D, STACK))],
        out_specs=[image_rows(), grad, grad],
        out_shape=[jax.ShapeDtypeStruct((images, SEQ, D), bf16)]
        + [jax.ShapeDtypeStruct((D, STACK), bf16)] * 2,
        scratch_shapes=[pltpu.VMEM((STACK, D), f32)] * 2 + spread_scratch(sources, 1),
        compiler_params=params(),
        cost_estimate=cost(2 * images * SEQ * D * D, 12 << 20),
        name="out_back",
    )(table, index, filled, dh, o, low, *sources, down, up)


def mlp_kernel(sides, *refs):
    index_ref, filled_ref, h_ref, cot_ref, first_ref, second_ref, down1_ref = refs[:7]
    up1_refs = refs[7 : 7 + sides]
    down2_refs = refs[7 + sides : 7 + 2 * sides]
    (
        up2_ref, bias1_ref, bias2_ref, gain_ref, shift_ref,
        out_ref, dh_ref, grad_up2_ref, grad_down2_ref, grad_up1_ref, grad_down1_ref,
        a_s, dz_s, low3_s, dlow4_s, z_s, da_s, low4_s, dlow3_s,
        grad_up2_s, grad_down2_s, grad_up1_s, grad_down1_s,
    ) = refs[7 + 2 * sides :]
    width = grad_up1_ref.shape[0]
    tall = lambda parts: jnp.concatenate([part[...] for part in parts], axis=2).reshape(
        width, STACK
    )
    up1 = tall(up1_refs)
    down2 = tall(down2_refs)
    tile = pl.program_id(0)
    image = pl.program_id(1)
    last = tile == pl.num_programs(0) - 1
    final = image == pl.num_programs(1) - 1
    adapter = index_ref[image]
    mask = filled_ref[image].astype(f32)

    @pl.when(image == 0)
    def _():
        grad_down2_s[...] = jnp.zeros_like(grad_down2_s)
        grad_up1_s[...] = jnp.zeros_like(grad_up1_s)

    @pl.when(tile == 0)
    def _():
        for ref in (z_s, da_s, low4_s, dlow3_s):
            ref[image] = jnp.zeros(ref.shape[1:], f32)
        normed, _ = normalize(h_ref[image])
        a = (normed * gain_ref[...] + shift_ref[...]).astype(bf16)
        a_s[image] = a
        dz = (cot_ref[image].astype(f32) * mask).astype(bf16)
        dz_s[image] = dz
        low3_s[image] = keep(dot(a, down1_ref[...], NN), adapter)
        dlow4_s[image] = keep(dot(dz, up2_ref[...], NN), adapter)

    a = a_s[image]
    dz = dz_s[image]
    low3 = low3_s[image]
    dlow4 = dlow4_s[image]
    first = flat(first_ref[...])
    second = flat(second_ref[...])
    before = dot(a, first, NN) + dot(low3, up1, NT) + bias1_ref[...]
    density = jnp.exp(before * before * -0.5) * 0.3989422804014327
    below = 0.5 * lax.erf(before * 0.7071067811865476) + 0.5
    g = (before * below).astype(bf16)
    slope = below + before * density
    dg = dot(dz, second, NN) + dot(dlow4, down2, NT)
    df = (dg * slope).astype(bf16)
    z_s[image] += dot(g, second, NT)
    da_s[image] += dot(df, first, NT)
    low4_s[image] += dot(g, down2, NN)
    dlow3_s[image] += dot(df, up1, NN)
    grad_down2_s[...] += dot(dlow4, g, TN)
    grad_up1_s[...] += dot(low3, df, TN)

    @pl.when(final)
    def _():
        grad_down2_ref[...] = grad_down2_s[...].T.astype(bf16)
        grad_up1_ref[...] = grad_up1_s[...].T.astype(bf16)

    @pl.when(last)
    def _():
        low4 = keep(low4_s[image], adapter)
        h = h_ref[image]
        z = z_s[image] + dot(low4, up2_ref[...], NT) + bias2_ref[...]
        outputs = (h + mask * z).astype(bf16)
        for number in range(out_ref.shape[1]):

            @pl.when(image == number)
            def _(number=number):
                out_ref[:, number, :] = outputs

        add_to(grad_up2_s, dot(low4, dz, TN), image == 0)
        dlow3 = keep(dlow3_s[image], adapter)
        da = da_s[image] + dot(dlow3, down1_ref[...], NT)
        add_to(grad_down1_s, dot(dlow3, a, TN), image == 0)
        normed, inverse = normalize(h)
        dh_ref[...] = cot_ref[image].astype(f32) + norm_back(
            da, normed, inverse, gain_ref[...]
        )

    @pl.when(jnp.logical_and(last, final))
    def _():
        grad_up2_ref[...] = grad_up2_s[...].T.astype(bf16)
        grad_down1_ref[...] = grad_down1_s[...].T.astype(bf16)


def mlp(h, cot, weights, down1, up1, down2, up2, index, filled, bias1, bias2, gain, shift):
    images = h.shape[0]
    members, groups, rows, _ = weights.shape
    hidden = FF // groups
    width = min(TILE, hidden)
    per_group = hidden // width
    tiles = FF // width
    sq = pl.Squeezed()

    def weight(base):
        return pl.BlockSpec(
            (members, sq, rows, width),
            lambda j, i: (0, j // per_group, 0, base * per_group + j % per_group),
        )

    tall = pl.BlockSpec((width, STACK), lambda j, i: (j, 0))
    sides = up1 + down2

    def side_block(array, lane):
        shape = (16 * width // FF, 2, FF // 32 // len(up1), STACK)
        return pl.BlockSpec(shape, lambda j, i: (j, 0, 0, lane))

    short = pl.BlockSpec((D, STACK), lambda j, i: (0, 0))
    late = pl.BlockSpec((sq, SEQ, D), lambda j, i: (jnp.where(j == tiles - 1, i, 0), 0, 0))
    return pl.pallas_call(
        partial(mlp_kernel, len(up1)),
        grid=(tiles, images),
        in_specs=[
            smem(),
            smem(),
            whole((images, SEQ, D)),
            whole((images, SEQ, D)),
            weight(0),
            weight(1),
            whole((D, STACK)),
        ]
        + [side_block(*side) for side in sides]
        + [
            whole((D, STACK)),
            pl.BlockSpec((1, width), lambda j, i: (0, j)),
            whole((1, D)),
            whole((1, D)),
            whole((1, D)),
        ],
        out_specs=[pl.BlockSpec((SEQ, images, D), lambda j, i: (0, 0, 0)), late, short, tall, tall, short],
        out_shape=[
            jax.ShapeDtypeStruct((SEQ, images, D), bf16),
            jax.ShapeDtypeStruct((images, SEQ, D), f32),
            jax.ShapeDtypeStruct((D, STACK), bf16),
            jax.ShapeDtypeStruct((FF, STACK), bf16),
            jax.ShapeDtypeStruct((FF, STACK), bf16),
            jax.ShapeDtypeStruct((D, STACK), bf16),
        ],
        scratch_shapes=[
            pltpu.VMEM((images, SEQ, D), bf16),
            pltpu.VMEM((images, SEQ, D), bf16),
            pltpu.VMEM((images, SEQ, STACK), bf16),
            pltpu.VMEM((images, SEQ, STACK), bf16),
            pltpu.VMEM((images, SEQ, D), f32),
            pltpu.VMEM((images, SEQ, D), f32),
            pltpu.VMEM((images, SEQ, STACK), f32),
            pltpu.VMEM((images, SEQ, STACK), f32),
            pltpu.VMEM((STACK, D), f32),
            pltpu.VMEM((STACK, width), f32),
            pltpu.VMEM((STACK, width), f32),
            pltpu.VMEM((STACK, D), f32),
        ],
        compiler_params=params(),
        cost_estimate=cost(8 * images * SEQ * D * FF, 40 << 20, 2 * images * SEQ * FF),
        name="mlp",
    )(
        index, filled, h, cot, weights, weights, down1, *[array for array, _ in sides], up2,
        bias1, bias2, gain, shift,
    )


def qkv_grads_kernel(
    index_ref, tokens_ref, dq_ref, dk_ref, dv_ref, low_ref, up_ref, gain_ref, shift_ref,
    low_grad_ref, grad_up_ref, grad_down_ref, grad_up_s, grad_down_s,
):
    image = pl.program_id(0)
    parts = (dq_ref, dk_ref, dv_ref)

    @pl.when(image == 0)
    def _():
        grad_up_s[...] = jnp.zeros_like(grad_up_s)
        grad_down_s[...] = jnp.zeros_like(grad_down_s)

    low = low_ref[...]
    low_grad = dot(parts[0][...], up_ref[0:D, :], NN)
    for part in (1, 2):
        low_grad += dot(parts[part][...], up_ref[part * D : (part + 1) * D, :], NN)
    low_grad = keep(low_grad, index_ref[image])
    low_grad_ref[...] = low_grad
    for part in range(3):
        grad_up_s[part] += dot(low, parts[part][...], TN)
    normed, _ = normalize(tokens_ref[...].astype(f32))
    a = (normed * gain_ref[...] + shift_ref[...]).astype(bf16)
    grad_down_s[...] += dot(low_grad, a, TN)

    @pl.when(image == pl.num_programs(0) - 1)
    def _():
        for part in range(3):
            grad_up_ref[part * D : (part + 1) * D, :] = grad_up_s[part].T.astype(bf16)
        grad_down_ref[...] = grad_down_s[...].T.astype(bf16)


def qkv_grads(tokens, dq, dk, dv, low, up, index, gain, shift):
    images = tokens.shape[0]
    return pl.pallas_call(
        qkv_grads_kernel,
        grid=(images,),
        in_specs=[smem()]
        + [image_rows()] * 4
        + [image_rows(STACK), whole((3 * D, STACK)), whole((1, D)), whole((1, D))],
        out_specs=[
            image_rows(STACK),
            pl.BlockSpec((3 * D, STACK), lambda i: (0, 0)),
            pl.BlockSpec((D, STACK), lambda i: (0, 0)),
        ],
        out_shape=[
            jax.ShapeDtypeStruct((images, SEQ, STACK), bf16),
            jax.ShapeDtypeStruct((3 * D, STACK), bf16),
            jax.ShapeDtypeStruct((D, STACK), bf16),
        ],
        scratch_shapes=[pltpu.VMEM((3, STACK, D), f32), pltpu.VMEM((STACK, D), f32)],
        compiler_params=params(),
        cost_estimate=cost(2 * images * SEQ * D * D, 12 << 20),
        name="qkv_grads",
    )(index, tokens, dq, dk, dv, low, up, gain, shift)


def qkv_back_kernel(count, image, *refs):
    table_ref = refs[0]
    arrays = refs[1:6]
    low_grad_ref = refs[6]
    sources = refs[7 : 7 + count]
    down_ref, gain_ref = refs[7 + count : 9 + count]
    grad_ref, dq_s, dk_s, dv_s, tokens_s, dh_s, earlier_s, row_sems, weight_s, sems = refs[-10:]
    earlier_refs = refs[9 + count : -10]
    weights = list(spread_copies(sources, 0, 3, table_ref, weight_s, sems))
    held = (tokens_s, dh_s, dq_s, dk_s, dv_s)
    rows = [
        pltpu.make_async_copy(array.at[image], into_ref, row_sems.at[number])
        for number, (array, into_ref) in enumerate(zip(arrays, held))
    ]
    before = [
        pltpu.make_async_copy(ref, earlier_s.at[number], row_sems.at[len(rows) + number])
        for number, ref in enumerate(earlier_refs)
    ]
    for part in range(3):
        rows[2 + part].start()
        for copy in weights[part::3]:
            copy.start()
    for copy in (rows[0], rows[1], *before):
        copy.start()
    da = dot(low_grad_ref[...], down_ref[...], NT)
    for part, part_s in enumerate((dq_s, dk_s, dv_s)):
        rows[2 + part].wait()
        for copy in weights[part::3]:
            copy.wait()
        da += dot(part_s[...], flat(weight_s[:, :, part * D : (part + 1) * D]), NT)
    rows[0].wait()
    normed, inverse = normalize(tokens_s[...].astype(f32))
    rows[1].wait()
    grad = dh_s[...] + norm_back(da, normed, inverse, gain_ref[...])
    if len(grad_ref.shape) == 2:
        grad_ref[...] = grad
    else:
        for number, copy in enumerate(before):
            copy.wait()
            grad_ref[:, number, :] = earlier_s[number]
        grad_ref[:, len(before), :] = grad


def qkv_back(tokens, dh, dq, dk, dv, low_grad, sources, table, down, gain, earlier):
    images = tokens.shape[0]
    image = len(earlier)
    out = (SEQ, D) if image + 1 < images else (SEQ, images, D)
    return pl.pallas_call(
        partial(qkv_back_kernel, len(sources), image),
        grid=(1,),
        in_specs=[smem()]
        + [any_space()] * 5
        + [pl.BlockSpec((pl.Squeezed(), SEQ, STACK), lambda i: (image, 0, 0))]
        + [any_space()] * len(sources)
        + [whole((D, STACK)), whole((1, D))]
        + [any_space()] * image,
        out_specs=whole(out),
        out_shape=jax.ShapeDtypeStruct(out, f32),
        scratch_shapes=[pltpu.VMEM((SEQ, D), bf16)] * 4
        + [
            pltpu.VMEM((SEQ, D), f32),
            pltpu.VMEM((max(image, 1), SEQ, D), f32),
            pltpu.SemaphoreType.DMA((5 + max(image, 1),)),
        ]
        + spread_scratch(sources, 3),
        compiler_params=params(),
        cost_estimate=cost(6 * SEQ * D * D, 18 << 20),
        name="qkv_back",
    )(table, tokens, dh, dq, dk, dv, low_grad, *sources, down, gain, *earlier)


STEPS = (16, 2, 2)


def along_x(array):
    return lax.ppermute(array, "fsdp", [(f, f ^ 1) for f in range(16)])


def along_y(array):
    return lax.ppermute(array, "fsdp", [(f, f ^ 2) for f in range(16)])


def along_z(array, shift):
    pairs = [(f, (f // 4 + shift) % 4 * 4 + f % 4) for f in range(16)]
    return lax.ppermute(array, "fsdp", pairs)


def other_core(array):
    return lax.ppermute(array, "tensor", [(0, 1), (1, 0)])


def positions():
    f = lax.axis_index("fsdp")
    t = lax.axis_index("tensor")
    z, y, x = f // 4, f // 2 % 2, f % 2
    places = [z, (z + 3) % 4, (z + 2) % 4, (z + 1) % 4, y, 1 - y, x, 1 - x, t, 1 - t]
    return jnp.stack(places).astype(jnp.int32)


def move(name, places, parts, outs, moves, room=None):
    room = room or (4 << 20) + sum(2 * math.prod(shape) for shape in outs)

    def kernel(places_ref, *refs):
        sems = refs[-1]
        copies = []
        for number, (part, out, source, target) in enumerate(moves):
            copies.append(
                pltpu.make_async_copy(
                    source(refs[part], places_ref),
                    target(refs[len(parts) + out], places_ref),
                    sems.at[number],
                )
            )
            copies[-1].start()
        for copy in copies:
            copy.wait()

    return pl.pallas_call(
        kernel,
        in_specs=[smem()] + [any_space()] * len(parts),
        out_specs=[pl.BlockSpec(memory_space=pltpu.VMEM)] * len(outs),
        out_shape=[jax.ShapeDtypeStruct(shape, bf16) for shape in outs],
        scratch_shapes=[pltpu.SemaphoreType.DMA((len(moves),))],
        compiler_params=pltpu.CompilerParams(vmem_limit_bytes=room),
        name=name,
    )(places, *parts)


def everything(ref, places):
    return ref


def after(value, *others):
    return lax.optimization_barrier((value, *others))[0]


class Piece:
    def __init__(self, shard, places, tag):
        self.shard, self.places, self.tag = shard, places, tag
        self.rows, self.half = shard.shape[0], shard.shape[1] // 2

    def send_z(self):
        self.parts = [self.shard] + [along_z(self.shard, shift) for shift in (1, 2, 3)]

    def wait_for(self, other):
        self.parts[0] = after(self.parts[0], other)

    def join_z(self):
        half = self.half
        self.a, self.b = move(
            "gather_z" + self.tag, self.places, self.parts, [(4, self.rows, half)] * 2,
            [
                (
                    shift, side,
                    lambda ref, p, side=side: ref.at[:, pl.ds(side * half, half)],
                    lambda ref, p, shift=shift: ref.at[p[shift]],
                )
                for shift in range(4)
                for side in range(2)
            ],
        )

    def send_half(self):
        self.parts = [self.a, along_y(self.a), self.b, along_x(self.b)]

    def join_half(self):
        self.a, self.b = move(
            "gather_yx" + self.tag, self.places, self.parts, [(4, 2, self.rows, self.half)] * 2,
            [
                (0, 0, everything, lambda ref, p: ref.at[:, p[4]]),
                (1, 0, everything, lambda ref, p: ref.at[:, p[5]]),
                (2, 1, everything, lambda ref, p: ref.at[:, p[6]]),
                (3, 1, everything, lambda ref, p: ref.at[:, p[7]]),
            ],
        )

    def send_rest(self):
        self.parts = [self.a, along_x(self.a), self.b, along_y(self.b)]

    def join_rest(self):
        (joined,) = move(
            "gather_xy" + self.tag, self.places, self.parts,
            [(2, 4, 2, 2, self.rows, self.half)],
            [
                (0, 0, everything, lambda ref, p: ref.at[0, :, :, p[6]]),
                (1, 0, everything, lambda ref, p: ref.at[0, :, :, p[7]]),
                (2, 0, everything, lambda ref, p: ref.at[1, :, p[4]]),
                (3, 0, everything, lambda ref, p: ref.at[1, :, p[5]]),
            ],
        )
        self.own = joined.reshape(2, 16, self.rows, self.half)
        self.sources = (self.own, other_core(self.own))


class SmallPiece(Piece):
    def join_z(self):
        (self.a,) = move(
            "gather_z" + self.tag, self.places, self.parts, [(4, self.rows, 2 * self.half)],
            [
                (shift, 0, everything, lambda ref, p, shift=shift: ref.at[p[shift]])
                for shift in range(4)
            ],
        )

    def send_layer(self):
        diagonal = lax.ppermute(self.a, "fsdp", [(f, f ^ 3) for f in range(16)])
        self.parts = [self.a, along_x(self.a), along_y(self.a), diagonal]

    def join_layer(self):
        half = self.half
        (joined,) = move(
            "gather_layer" + self.tag, self.places, self.parts,
            [(2, 4, 2, 2, self.rows, half)],
            [
                (
                    part, 0,
                    lambda ref, p, side=side: ref.at[:, :, pl.ds(side * half, half)],
                    lambda ref, p, side=side, y=y, x=x: ref.at[side, :, p[y], p[x]],
                )
                for part, (y, x) in enumerate(((4, 6), (4, 7), (5, 6), (5, 7)))
                for side in range(2)
            ],
        )
        self.own = joined.reshape(2, 16, self.rows, half)
        self.sources = (self.own, other_core(self.own))


def transposed(stacked):
    return stacked.reshape(STACK, -1).T


def halves(rows_by_lanes, pieces):
    rows = rows_by_lanes.shape[0]
    split = rows_by_lanes.reshape(rows, pieces, 2, -1)
    return [split[:, :, side].reshape(rows, -1) for side in range(2)]


class StepGather:
    def __init__(self, qkv_weight, out_weight, fc1_weight, fc2_weight, shards):
        rows, _, column = qkv_weight.shape
        qd, qu, od, ou, f1d, f1u, f2d, f2u = shards
        places = positions()
        t = lax.axis_index("tensor")
        qkv_a, qkv_b = halves(qkv_weight.reshape(rows, 3 * column), 3)
        out_a, out_b = halves(out_weight.T, 1)
        low1 = jnp.concatenate([qd, qu], axis=0)
        low2 = jnp.concatenate([od, ou], axis=0)
        low3 = jnp.concatenate([f1d, f2u], axis=0)
        self.piece1 = Piece(
            jnp.concatenate([qkv_a, low1[:64], qkv_b, low1[64:]], axis=1), places, "1"
        )
        self.piece2 = SmallPiece(jnp.concatenate([out_a, low2, out_b, low3], axis=1), places, "2")
        hidden = jnp.concatenate(
            [fc1_weight, fc2_weight.T, f1u[:64], f1u[64:], f2d[:64], f2d[64:]], axis=1
        )
        self.hidden = hidden
        self.places, self.column = places, column
        self.width = fc1_weight.shape[1]
        self.groups = jnp.stack([2 * t, 2 * t + 1, 2 - 2 * t, 3 - 2 * t]).astype(jnp.int32)
        self.lane = 0

    def first(self, tokens):
        one, two = self.piece1, self.piece2
        one.send_z()
        one.join_z()
        hidden = after(self.hidden, one.a)
        two.shard = after(two.shard, one.a)
        self.hidden = lax.all_gather(hidden, BOTH, axis=0).reshape(16, 2, *hidden.shape)
        one.send_half()
        one.wait_for(tokens)
        one.join_half()
        one.send_rest()
        one.join_rest()
        lanes = pl.ds(3 * self.column // 2, STACK)
        qd, qu = move(
            "stacks1", self.places, one.sources, [(16, 2, 32, STACK), (16, 2, 96, STACK)],
            [
                m
                for source, core in ((0, 8), (1, 9))
                for m in (
                    (source, 0, lambda ref, p: ref.at[0, :, pl.ds(0, 32), lanes],
                     lambda ref, p, core=core: ref.at[:, p[core]]),
                    (source, 1, lambda ref, p: ref.at[0, :, pl.ds(32, 32), lanes],
                     lambda ref, p, core=core: ref.at[:, p[core], pl.ds(0, 32)]),
                    (source, 1, lambda ref, p: ref.at[1, :, :, lanes],
                     lambda ref, p, core=core: ref.at[:, p[core], pl.ds(32, 64)]),
                )
            ],
        )
        return one.sources, qd.reshape(-1, STACK), qu.reshape(-1, STACK)

    def after_qkv(self, q):
        two = self.piece2
        two.shard = after(two.shard, q)
        two.send_z()
        return q

    def between_images(self, o):
        two = self.piece2
        two.wait_for(o)
        two.join_z()
        two.send_layer()
        return after(o, two.a)

    def second(self, o):
        self.piece2.wait_for(o)
        self.piece2.join_layer()
        lanes = pl.ds(self.column // 2, STACK)
        stacks = move(
            "stacks2", self.places, self.piece2.sources, [(16, 2, 32, STACK)] * 4,
            [
                (source, out,
                 lambda ref, p, out=out: ref.at[out // 2, :, pl.ds(out % 2 * 32, 32), lanes],
                 lambda ref, p, core=core: ref.at[:, p[core]])
                for source, core in ((0, 8), (1, 9))
                for out in range(4)
            ],
        )
        od, ou, f1d, f2u = [stack.reshape(-1, STACK) for stack in stacks]
        self.stacks = (f1d, f2u)
        return self.piece2.sources, od, ou

    def third(self):
        f1d, f2u = self.stacks
        base = 2 * self.width // STACK
        sides = [[(self.hidden, base + 2 * out + side) for side in range(2)] for out in range(2)]
        return self.hidden, f1d, sides[0], sides[1], f2u


class WholeGather:
    def __init__(self, qkv_weight, out_weight, fc1_weight, fc2_weight, shards):
        rows, _, column = qkv_weight.shape
        piece = jnp.concatenate(
            [fc1_weight, fc2_weight.T, qkv_weight.reshape(rows, 3 * column), out_weight.T],
            axis=1,
        )
        groups = lax.axis_size("tensor")
        self.joined = lax.all_gather(piece, BOTH, axis=0).reshape(-1, groups, *piece.shape)
        stacked = lax.all_gather(jnp.concatenate(shards, axis=0), BOTH, axis=0)
        self.full = []
        offset = 0
        for shard in shards:
            part = stacked[:, offset : offset + shard.shape[0]]
            self.full.append(part.reshape(-1, STACK))
            offset += shard.shape[0]
        start = 2 * fc1_weight.shape[1]
        by_group = self.joined[..., start:].transpose(1, 0, 2, 3)
        self.qkv, self.out = by_group[..., : 3 * column], by_group[..., 3 * column :]
        self.groups = jnp.arange(groups, dtype=jnp.int32)
        self.lane = 0

    def first(self, tokens):
        return (self.qkv,), self.full[0], self.full[1]

    def after_qkv(self, q):
        return q

    def between_images(self, o):
        return o

    def second(self, o):
        return (self.out,), self.full[2], self.full[3]

    def third(self):
        down1, up1, down2, up2 = self.full[4:]
        view = lambda stack: [(stack.reshape(16, 2, -1, STACK), 0)]
        return self.joined, down1, view(up1), view(down2), up2


def small_call(name, kernel, places, parts, outs):
    vmem = pl.BlockSpec(memory_space=pltpu.VMEM)
    return pl.pallas_call(
        kernel,
        in_specs=[smem()] + [vmem] * len(parts),
        out_specs=[vmem] * len(outs),
        out_shape=[jax.ShapeDtypeStruct(shape, dtype) for shape, dtype in outs],
        compiler_params=pltpu.CompilerParams(vmem_limit_bytes=24 << 20),
        name=name,
    )(places, *parts)


def add(*values):
    total = values[0].astype(f32)
    for value in values[1:]:
        total += value.astype(f32)
    return total


class StepScatter:
    def __init__(self, terms, tag):
        self.places, self.tag = positions(), tag
        self.widths = [term.shape[0] // 32 for term in terms]
        self.total = sum(self.widths)
        moves = []
        offset = 0
        for number, width in enumerate(self.widths):
            for out, core in enumerate((8, 9)):
                moves.append(
                    (number, out,
                     lambda ref, p, core=core: ref.at[:, :, :, p[core]],
                     lambda ref, p, offset=offset, width=width: ref.at[
                         :, :, :, pl.ds(offset, width)])
                )
            offset += width
        split = [
            term.reshape(4, 2, 2, 2, width, STACK) for term, width in zip(terms, self.widths)
        ]
        kept, sent = move(
            "scatter_core" + tag, self.places, split, [(4, 2, 2, self.total, STACK)] * 2, moves,
            room=60 << 20,
        )
        self.parts = [kept, other_core(sent)]
        self.mark = kept

    def wait_for(self, other):
        self.parts[0] = after(self.parts[0], other)

    def layer(self):
        def kernel(p, kept, came, *outs):
            for out, y, x in zip(outs, (4, 4, 5, 5), (6, 7, 6, 7)):
                out[...] = add(kept[:, p[y], p[x]], came[:, p[y], p[x]]).astype(bf16)

        shape = ((4, self.total, STACK), bf16)
        own, to_x, to_y, to_both = small_call(
            "scatter_layer" + self.tag, kernel, self.places, self.parts, [shape] * 4
        )
        diagonal = lax.ppermute(to_both, "fsdp", [(f, f ^ 3) for f in range(16)])
        self.parts = [own, along_x(to_x), along_y(to_y), diagonal]
        self.mark = own

    def layers(self):
        def kernel(p, one, two, three, four, *outs):
            for shift, out in enumerate(outs):
                z = (p[0] + shift) % 4
                out[...] = add(one[z], two[z], three[z], four[z]).astype(out.dtype)

        own, *sends = small_call(
            "scatter_layers" + self.tag, kernel, self.places, self.parts,
            [((self.total, STACK), f32)] + [((self.total, STACK), bf16)] * 3,
        )
        self.parts = [own] + [along_z(send, shift + 1) for shift, send in enumerate(sends)]
        self.mark = own

    def finish(self):
        def kernel(p, own, first, second, third, *outs):
            value = add(own[...], first[...], second[...], third[...])
            offset = 0
            for width, out in zip(self.widths, outs):
                out[...] = value[offset : offset + width].T
                offset += width

        return small_call(
            "scatter_sum" + self.tag, kernel, self.places, self.parts,
            [((STACK, width), f32) for width in self.widths],
        )


class WholeScatter:
    def __init__(self, terms, tag):
        members = lax.axis_size(BOTH)
        packed = jnp.concatenate(
            [term.reshape(members, -1, STACK).astype(f32) for term in terms], axis=1
        )
        self.widths = [term.shape[0] // members for term in terms]
        self.summed = lax.psum_scatter(packed, BOTH, scatter_dimension=0, tiled=False)
        self.mark = terms[0]

    def wait_for(self, other):
        pass

    def layer(self):
        pass

    def layers(self):
        pass

    def finish(self):
        grads = []
        offset = 0
        for width in self.widths:
            grads.append(self.summed[offset : offset + width].T)
            offset += width
        return grads


def on_device(
    tokens,
    cotangent,
    adapter_index,
    filled,
    ln1_gain,
    ln1_shift,
    qkv_weight,
    qv_bias,
    out_weight,
    out_bias,
    ln2_gain,
    ln2_shift,
    fc1_weight,
    fc1_bias,
    fc2_weight,
    fc2_bias,
    qkv_down,
    qkv_up,
    out_down,
    out_up,
    fc1_down,
    fc1_up,
    fc2_down,
    fc2_up,
):
    images = tokens.shape[0]
    own_start = lax.axis_index("tensor") * images
    index = lax.dynamic_slice_in_dim(adapter_index, own_start, images, 0)
    mask = lax.dynamic_slice_in_dim(filled, own_start, images, 0)
    stack_list = (qkv_down, qkv_up, out_down, out_up, fc1_down, fc1_up, fc2_down, fc2_up)
    steps = (lax.axis_size("fsdp"), lax.axis_size("tensor"), images) == STEPS
    shards = [transposed(stacked) for stacked in stack_list]
    gather = (StepGather if steps else WholeGather)(
        qkv_weight, out_weight, fc1_weight, fc2_weight, shards
    )
    scatter = StepScatter if steps else WholeScatter
    groups = gather.groups
    row = lambda vector: vector.astype(f32)[None, :]
    tokens = untangle(tokens)
    qkv_sources, qkv_down_full, qkv_up_full = gather.first(tokens)
    q, k, v, low_one = qkv_project(
        tokens, qkv_sources, groups, qkv_down_full, qkv_up_full, index, qv_bias, row(ln1_gain),
        row(ln1_shift),
    )
    q = gather.after_qkv(q)
    mixed = None
    for image in range(images):
        mixed = attend(q, k, v, image, mixed)
        if image == 0 and images > 1:
            mixed = (gather.between_images(mixed[0]), *mixed[1:])
    o, *kept = mixed
    out_sources, out_down_full, out_up_full = gather.second(o)
    h, low_out = out_project(
        tokens, o, out_sources, gather.lane, groups, out_down_full, out_up_full, index, mask,
        row(out_bias),
    )
    mlp_weights, *stacks = gather.third()
    outputs, dh, grad_up2, grad_down2, grad_up1, grad_down1 = mlp(
        h, cotangent, mlp_weights, *stacks, index, mask,
        row(fc1_bias), row(fc2_bias), row(ln2_gain), row(ln2_shift),
    )
    do, grad_out_up, grad_out_down = out_back(
        dh, o, low_out, out_sources, gather.lane, groups, out_down_full, out_up_full, index, mask
    )
    early = scatter(
        [grad_out_down, grad_out_up, grad_down1, grad_up1, grad_down2, grad_up2], "1"
    )
    do = after(do, early.mark)
    grads = None
    for image in range(images):
        grads = attend_back(q, k, v, do, o, kept, image, grads)
        if image == 0:
            early.wait_for(grads[0])
            early.layer()
            grads = (after(grads[0], early.mark), *grads[1:])
    dq, dk, dv = grads
    early.wait_for(dq)
    early.layers()
    dq = after(dq, early.mark)
    low_grad, grad_qkv_up, grad_qkv_down = qkv_grads(
        tokens, dq, dk, dv, low_one, qkv_up_full, index, row(ln1_gain), row(ln1_shift)
    )
    late = scatter([grad_qkv_down, grad_qkv_up], "2")
    early_grads = early.finish()
    low_grad = after(low_grad, late.mark, early_grads[0])
    rows_grads = []
    for image in range(images):
        rows_grads.append(
            qkv_back(
                tokens, dh, dq, dk, dv, low_grad, qkv_sources, groups, qkv_down_full,
                row(ln1_gain), rows_grads,
            )
        )
        if image == 0:
            late.wait_for(rows_grads[0])
            late.layer()
            rows_grads[0] = after(rows_grads[0], late.mark)
    input_grad = rows_grads[-1].transpose(1, 0, 2)
    late.layers()
    grads = [grad.reshape(ADAPTERS, RANK, -1) for grad in (*late.finish(), *early_grads)]
    return (outputs.transpose(1, 0, 2), input_grad, *grads)


def solution(mesh):
    images = P(BOTH, None, None)
    stacked = P(None, None, BOTH)
    in_specs = (
        images, images, P("fsdp"), P("fsdp"), P(), P(), P("fsdp", None, "tensor"), P(),
        P("tensor", "fsdp"), P(), P(), P(), P("fsdp", "tensor"), P(), P("tensor", "fsdp"), P(),
    ) + (stacked,) * 8
    out_specs = (images, images) + (stacked,) * 8
    return jax.shard_map(
        on_device, mesh=mesh, in_specs=in_specs, out_specs=out_specs, check_vma=False
    )
```

```python
import math
from functools import partial

import jax
import jax.numpy as jnp
from jax import lax
from jax.experimental import pallas as pl
from jax.experimental.pallas import tpu as pltpu
from jax.sharding import PartitionSpec as P

D = 1024
HEADS = 16
HEAD_DIM = 64
FF = 4096
SEQ = 577
RANK = 16
ADAPTERS = 8
STACK = ADAPTERS * RANK
TILE = 1024
STACK_SHAPES = ((16, 2, 32, STACK), (16, 2, 96, STACK))

epsilon = 1e-05
bf16 = jnp.bfloat16
f32 = jnp.float32
NN = (((1,), (0,)), ((), ()))
NT = (((1,), (1,)), ((), ()))
TN = (((0,), (0,)), ((), ()))
BOTH = ("fsdp", "tensor")


def dot(left, right, dims):
    return lax.dot_general(left, right, dims, preferred_element_type=f32)


def params():
    return pltpu.CompilerParams(vmem_limit_bytes=60 << 20)


def cost(flops, moved, exps=0):
    return pl.CostEstimate(flops=flops, bytes_accessed=moved, transcendentals=exps)


def smem():
    return pl.BlockSpec(memory_space=pltpu.SMEM)


def whole(shape):
    return pl.BlockSpec(shape, lambda *_: (0,) * len(shape), pipeline_mode=pl.Buffered(1))


GAIN1, SHIFT1, OUT_BIAS, GAIN2, SHIFT2, BIAS2, BIAS1 = range(7)


def vector(place):
    return pl.BlockSpec((1, D), lambda *_: (0, place), pipeline_mode=pl.Buffered(1))


def image_rows(width=D):
    return pl.BlockSpec((pl.Squeezed(), SEQ, width), lambda i: (i, 0, 0))


def normalize(values):
    center = values - jnp.mean(values, axis=-1, keepdims=True)
    inverse = lax.rsqrt(jnp.mean(center * center, axis=-1, keepdims=True) + epsilon)
    return center * inverse, inverse


def norm_back(upstream, normed, inverse, gain_row):
    scaled = upstream * gain_row
    return inverse * (
        scaled
        - jnp.mean(scaled, axis=-1, keepdims=True)
        - normed * jnp.mean(scaled * normed, axis=-1, keepdims=True)
    )


def chosen_lanes(adapter):
    lanes = lax.broadcasted_iota(jnp.int32, (1, STACK), 1)
    return (lanes // RANK) == adapter


def keep(product, adapter):
    return jnp.where(chosen_lanes(adapter), product, 0.0).astype(bf16)


def add_to(ref, value, first):
    @pl.when(first)
    def _():
        ref[...] = value

    @pl.when(jnp.logical_not(first))
    def _():
        ref[...] += value


def flat(block):
    return block.reshape(D, block.shape[-1])


def any_space():
    return pl.BlockSpec(memory_space=pl.ANY)


def untangle_kernel(mixed_ref, out_ref):
    for image in range(out_ref.shape[0]):
        out_ref[image] = mixed_ref[:, image, :]


def untangle(array):
    images = array.shape[0]
    return pl.pallas_call(
        untangle_kernel,
        grid=(1,),
        in_specs=[whole((SEQ, images, D))],
        out_specs=whole((images, SEQ, D)),
        out_shape=jax.ShapeDtypeStruct((images, SEQ, D), array.dtype),
        compiler_params=pltpu.CompilerParams(vmem_limit_bytes=32 << 20),
        name="untangle",
    )(array.transpose(1, 0, 2))


class Stream:
    def __init__(self, sources, lane, width, slots, sems):
        self.sources, self.lane, self.width = sources, lane, width
        self.slots, self.sems = slots, sems

    def copy(self, source, inner, slot):
        lanes = pl.ds(self.lane, self.width)
        return pltpu.make_async_copy(
            source.at[inner, :, :, lanes], self.slots.at[slot], self.sems.at[slot]
        )

    def start(self, group, slot):
        offset = 0
        for source in self.sources:
            count = source.shape[0]

            @pl.when(jnp.logical_and(group >= offset, group < offset + count))
            def _(source=source, offset=offset):
                self.copy(source, group - offset, slot).start()

            offset += count

    def wait(self, slot):
        self.copy(self.sources[0], 0, slot).wait()


def spread_copies(sources, lane, parts, table_ref, weight_ref, sem):
    members, rows, total = weight_ref.shape
    groups = group_count(sources)
    width = total // parts // groups
    group = 0
    for source in sources:
        for inner in range(source.shape[0]):
            start = pl.multiple_of(table_ref[group] * width, width)
            for part in range(parts):
                yield pltpu.make_async_copy(
                    source.at[inner, :, :, pl.ds(lane + part * width, width)],
                    weight_ref.at[:, :, pl.ds(part * width * groups + start, width)],
                    sem.at[group * parts + part],
                )
            group += 1


def spread_scratch(sources, parts):
    members, rows = sources[0].shape[1:3]
    return [
        pltpu.VMEM((members, rows, parts * D), bf16),
        pltpu.SemaphoreType.DMA((group_count(sources) * parts,)),
    ]


def qkv_kernel(count, moves, *refs):
    table_ref, places_ref, index_ref, tokens_ref = refs[:4]
    sources = refs[4 : 4 + count]
    stacks = refs[4 + count : 6 + count]
    bias_ref, gain_ref, shift_ref = refs[6 + count : 9 + count]
    (
        q_ref, k_ref, v_ref, low_ref, down_ref, up_ref,
        a_s, low_s, up_s, slots, sems, stack_sems,
    ) = refs[9 + count :]
    copies = [
        pltpu.make_async_copy(
            source(stacks[part], places_ref),
            target((down_ref, up_ref)[out], places_ref),
            stack_sems.at[number],
        )
        for number, (part, out, source, target) in enumerate(moves)
    ]
    group = pl.program_id(0)
    image = pl.program_id(1)
    width = q_ref.shape[-1]
    stream = Stream(sources, 0, 3 * width, slots, sems)
    slot = group % 2

    @pl.when(jnp.logical_and(group == 0, image == 0))
    def _():
        for copy in copies:
            copy.start()
        stream.start(group, 0)

    @pl.when(group == 0)
    def _():
        normed, _ = normalize(tokens_ref[...].astype(f32))
        a_s[image] = (normed * gain_ref[...] + shift_ref[...]).astype(bf16)

    @pl.when(jnp.logical_and(group == 0, image == 0))
    def _():
        for copy in copies:
            copy.wait()
        up_s[...] = up_ref[...].reshape(3 * D, STACK)

    @pl.when(group == 0)
    def _():
        down = down_ref[...].reshape(D, STACK)
        low_s[image] = keep(dot(a_s[image], down, NN), index_ref[0, image])

    @pl.when(image == 0)
    def _():
        stream.wait(slot)

        @pl.when(group + 1 < pl.num_programs(0))
        def _():
            stream.start(group + 1, 1 - slot)

    a = a_s[image]
    low = low_s[image]
    low_ref[...] = low
    weight = flat(slots[slot])
    start = pl.multiple_of(table_ref[group] * width, width)
    bias = bias_ref[...].astype(f32)
    for part, out_ref in enumerate((q_ref, k_ref, v_ref)):
        value = dot(a, weight[:, part * width : (part + 1) * width], NN)
        value += dot(low, up_s[pl.ds(part * D + start, width), :], NT)
        if part != 1:
            value += bias[part // 2 : part // 2 + 1]
        out_ref[...] = value.astype(bf16)


def group_count(sources):
    return sum(source.shape[0] for source in sources)


def qkv_project(tokens, sources, table, places, stacks, moves, who, bias, vectors):
    images = tokens.shape[0]
    members, rows = sources[0].shape[1:3]
    groups = group_count(sources)
    width = D // groups
    sq = pl.Squeezed()
    out = pl.BlockSpec((sq, SEQ, width), lambda g, i, t: (i, 0, t[g]))
    grid_spec = pltpu.PrefetchScalarGridSpec(
        num_scalar_prefetch=1,
        grid=(groups, images),
        in_specs=[smem(), smem(), pl.BlockSpec((sq, SEQ, D), lambda g, i, t: (i, 0, 0))]
        + [any_space()] * (len(sources) + 2)
        + [pl.BlockSpec((2, width), lambda g, i, t: (0, t[g])), vector(GAIN1), vector(SHIFT1)],
        out_specs=[out, out, out, pl.BlockSpec((sq, SEQ, STACK), lambda g, i, t: (i, 0, 0))]
        + [pl.BlockSpec(shape, lambda g, i, t: (0, 0, 0, 0)) for shape in STACK_SHAPES],
        scratch_shapes=[
            pltpu.VMEM((images, SEQ, D), bf16),
            pltpu.VMEM((images, SEQ, STACK), bf16),
            pltpu.VMEM((3 * D, STACK), bf16),
            pltpu.VMEM((2, members, rows, 3 * width), bf16),
            pltpu.SemaphoreType.DMA((2,)),
            pltpu.SemaphoreType.DMA((len(moves),)),
        ],
    )
    return pl.pallas_call(
        partial(qkv_kernel, len(sources), moves),
        grid_spec=grid_spec,
        out_shape=[jax.ShapeDtypeStruct((images, SEQ, D), bf16)] * 3
        + [jax.ShapeDtypeStruct((images, SEQ, STACK), bf16)]
        + [jax.ShapeDtypeStruct(shape, bf16) for shape in STACK_SHAPES],
        compiler_params=params(),
        cost_estimate=cost(6 * images * SEQ * D * D, 20 << 20),
        name="qkv_project",
    )(table, places, who, tokens, *sources, *stacks, bias, vectors, vectors)


def attend_kernel(q_ref, k_ref, v_ref, o_ref, w_ref, scale_ref):
    q = q_ref[...]
    k = k_ref[...]
    v = v_ref[...]
    low = lax.broadcasted_iota(jnp.int32, q.shape, 1) < HEAD_DIM
    both = jnp.concatenate([v, jnp.ones_like(v)], axis=1)
    outs = []
    for head in range(2):
        own = low if head == 0 else jnp.logical_not(low)
        queries = jnp.where(own, q * HEAD_DIM**-0.5, jnp.zeros_like(q)).astype(bf16)
        scores = dot(queries, k, NT)
        raised = jnp.exp(scores - jnp.max(scores, axis=-1, keepdims=True)).astype(bf16)
        w_ref[head] = raised
        outs.append(dot(raised, both, NN))
    width = v.shape[-1]
    scale = 1.0 / jnp.where(low, outs[0][:, width:], outs[1][:, width:])
    scale_ref[...] = scale
    o_ref[...] = (jnp.where(low, outs[0][:, :width], outs[1][:, :width]) * scale).astype(bf16)


def pair_rows(image):
    return pl.BlockSpec((pl.Squeezed(), SEQ, 2 * HEAD_DIM), lambda h: (image, 0, h))


def pair_weights(image):
    return pl.BlockSpec((2, SEQ, SEQ), lambda h: (image * (HEADS // 2) + h, 0, 0))


def into(kernel, inputs):
    def body(*refs):
        kernel(*refs[:inputs], *refs[len(refs) - (len(refs) - inputs) // 2 :])

    return body


def per_image(kernel, name, image, inputs, in_specs, outs, out_specs, filled, flops, moved, exps):
    count = len(inputs)
    if filled is None:
        return pl.pallas_call(
            kernel, grid=(HEADS // 2,), in_specs=in_specs, out_specs=out_specs, out_shape=outs,
            compiler_params=params(), cost_estimate=cost(flops, moved, exps), name=name,
        )(*inputs)
    return pl.pallas_call(
        into(kernel, count), grid=(HEADS // 2,), in_specs=in_specs + [any_space()] * len(outs),
        out_specs=out_specs, out_shape=outs,
        input_output_aliases={count + n: n for n in range(len(outs))},
        compiler_params=params(), cost_estimate=cost(flops, moved, exps), name=name,
    )(*inputs, *filled)


def attend(q, k, v, image, filled):
    images = q.shape[0]
    outs = [
        jax.ShapeDtypeStruct((images, SEQ, D), bf16),
        jax.ShapeDtypeStruct((images * HEADS, SEQ, SEQ), bf16),
        jax.ShapeDtypeStruct((images, SEQ, D), f32),
    ]
    return per_image(
        attend_kernel, "attend", image, (q, k, v), [pair_rows(image)] * 3, outs,
        [pair_rows(image), pair_weights(image), pair_rows(image)], filled,
        16 * SEQ * SEQ * D, 20 << 20, HEADS * SEQ * SEQ,
    )


def attend_back_kernel(
    q_ref, k_ref, v_ref, do_ref, o_ref, w_ref, scale_ref, dq_ref, dk_ref, dv_ref
):
    q = q_ref[...]
    k = k_ref[...]
    v = v_ref[...]
    do = (do_ref[...].astype(f32) * scale_ref[...]).astype(bf16)
    products = do.astype(f32) * o_ref[...].astype(f32)
    low = lax.broadcasted_iota(jnp.int32, q.shape, 1) < HEAD_DIM
    grads = []
    for head in range(2):
        own = low if head == 0 else jnp.logical_not(low)
        mixed_grad = jnp.where(own, do, jnp.zeros_like(do))
        inner = jnp.sum(jnp.where(own, products, 0.0), axis=-1, keepdims=True)
        raised = w_ref[head]
        prob_grad = dot(mixed_grad, v, NT)
        score_grad = (raised.astype(f32) * (prob_grad - inner)).astype(bf16)
        grads.append((dot(score_grad, k, NN), dot(score_grad, q, TN), dot(raised, do, TN)))
    scale = HEAD_DIM**-0.5
    dq_ref[...] = (jnp.where(low, grads[0][0], grads[1][0]) * scale).astype(bf16)
    dk_ref[...] = (jnp.where(low, grads[0][1], grads[1][1]) * scale).astype(bf16)
    dv_ref[...] = jnp.where(low, grads[0][2], grads[1][2]).astype(bf16)


def attend_back(q, k, v, do, o, kept, image, filled):
    outs = [jax.ShapeDtypeStruct(q.shape, bf16)] * 3
    return per_image(
        attend_back_kernel, "attend_back", image, (q, k, v, do, o, *kept),
        [pair_rows(image)] * 5 + [pair_weights(image), pair_rows(image)], outs,
        [pair_rows(image)] * 3, filled, 32 * SEQ * SEQ * D, 24 << 20, 0,
    )


def out_kernel(count, lane, *refs):
    table_ref, index_ref, filled_ref, tokens_ref, o_ref = refs[:5]
    sources = refs[5 : 5 + count]
    down_ref, up_ref, bias_ref, h_ref, low_ref, weight_s, sems = refs[5 + count :]
    image = pl.program_id(0)

    @pl.when(image == 0)
    def _():
        for copy in spread_copies(sources, lane, 1, table_ref, weight_s, sems):
            copy.start()

    low = keep(dot(o_ref[...], down_ref[...], NN), index_ref[0, image])
    low_ref[...] = low

    @pl.when(image == 0)
    def _():
        for copy in spread_copies(sources, lane, 1, table_ref, weight_s, sems):
            copy.wait()

    value = dot(o_ref[...], flat(weight_s[...]), NT) + dot(low, up_ref[...], NT) + bias_ref[...]
    h_ref[...] = tokens_ref[...].astype(f32) + filled_ref[1, image].astype(f32) * value


def out_project(tokens, o, sources, lane, table, down, up, who, vectors):
    images = tokens.shape[0]
    return pl.pallas_call(
        partial(out_kernel, len(sources), lane),
        grid=(images,),
        in_specs=[smem(), smem(), smem(), image_rows(), image_rows()]
        + [any_space()] * len(sources)
        + [whole((D, STACK)), whole((D, STACK)), vector(OUT_BIAS)],
        out_specs=[image_rows(), image_rows(STACK)],
        out_shape=[
            jax.ShapeDtypeStruct((images, SEQ, D), f32),
            jax.ShapeDtypeStruct((images, SEQ, STACK), bf16),
        ],
        scratch_shapes=spread_scratch(sources, 1),
        compiler_params=params(),
        cost_estimate=cost(2 * images * SEQ * D * D, 12 << 20),
        name="out_project",
    )(table, who, who, tokens, o, *sources, down, up, vectors)


def out_back_kernel(count, lane, *refs):
    table_ref, index_ref, filled_ref, dh_ref, o_ref, low_ref = refs[:6]
    sources = refs[6 : 6 + count]
    down_ref, up_ref, do_ref, grad_up_ref, grad_down_ref = refs[6 + count : 11 + count]
    grad_up_s, grad_down_s, weight_s, sems = refs[11 + count :]
    image = pl.program_id(0)
    last = image == pl.num_programs(0) - 1

    @pl.when(image == 0)
    def _():
        for copy in spread_copies(sources, lane, 1, table_ref, weight_s, sems):
            copy.start()
        grad_up_s[...] = jnp.zeros_like(grad_up_s)
        grad_down_s[...] = jnp.zeros_like(grad_down_s)

    branch = (dh_ref[...] * filled_ref[1, image].astype(f32)).astype(bf16)
    low_grad = keep(dot(branch, up_ref[...], NN), index_ref[0, image])
    grad_up_s[...] += dot(low_ref[...], branch, TN)
    grad_down_s[...] += dot(low_grad, o_ref[...], TN)

    @pl.when(image == 0)
    def _():
        for copy in spread_copies(sources, lane, 1, table_ref, weight_s, sems):
            copy.wait()

    value = dot(branch, flat(weight_s[...]), NN) + dot(low_grad, down_ref[...], NT)
    do_ref[...] = value.astype(bf16)

    @pl.when(last)
    def _():
        grad_up_ref[...] = grad_up_s[...].T.astype(bf16)
        grad_down_ref[...] = grad_down_s[...].T.astype(bf16)


def out_back(dh, o, low, sources, lane, table, down, up, who):
    images = dh.shape[0]
    grad = pl.BlockSpec((D, STACK), lambda i: (0, 0))
    return pl.pallas_call(
        partial(out_back_kernel, len(sources), lane),
        grid=(images,),
        in_specs=[smem(), smem(), smem(), image_rows(), image_rows(), image_rows(STACK)]
        + [any_space()] * len(sources)
        + [whole((D, STACK)), whole((D, STACK))],
        out_specs=[image_rows(), grad, grad],
        out_shape=[jax.ShapeDtypeStruct((images, SEQ, D), bf16)]
        + [jax.ShapeDtypeStruct((D, STACK), bf16)] * 2,
        scratch_shapes=[pltpu.VMEM((STACK, D), f32)] * 2 + spread_scratch(sources, 1),
        compiler_params=params(),
        cost_estimate=cost(2 * images * SEQ * D * D, 12 << 20),
        name="out_back",
    )(table, who, who, dh, o, low, *sources, down, up)


def mlp_kernel(sides, *refs):
    index_ref, filled_ref, h_ref, cot_ref, first_ref, second_ref, down1_ref = refs[:7]
    up1_refs = refs[7 : 7 + sides]
    down2_refs = refs[7 + sides : 7 + 2 * sides]
    (
        up2_ref, bias1_ref, bias2_ref, gain_ref, shift_ref,
        out_ref, dh_ref, grad_up2_ref, grad_down2_ref, grad_up1_ref, grad_down1_ref,
        a_s, dz_s, low3_s, dlow4_s, z_s, da_s, low4_s, dlow3_s,
        grad_up2_s, grad_down2_s, grad_up1_s, grad_down1_s,
    ) = refs[7 + 2 * sides :]
    width = grad_up1_ref.shape[0]
    tall = lambda parts: jnp.concatenate([part[...] for part in parts], axis=2).reshape(
        width, STACK
    )
    up1 = tall(up1_refs)
    down2 = tall(down2_refs)
    tile = pl.program_id(0)
    image = pl.program_id(1)
    last = tile == pl.num_programs(0) - 1
    final = image == pl.num_programs(1) - 1
    adapter = index_ref[0, image]
    mask = filled_ref[1, image].astype(f32)

    @pl.when(image == 0)
    def _():
        grad_down2_s[...] = jnp.zeros_like(grad_down2_s)
        grad_up1_s[...] = jnp.zeros_like(grad_up1_s)

    @pl.when(tile == 0)
    def _():
        for ref in (z_s, da_s, low4_s, dlow3_s):
            ref[image] = jnp.zeros(ref.shape[1:], f32)
        normed, _ = normalize(h_ref[image])
        a = (normed * gain_ref[...] + shift_ref[...]).astype(bf16)
        a_s[image] = a
        dz = (cot_ref[image].astype(f32) * mask).astype(bf16)
        dz_s[image] = dz
        low3_s[image] = keep(dot(a, down1_ref[...], NN), adapter)
        dlow4_s[image] = keep(dot(dz, up2_ref[...], NN), adapter)

    a = a_s[image]
    dz = dz_s[image]
    low3 = low3_s[image]
    dlow4 = dlow4_s[image]
    first = flat(first_ref[...])
    second = flat(second_ref[...])
    before = dot(a, first, NN) + dot(low3, up1, NT) + bias1_ref[...]
    density = jnp.exp(before * before * -0.5) * 0.3989422804014327
    below = 0.5 * lax.erf(before * 0.7071067811865476) + 0.5
    g = (before * below).astype(bf16)
    slope = below + before * density
    dg = dot(dz, second, NN) + dot(dlow4, down2, NT)
    df = (dg * slope).astype(bf16)
    z_s[image] += dot(g, second, NT)
    da_s[image] += dot(df, first, NT)
    low4_s[image] += dot(g, down2, NN)
    dlow3_s[image] += dot(df, up1, NN)
    grad_down2_s[...] += dot(dlow4, g, TN)
    grad_up1_s[...] += dot(low3, df, TN)

    @pl.when(final)
    def _():
        grad_down2_ref[...] = grad_down2_s[...].T.astype(bf16)
        grad_up1_ref[...] = grad_up1_s[...].T.astype(bf16)

    @pl.when(last)
    def _():
        low4 = keep(low4_s[image], adapter)
        h = h_ref[image]
        z = z_s[image] + dot(low4, up2_ref[...], NT) + bias2_ref[...]
        outputs = (h + mask * z).astype(bf16)
        for number in range(out_ref.shape[1]):

            @pl.when(image == number)
            def _(number=number):
                out_ref[:, number, :] = outputs

        add_to(grad_up2_s, dot(low4, dz, TN), image == 0)
        dlow3 = keep(dlow3_s[image], adapter)
        da = da_s[image] + dot(dlow3, down1_ref[...], NT)
        add_to(grad_down1_s, dot(dlow3, a, TN), image == 0)
        normed, inverse = normalize(h)
        dh_ref[...] = cot_ref[image].astype(f32) + norm_back(
            da, normed, inverse, gain_ref[...]
        )

    @pl.when(jnp.logical_and(last, final))
    def _():
        grad_up2_ref[...] = grad_up2_s[...].T.astype(bf16)
        grad_down1_ref[...] = grad_down1_s[...].T.astype(bf16)


def mlp(h, cot, weights, down1, up1, down2, up2, who, vectors):
    images = h.shape[0]
    members, groups, rows, _ = weights.shape
    hidden = FF // groups
    width = min(TILE, hidden)
    per_group = hidden // width
    tiles = FF // width
    sq = pl.Squeezed()

    def weight(base):
        return pl.BlockSpec(
            (members, sq, rows, width),
            lambda j, i: (0, j // per_group, 0, base * per_group + j % per_group),
        )

    tall = pl.BlockSpec((width, STACK), lambda j, i: (j, 0))
    sides = up1 + down2

    def side_block(array, lane):
        shape = (16 * width // FF, 2, FF // 32 // len(up1), STACK)
        return pl.BlockSpec(shape, lambda j, i: (j, 0, 0, lane))

    short = pl.BlockSpec((D, STACK), lambda j, i: (0, 0))
    late = pl.BlockSpec((sq, SEQ, D), lambda j, i: (jnp.where(j == tiles - 1, i, 0), 0, 0))
    return pl.pallas_call(
        partial(mlp_kernel, len(up1)),
        grid=(tiles, images),
        in_specs=[
            smem(),
            smem(),
            whole((images, SEQ, D)),
            whole((images, SEQ, D)),
            weight(0),
            weight(1),
            whole((D, STACK)),
        ]
        + [side_block(*side) for side in sides]
        + [
            whole((D, STACK)),
            pl.BlockSpec((1, width), lambda j, i: (0, BIAS1 * D // width + j)),
            vector(BIAS2),
            vector(GAIN2),
            vector(SHIFT2),
        ],
        out_specs=[pl.BlockSpec((SEQ, images, D), lambda j, i: (0, 0, 0)), late, short, tall, tall, short],
        out_shape=[
            jax.ShapeDtypeStruct((SEQ, images, D), bf16),
            jax.ShapeDtypeStruct((images, SEQ, D), f32),
            jax.ShapeDtypeStruct((D, STACK), bf16),
            jax.ShapeDtypeStruct((FF, STACK), bf16),
            jax.ShapeDtypeStruct((FF, STACK), bf16),
            jax.ShapeDtypeStruct((D, STACK), bf16),
        ],
        scratch_shapes=[
            pltpu.VMEM((images, SEQ, D), bf16),
            pltpu.VMEM((images, SEQ, D), bf16),
            pltpu.VMEM((images, SEQ, STACK), bf16),
            pltpu.VMEM((images, SEQ, STACK), bf16),
            pltpu.VMEM((images, SEQ, D), f32),
            pltpu.VMEM((images, SEQ, D), f32),
            pltpu.VMEM((images, SEQ, STACK), f32),
            pltpu.VMEM((images, SEQ, STACK), f32),
            pltpu.VMEM((STACK, D), f32),
            pltpu.VMEM((STACK, width), f32),
            pltpu.VMEM((STACK, width), f32),
            pltpu.VMEM((STACK, D), f32),
        ],
        compiler_params=params(),
        cost_estimate=cost(8 * images * SEQ * D * FF, 40 << 20, 2 * images * SEQ * FF),
        name="mlp",
    )(
        who, who, h, cot, weights, weights, down1, *[array for array, _ in sides], up2,
        vectors, vectors, vectors, vectors,
    )


def qkv_grads_kernel(
    index_ref, tokens_ref, dq_ref, dk_ref, dv_ref, low_ref, up_ref, gain_ref, shift_ref,
    low_grad_ref, grad_up_ref, grad_down_ref, grad_up_s, grad_down_s,
):
    image = pl.program_id(0)
    parts = (dq_ref, dk_ref, dv_ref)

    @pl.when(image == 0)
    def _():
        grad_up_s[...] = jnp.zeros_like(grad_up_s)
        grad_down_s[...] = jnp.zeros_like(grad_down_s)

    low = low_ref[...]
    low_grad = dot(parts[0][...], up_ref[0:D, :], NN)
    for part in (1, 2):
        low_grad += dot(parts[part][...], up_ref[part * D : (part + 1) * D, :], NN)
    low_grad = keep(low_grad, index_ref[0, image])
    low_grad_ref[...] = low_grad
    for part in range(3):
        grad_up_s[part] += dot(low, parts[part][...], TN)
    normed, _ = normalize(tokens_ref[...].astype(f32))
    a = (normed * gain_ref[...] + shift_ref[...]).astype(bf16)
    grad_down_s[...] += dot(low_grad, a, TN)

    @pl.when(image == pl.num_programs(0) - 1)
    def _():
        for part in range(3):
            grad_up_ref[part * D : (part + 1) * D, :] = grad_up_s[part].T.astype(bf16)
        grad_down_ref[...] = grad_down_s[...].T.astype(bf16)


def qkv_grads(tokens, dq, dk, dv, low, up, who, vectors):
    images = tokens.shape[0]
    return pl.pallas_call(
        qkv_grads_kernel,
        grid=(images,),
        in_specs=[smem()]
        + [image_rows()] * 4
        + [image_rows(STACK), whole((3 * D, STACK)), vector(GAIN1), vector(SHIFT1)],
        out_specs=[
            image_rows(STACK),
            pl.BlockSpec((3 * D, STACK), lambda i: (0, 0)),
            pl.BlockSpec((D, STACK), lambda i: (0, 0)),
        ],
        out_shape=[
            jax.ShapeDtypeStruct((images, SEQ, STACK), bf16),
            jax.ShapeDtypeStruct((3 * D, STACK), bf16),
            jax.ShapeDtypeStruct((D, STACK), bf16),
        ],
        scratch_shapes=[pltpu.VMEM((3, STACK, D), f32), pltpu.VMEM((STACK, D), f32)],
        compiler_params=params(),
        cost_estimate=cost(2 * images * SEQ * D * D, 12 << 20),
        name="qkv_grads",
    )(who, tokens, dq, dk, dv, low, up, vectors, vectors)


def qkv_back_kernel(count, image, *refs):
    table_ref = refs[0]
    arrays = refs[1:6]
    low_grad_ref = refs[6]
    sources = refs[7 : 7 + count]
    down_ref, gain_ref = refs[7 + count : 9 + count]
    grad_ref, dq_s, dk_s, dv_s, tokens_s, dh_s, earlier_s, row_sems, weight_s, sems = refs[-10:]
    earlier_refs = refs[9 + count : -10]
    weights = list(spread_copies(sources, 0, 3, table_ref, weight_s, sems))
    held = (tokens_s, dh_s, dq_s, dk_s, dv_s)
    rows = [
        pltpu.make_async_copy(array.at[image], into_ref, row_sems.at[number])
        for number, (array, into_ref) in enumerate(zip(arrays, held))
    ]
    before = [
        pltpu.make_async_copy(ref, earlier_s.at[number], row_sems.at[len(rows) + number])
        for number, ref in enumerate(earlier_refs)
    ]
    for part in range(3):
        rows[2 + part].start()
        for copy in weights[part::3]:
            copy.start()
    for copy in (rows[0], rows[1], *before):
        copy.start()
    da = dot(low_grad_ref[...], down_ref[...], NT)
    for part, part_s in enumerate((dq_s, dk_s, dv_s)):
        rows[2 + part].wait()
        for copy in weights[part::3]:
            copy.wait()
        da += dot(part_s[...], flat(weight_s[:, :, part * D : (part + 1) * D]), NT)
    rows[0].wait()
    normed, inverse = normalize(tokens_s[...].astype(f32))
    rows[1].wait()
    grad = dh_s[...] + norm_back(da, normed, inverse, gain_ref[...])
    if len(grad_ref.shape) == 2:
        grad_ref[...] = grad
    else:
        for number, copy in enumerate(before):
            copy.wait()
            grad_ref[:, number, :] = earlier_s[number]
        grad_ref[:, len(before), :] = grad


def qkv_back(tokens, dh, dq, dk, dv, low_grad, sources, table, down, vectors, earlier):
    images = tokens.shape[0]
    image = len(earlier)
    out = (SEQ, D) if image + 1 < images else (SEQ, images, D)
    return pl.pallas_call(
        partial(qkv_back_kernel, len(sources), image),
        grid=(1,),
        in_specs=[smem()]
        + [any_space()] * 5
        + [pl.BlockSpec((pl.Squeezed(), SEQ, STACK), lambda i: (image, 0, 0))]
        + [any_space()] * len(sources)
        + [whole((D, STACK)), vector(GAIN1)]
        + [any_space()] * image,
        out_specs=whole(out),
        out_shape=jax.ShapeDtypeStruct(out, f32),
        scratch_shapes=[pltpu.VMEM((SEQ, D), bf16)] * 4
        + [
            pltpu.VMEM((SEQ, D), f32),
            pltpu.VMEM((max(image, 1), SEQ, D), f32),
            pltpu.SemaphoreType.DMA((5 + max(image, 1),)),
        ]
        + spread_scratch(sources, 3),
        compiler_params=params(),
        cost_estimate=cost(6 * SEQ * D * D, 18 << 20),
        name="qkv_back",
    )(table, tokens, dh, dq, dk, dv, low_grad, *sources, down, vectors, *earlier)


STEPS = (16, 2, 2)


def along_x(array):
    return lax.ppermute(array, "fsdp", [(f, f ^ 1) for f in range(16)])


def along_y(array):
    return lax.ppermute(array, "fsdp", [(f, f ^ 2) for f in range(16)])


def along_z(array, shift):
    pairs = [(f, (f // 4 + shift) % 4 * 4 + f % 4) for f in range(16)]
    return lax.ppermute(array, "fsdp", pairs)


def other_core(array):
    return lax.ppermute(array, "tensor", [(0, 1), (1, 0)])


def positions():
    f = lax.axis_index("fsdp")
    t = lax.axis_index("tensor")
    z, y, x = f // 4, f // 2 % 2, f % 2
    places = [z, (z + 3) % 4, (z + 2) % 4, (z + 1) % 4, y, 1 - y, x, 1 - x, t, 1 - t]
    return jnp.stack(places).astype(jnp.int32)


def move(name, places, parts, outs, moves, room=None):
    room = room or (4 << 20) + sum(2 * math.prod(shape) for shape in outs)

    def kernel(places_ref, *refs):
        sems = refs[-1]
        copies = []
        for number, (part, out, source, target) in enumerate(moves):
            copies.append(
                pltpu.make_async_copy(
                    source(refs[part], places_ref),
                    target(refs[len(parts) + out], places_ref),
                    sems.at[number],
                )
            )
            copies[-1].start()
        for copy in copies:
            copy.wait()

    return pl.pallas_call(
        kernel,
        in_specs=[smem()] + [any_space()] * len(parts),
        out_specs=[pl.BlockSpec(memory_space=pltpu.VMEM)] * len(outs),
        out_shape=[jax.ShapeDtypeStruct(shape, bf16) for shape in outs],
        scratch_shapes=[pltpu.SemaphoreType.DMA((len(moves),))],
        compiler_params=pltpu.CompilerParams(vmem_limit_bytes=room),
        name=name,
    )(places, *parts)


def everything(ref, places):
    return ref


def after(value, *others):
    return lax.optimization_barrier((value, *others))[0]


class Piece:
    def __init__(self, shard, places, tag):
        self.shard, self.places, self.tag = shard, places, tag
        self.rows, self.half = shard.shape[0], shard.shape[1] // 2

    def send_z(self):
        self.parts = [self.shard] + [along_z(self.shard, shift) for shift in (1, 2, 3)]

    def wait_for(self, other):
        self.parts[0] = after(self.parts[0], other)

    def join_z(self):
        half = self.half
        self.a, self.b = move(
            "gather_z" + self.tag, self.places, self.parts, [(4, self.rows, half)] * 2,
            [
                (
                    shift, side,
                    lambda ref, p, side=side: ref.at[:, pl.ds(side * half, half)],
                    lambda ref, p, shift=shift: ref.at[p[shift]],
                )
                for shift in range(4)
                for side in range(2)
            ],
            room=60 << 20,
        )

    def send_half(self):
        self.parts = [self.a, along_y(self.a), self.b, along_x(self.b)]

    def join_half(self):
        self.a, self.b = move(
            "gather_yx" + self.tag, self.places, self.parts, [(4, 2, self.rows, self.half)] * 2,
            [
                (0, 0, everything, lambda ref, p: ref.at[:, p[4]]),
                (1, 0, everything, lambda ref, p: ref.at[:, p[5]]),
                (2, 1, everything, lambda ref, p: ref.at[:, p[6]]),
                (3, 1, everything, lambda ref, p: ref.at[:, p[7]]),
            ],
        )

    def send_rest(self):
        self.parts = [self.a, along_x(self.a), self.b, along_y(self.b)]

    def join_rest(self):
        (joined,) = move(
            "gather_xy" + self.tag, self.places, self.parts,
            [(2, 4, 2, 2, self.rows, self.half)],
            [
                (0, 0, everything, lambda ref, p: ref.at[0, :, :, p[6]]),
                (1, 0, everything, lambda ref, p: ref.at[0, :, :, p[7]]),
                (2, 0, everything, lambda ref, p: ref.at[1, :, p[4]]),
                (3, 0, everything, lambda ref, p: ref.at[1, :, p[5]]),
            ],
        )
        self.own = joined.reshape(2, 16, self.rows, self.half)
        self.sources = (self.own, other_core(self.own))


class SmallPiece(Piece):
    def join_z(self):
        (self.a,) = move(
            "gather_z" + self.tag, self.places, self.parts, [(4, self.rows, 2 * self.half)],
            [
                (shift, 0, everything, lambda ref, p, shift=shift: ref.at[p[shift]])
                for shift in range(4)
            ],
        )

    def send_layer(self):
        diagonal = lax.ppermute(self.a, "fsdp", [(f, f ^ 3) for f in range(16)])
        self.parts = [self.a, along_x(self.a), along_y(self.a), diagonal]

    def join_layer(self):
        half = self.half
        (joined,) = move(
            "gather_layer" + self.tag, self.places, self.parts,
            [(2, 4, 2, 2, self.rows, half)],
            [
                (
                    part, 0,
                    lambda ref, p, side=side: ref.at[:, :, pl.ds(side * half, half)],
                    lambda ref, p, side=side, y=y, x=x: ref.at[side, :, p[y], p[x]],
                )
                for part, (y, x) in enumerate(((4, 6), (4, 7), (5, 6), (5, 7)))
                for side in range(2)
            ],
        )
        self.own = joined.reshape(2, 16, self.rows, half)
        self.sources = (self.own, other_core(self.own))


def transposed(stacked):
    return stacked.reshape(STACK, -1).T


def halves(rows_by_lanes, pieces):
    rows = rows_by_lanes.shape[0]
    split = rows_by_lanes.reshape(rows, pieces, 2, -1)
    return [split[:, :, side].reshape(rows, -1) for side in range(2)]


class StepGather:
    def __init__(self, qkv_weight, out_weight, fc1_weight, fc2_weight, shards):
        rows, _, column = qkv_weight.shape
        qd, qu, od, ou, f1d, f1u, f2d, f2u = shards
        places = positions()
        t = lax.axis_index("tensor")
        qkv_a, qkv_b = halves(qkv_weight.reshape(rows, 3 * column), 3)
        out_a, out_b = halves(out_weight.T, 1)
        low1 = jnp.concatenate([qd, qu], axis=0)
        low2 = jnp.concatenate([od, ou], axis=0)
        low3 = jnp.concatenate([f1d, f2u], axis=0)
        self.piece1 = Piece(
            jnp.concatenate([qkv_a, low1[:64], qkv_b, low1[64:]], axis=1), places, "1"
        )
        self.piece2 = SmallPiece(jnp.concatenate([out_a, low2, out_b, low3], axis=1), places, "2")
        hidden = jnp.concatenate(
            [fc1_weight, fc2_weight.T, f1u[:64], f1u[64:], f2d[:64], f2d[64:]], axis=1
        )
        self.hidden = hidden
        self.places, self.column = places, column
        self.width = fc1_weight.shape[1]
        self.groups = jnp.stack([2 * t, 2 * t + 1, 2 - 2 * t, 3 - 2 * t]).astype(jnp.int32)
        self.lane = 0

    def first(self, tokens, *others):
        one, two = self.piece1, self.piece2
        one.send_z()
        one.join_z()
        hidden = after(self.hidden, one.a)
        two.shard = after(two.shard, one.a)
        self.hidden = lax.all_gather(hidden, BOTH, axis=0).reshape(16, 2, *hidden.shape)
        one.send_half()
        one.wait_for(tokens)
        one.join_half()
        one.send_rest()
        one.parts[0] = after(one.parts[0], *others)
        one.join_rest()
        lanes = pl.ds(3 * self.column // 2, STACK)
        moves = [
            m
            for source, core in ((0, 8), (1, 9))
            for m in (
                (source, 0, lambda ref, p: ref.at[0, :, pl.ds(0, 32), lanes],
                 lambda ref, p, core=core: ref.at[:, p[core]]),
                (source, 1, lambda ref, p: ref.at[0, :, pl.ds(32, 32), lanes],
                 lambda ref, p, core=core: ref.at[:, p[core], pl.ds(0, 32)]),
                (source, 1, lambda ref, p: ref.at[1, :, :, lanes],
                 lambda ref, p, core=core: ref.at[:, p[core], pl.ds(32, 64)]),
            )
        ]
        return one.sources, self.places, one.sources, moves

    def after_qkv(self, q):
        two = self.piece2
        two.shard = after(two.shard, q)
        two.send_z()
        return q

    def between_images(self, o):
        two = self.piece2
        two.wait_for(o)
        two.join_z()
        two.send_layer()
        return after(o, two.a)

    def second(self, o):
        self.piece2.wait_for(o)
        self.piece2.join_layer()
        lanes = pl.ds(self.column // 2, STACK)
        stacks = move(
            "stacks2", self.places, self.piece2.sources, [(16, 2, 32, STACK)] * 4,
            [
                (source, out,
                 lambda ref, p, out=out: ref.at[out // 2, :, pl.ds(out % 2 * 32, 32), lanes],
                 lambda ref, p, core=core: ref.at[:, p[core]])
                for source, core in ((0, 8), (1, 9))
                for out in range(4)
            ],
            room=60 << 20,
        )
        od, ou, f1d, f2u = [stack.reshape(-1, STACK) for stack in stacks]
        self.stacks = (f1d, f2u)
        return self.piece2.sources, od, ou

    def third(self):
        f1d, f2u = self.stacks
        base = 2 * self.width // STACK
        sides = [[(self.hidden, base + 2 * out + side) for side in range(2)] for out in range(2)]
        return self.hidden, f1d, sides[0], sides[1], f2u


class WholeGather:
    def __init__(self, qkv_weight, out_weight, fc1_weight, fc2_weight, shards):
        rows, _, column = qkv_weight.shape
        piece = jnp.concatenate(
            [fc1_weight, fc2_weight.T, qkv_weight.reshape(rows, 3 * column), out_weight.T],
            axis=1,
        )
        groups = lax.axis_size("tensor")
        self.joined = lax.all_gather(piece, BOTH, axis=0).reshape(-1, groups, *piece.shape)
        stacked = lax.all_gather(jnp.concatenate(shards, axis=0), BOTH, axis=0)
        self.full = []
        offset = 0
        for shard in shards:
            part = stacked[:, offset : offset + shard.shape[0]]
            self.full.append(part.reshape(-1, STACK))
            offset += shard.shape[0]
        start = 2 * fc1_weight.shape[1]
        by_group = self.joined[..., start:].transpose(1, 0, 2, 3)
        self.qkv, self.out = by_group[..., : 3 * column], by_group[..., 3 * column :]
        self.groups = jnp.arange(groups, dtype=jnp.int32)
        self.lane = 0

    def first(self, tokens, *others):
        stacks = [part.reshape(shape) for part, shape in zip(self.full[:2], STACK_SHAPES)]
        moves = [(part, part, everything, everything) for part in range(2)]
        return (self.qkv,), jnp.zeros((1,), jnp.int32), stacks, moves

    def after_qkv(self, q):
        return q

    def between_images(self, o):
        return o

    def second(self, o):
        return (self.out,), self.full[2], self.full[3]

    def third(self):
        down1, up1, down2, up2 = self.full[4:]
        view = lambda stack: [(stack.reshape(16, 2, -1, STACK), 0)]
        return self.joined, down1, view(up1), view(down2), up2


def small_call(name, kernel, places, parts, outs):
    vmem = pl.BlockSpec(memory_space=pltpu.VMEM)
    return pl.pallas_call(
        kernel,
        in_specs=[smem()] + [vmem] * len(parts),
        out_specs=[vmem] * len(outs),
        out_shape=[jax.ShapeDtypeStruct(shape, dtype) for shape, dtype in outs],
        compiler_params=pltpu.CompilerParams(vmem_limit_bytes=24 << 20),
        name=name,
    )(places, *parts)


def add(*values):
    total = values[0].astype(f32)
    for value in values[1:]:
        total += value.astype(f32)
    return total


class StepScatter:
    def __init__(self, terms, tag):
        self.places, self.tag = positions(), tag
        self.widths = [term.shape[0] // 32 for term in terms]
        self.total = sum(self.widths)
        moves = []
        offset = 0
        for number, width in enumerate(self.widths):
            for out, core in enumerate((8, 9)):
                moves.append(
                    (number, out,
                     lambda ref, p, core=core: ref.at[:, :, :, p[core]],
                     lambda ref, p, offset=offset, width=width: ref.at[
                         :, :, :, pl.ds(offset, width)])
                )
            offset += width
        split = [
            term.reshape(4, 2, 2, 2, width, STACK) for term, width in zip(terms, self.widths)
        ]
        kept, sent = move(
            "scatter_core" + tag, self.places, split, [(4, 2, 2, self.total, STACK)] * 2, moves,
            room=60 << 20,
        )
        self.parts = [kept, other_core(sent)]
        self.mark = kept

    def wait_for(self, other):
        self.parts[0] = after(self.parts[0], other)

    def layer(self):
        def kernel(p, kept, came, *outs):
            for out, y, x in zip(outs, (4, 4, 5, 5), (6, 7, 6, 7)):
                out[...] = add(kept[:, p[y], p[x]], came[:, p[y], p[x]]).astype(bf16)

        shape = ((4, self.total, STACK), bf16)
        own, to_x, to_y, to_both = small_call(
            "scatter_layer" + self.tag, kernel, self.places, self.parts, [shape] * 4
        )
        diagonal = lax.ppermute(to_both, "fsdp", [(f, f ^ 3) for f in range(16)])
        self.parts = [own, along_x(to_x), along_y(to_y), diagonal]
        self.mark = own

    def layers(self):
        def kernel(p, one, two, three, four, *outs):
            for shift, out in enumerate(outs):
                z = (p[0] + shift) % 4
                out[...] = add(one[z], two[z], three[z], four[z]).astype(out.dtype)

        own, *sends = small_call(
            "scatter_layers" + self.tag, kernel, self.places, self.parts,
            [((self.total, STACK), f32)] + [((self.total, STACK), bf16)] * 3,
        )
        self.parts = [own] + [along_z(send, shift + 1) for shift, send in enumerate(sends)]
        self.mark = own

    def finish(self):
        def kernel(p, own, first, second, third, *outs):
            value = add(own[...], first[...], second[...], third[...])
            offset = 0
            for width, out in zip(self.widths, outs):
                out[...] = value[offset : offset + width].T
                offset += width

        return small_call(
            "scatter_sum" + self.tag, kernel, self.places, self.parts,
            [((STACK, width), f32) for width in self.widths],
        )


class WholeScatter:
    def __init__(self, terms, tag):
        members = lax.axis_size(BOTH)
        packed = jnp.concatenate(
            [term.reshape(members, -1, STACK).astype(f32) for term in terms], axis=1
        )
        self.widths = [term.shape[0] // members for term in terms]
        self.summed = lax.psum_scatter(packed, BOTH, scatter_dimension=0, tiled=False)
        self.mark = terms[0]

    def wait_for(self, other):
        pass

    def layer(self):
        pass

    def layers(self):
        pass

    def finish(self):
        grads = []
        offset = 0
        for width in self.widths:
            grads.append(self.summed[offset : offset + width].T)
            offset += width
        return grads


def on_device(
    tokens,
    cotangent,
    adapter_index,
    filled,
    ln1_gain,
    ln1_shift,
    qkv_weight,
    qv_bias,
    out_weight,
    out_bias,
    ln2_gain,
    ln2_shift,
    fc1_weight,
    fc1_bias,
    fc2_weight,
    fc2_bias,
    qkv_down,
    qkv_up,
    out_down,
    out_up,
    fc1_down,
    fc1_up,
    fc2_down,
    fc2_up,
):
    images = tokens.shape[0]
    own_start = lax.axis_index("tensor") * images
    who = lax.dynamic_slice_in_dim(
        jnp.stack([adapter_index, filled]), own_start, images, 1
    )
    vectors = jnp.concatenate(
        [ln1_gain, ln1_shift, out_bias, ln2_gain, ln2_shift, fc2_bias, fc1_bias]
    ).astype(f32)[None, :]
    stack_list = (qkv_down, qkv_up, out_down, out_up, fc1_down, fc1_up, fc2_down, fc2_up)
    steps = (lax.axis_size("fsdp"), lax.axis_size("tensor"), images) == STEPS
    shards = [transposed(stacked) for stacked in stack_list]
    gather = (StepGather if steps else WholeGather)(
        qkv_weight, out_weight, fc1_weight, fc2_weight, shards
    )
    scatter = StepScatter if steps else WholeScatter
    groups = gather.groups
    tokens = untangle(tokens)
    cotangent = untangle(cotangent)
    qkv_sources, places, stacks, moves = gather.first(tokens, cotangent, vectors, who)
    q, k, v, low_one, qkv_down_full, qkv_up_full = qkv_project(
        tokens, qkv_sources, groups, places, stacks, moves, who, qv_bias, vectors
    )
    qkv_down_full = qkv_down_full.reshape(D, STACK)
    qkv_up_full = qkv_up_full.reshape(3 * D, STACK)
    q = gather.after_qkv(q)
    mixed = None
    for image in range(images):
        mixed = attend(q, k, v, image, mixed)
        if image == 0 and images > 1:
            mixed = (gather.between_images(mixed[0]), *mixed[1:])
    o, *kept = mixed
    out_sources, out_down_full, out_up_full = gather.second(o)
    h, low_out = out_project(
        tokens, o, out_sources, gather.lane, groups, out_down_full, out_up_full, who, vectors
    )
    mlp_weights, *stacks = gather.third()
    outputs, dh, grad_up2, grad_down2, grad_up1, grad_down1 = mlp(
        h, cotangent, mlp_weights, *stacks, who, vectors
    )
    do, grad_out_up, grad_out_down = out_back(
        dh, o, low_out, out_sources, gather.lane, groups, out_down_full, out_up_full, who
    )
    early = scatter(
        [grad_out_down, grad_out_up, grad_down1, grad_up1, grad_down2, grad_up2], "1"
    )
    do = after(do, early.mark)
    grads = None
    for image in range(images):
        grads = attend_back(q, k, v, do, o, kept, image, grads)
        if image == 0:
            early.wait_for(grads[0])
            early.layer()
            grads = (after(grads[0], early.mark), *grads[1:])
    dq, dk, dv = grads
    early.wait_for(dq)
    early.layers()
    dq = after(dq, early.mark)
    low_grad, grad_qkv_up, grad_qkv_down = qkv_grads(
        tokens, dq, dk, dv, low_one, qkv_up_full, who, vectors
    )
    late = scatter([grad_qkv_down, grad_qkv_up], "2")
    early_grads = early.finish()
    low_grad = after(low_grad, late.mark, early_grads[0])
    rows_grads = []
    for image in range(images):
        rows_grads.append(
            qkv_back(
                tokens, dh, dq, dk, dv, low_grad, qkv_sources, groups, qkv_down_full,
                vectors, rows_grads,
            )
        )
        if image == 0:
            late.wait_for(rows_grads[0])
            late.layer()
            rows_grads[0] = after(rows_grads[0], late.mark)
    input_grad = rows_grads[-1].transpose(1, 0, 2)
    late.layers()
    grads = [grad.reshape(ADAPTERS, RANK, -1) for grad in (*late.finish(), *early_grads)]
    return (outputs.transpose(1, 0, 2), input_grad, *grads)


def solution(mesh):
    images = P(BOTH, None, None)
    stacked = P(None, None, BOTH)
    in_specs = (
        images, images, P("fsdp"), P("fsdp"), P(), P(), P("fsdp", None, "tensor"), P(),
        P("tensor", "fsdp"), P(), P(), P(), P("fsdp", "tensor"), P(), P("tensor", "fsdp"), P(),
    ) + (stacked,) * 8
    out_specs = (images, images) + (stacked,) * 8
    return jax.shard_map(
        on_device, mesh=mesh, in_specs=in_specs, out_specs=out_specs, check_vma=False
    )
```

```python
import math
from functools import partial

import jax
import jax.numpy as jnp
from jax import lax
from jax.experimental import pallas as pl
from jax.experimental.pallas import tpu as pltpu
from jax.sharding import PartitionSpec as P

D = 1024
HEADS = 16
HEAD_DIM = 64
FF = 4096
SEQ = 577
RANK = 16
ADAPTERS = 8
STACK = ADAPTERS * RANK
TILE = 1024
STACK_SHAPES = ((16, 2, 32, STACK), (16, 2, 96, STACK))

epsilon = 1e-05
bf16 = jnp.bfloat16
f32 = jnp.float32
NN = (((1,), (0,)), ((), ()))
NT = (((1,), (1,)), ((), ()))
TN = (((0,), (0,)), ((), ()))
BOTH = ("fsdp", "tensor")


def dot(left, right, dims):
    return lax.dot_general(left, right, dims, preferred_element_type=f32)


def params():
    return pltpu.CompilerParams(vmem_limit_bytes=60 << 20)


def cost(flops, moved, exps=0):
    return pl.CostEstimate(flops=flops, bytes_accessed=moved, transcendentals=exps)


def smem():
    return pl.BlockSpec(memory_space=pltpu.SMEM)


def whole(shape):
    return pl.BlockSpec(shape, lambda *_: (0,) * len(shape), pipeline_mode=pl.Buffered(1))


GAIN1, SHIFT1, OUT_BIAS, GAIN2, SHIFT2, BIAS2, BIAS1 = range(7)


def vector(place):
    return pl.BlockSpec((1, D), lambda *_: (0, place), pipeline_mode=pl.Buffered(1))


def image_rows(width=D):
    return pl.BlockSpec((pl.Squeezed(), SEQ, width), lambda i: (i, 0, 0))


def normalize(values):
    center = values - jnp.mean(values, axis=-1, keepdims=True)
    inverse = lax.rsqrt(jnp.mean(center * center, axis=-1, keepdims=True) + epsilon)
    return center * inverse, inverse


def norm_back(upstream, normed, inverse, gain_row):
    scaled = upstream * gain_row
    return inverse * (
        scaled
        - jnp.mean(scaled, axis=-1, keepdims=True)
        - normed * jnp.mean(scaled * normed, axis=-1, keepdims=True)
    )


def chosen_lanes(adapter):
    lanes = lax.broadcasted_iota(jnp.int32, (1, STACK), 1)
    return (lanes // RANK) == adapter


def keep(product, adapter):
    return jnp.where(chosen_lanes(adapter), product, 0.0).astype(bf16)


def add_to(ref, value, first):
    @pl.when(first)
    def _():
        ref[...] = value

    @pl.when(jnp.logical_not(first))
    def _():
        ref[...] += value


def flat(block):
    return block.reshape(D, block.shape[-1])


def any_space():
    return pl.BlockSpec(memory_space=pl.ANY)


def untangle_kernel(mixed_ref, out_ref):
    for image in range(out_ref.shape[0]):
        out_ref[image] = mixed_ref[:, image, :]


def untangle(array):
    images = array.shape[0]
    return pl.pallas_call(
        untangle_kernel,
        grid=(1,),
        in_specs=[whole((SEQ, images, D))],
        out_specs=whole((images, SEQ, D)),
        out_shape=jax.ShapeDtypeStruct((images, SEQ, D), array.dtype),
        compiler_params=pltpu.CompilerParams(vmem_limit_bytes=32 << 20),
        name="untangle",
    )(array.transpose(1, 0, 2))


class Stream:
    def __init__(self, sources, lane, width, slots, sems):
        self.sources, self.lane, self.width = sources, lane, width
        self.slots, self.sems = slots, sems

    def copy(self, source, inner, slot):
        lanes = pl.ds(self.lane, self.width)
        return pltpu.make_async_copy(
            source.at[inner, :, :, lanes], self.slots.at[slot], self.sems.at[slot]
        )

    def start(self, group, slot):
        offset = 0
        for source in self.sources:
            count = source.shape[0]

            @pl.when(jnp.logical_and(group >= offset, group < offset + count))
            def _(source=source, offset=offset):
                self.copy(source, group - offset, slot).start()

            offset += count

    def wait(self, slot):
        self.copy(self.sources[0], 0, slot).wait()


def spread_copies(sources, lane, parts, table_ref, weight_ref, sem):
    members, rows, total = weight_ref.shape
    groups = group_count(sources)
    width = total // parts // groups
    group = 0
    for source in sources:
        for inner in range(source.shape[0]):
            start = pl.multiple_of(table_ref[group] * width, width)
            for part in range(parts):
                yield pltpu.make_async_copy(
                    source.at[inner, :, :, pl.ds(lane + part * width, width)],
                    weight_ref.at[:, :, pl.ds(part * width * groups + start, width)],
                    sem.at[group * parts + part],
                )
            group += 1


def spread_scratch(sources, parts):
    members, rows = sources[0].shape[1:3]
    return [
        pltpu.VMEM((members, rows, parts * D), bf16),
        pltpu.SemaphoreType.DMA((group_count(sources) * parts,)),
    ]


def qkv_kernel(count, moves, *refs):
    table_ref, places_ref, index_ref, tokens_ref = refs[:4]
    sources = refs[4 : 4 + count]
    stacks = refs[4 + count : 6 + count]
    bias_ref, gain_ref, shift_ref = refs[6 + count : 9 + count]
    (
        q_ref, k_ref, v_ref, low_ref, down_ref, up_ref,
        a_s, low_s, up_s, slots, sems, stack_sems,
    ) = refs[9 + count :]
    copies = [
        pltpu.make_async_copy(
            source(stacks[part], places_ref),
            target((down_ref, up_ref)[out], places_ref),
            stack_sems.at[number],
        )
        for number, (part, out, source, target) in enumerate(moves)
    ]
    group = pl.program_id(0)
    image = pl.program_id(1)
    width = q_ref.shape[-1]
    stream = Stream(sources, 0, 3 * width, slots, sems)
    slot = group % 2

    @pl.when(jnp.logical_and(group == 0, image == 0))
    def _():
        for copy in copies:
            copy.start()
        stream.start(group, 0)

    @pl.when(group == 0)
    def _():
        normed, _ = normalize(tokens_ref[...].astype(f32))
        a_s[image] = (normed * gain_ref[...] + shift_ref[...]).astype(bf16)

    @pl.when(jnp.logical_and(group == 0, image == 0))
    def _():
        for copy in copies:
            copy.wait()
        up_s[...] = up_ref[...].reshape(3 * D, STACK)

    @pl.when(group == 0)
    def _():
        down = down_ref[...].reshape(D, STACK)
        low_s[image] = keep(dot(a_s[image], down, NN), index_ref[0, image])

    @pl.when(image == 0)
    def _():
        stream.wait(slot)

        @pl.when(group + 1 < pl.num_programs(0))
        def _():
            stream.start(group + 1, 1 - slot)

    a = a_s[image]
    low = low_s[image]
    low_ref[...] = low
    weight = flat(slots[slot])
    start = pl.multiple_of(table_ref[group] * width, width)
    bias = bias_ref[...].astype(f32)
    for part, out_ref in enumerate((q_ref, k_ref, v_ref)):
        value = dot(a, weight[:, part * width : (part + 1) * width], NN)
        value += dot(low, up_s[pl.ds(part * D + start, width), :], NT)
        if part != 1:
            value += bias[part // 2 : part // 2 + 1]
        out_ref[...] = value.astype(bf16)


def group_count(sources):
    return sum(source.shape[0] for source in sources)


def qkv_project(tokens, sources, table, places, stacks, moves, who, bias, vectors):
    images = tokens.shape[0]
    members, rows = sources[0].shape[1:3]
    groups = group_count(sources)
    width = D // groups
    sq = pl.Squeezed()
    out = pl.BlockSpec((sq, SEQ, width), lambda g, i, t: (i, 0, t[g]))
    grid_spec = pltpu.PrefetchScalarGridSpec(
        num_scalar_prefetch=1,
        grid=(groups, images),
        in_specs=[smem(), smem(), pl.BlockSpec((sq, SEQ, D), lambda g, i, t: (i, 0, 0))]
        + [any_space()] * (len(sources) + 2)
        + [pl.BlockSpec((2, width), lambda g, i, t: (0, t[g])), vector(GAIN1), vector(SHIFT1)],
        out_specs=[out, out, out, pl.BlockSpec((sq, SEQ, STACK), lambda g, i, t: (i, 0, 0))]
        + [pl.BlockSpec(shape, lambda g, i, t: (0, 0, 0, 0)) for shape in STACK_SHAPES],
        scratch_shapes=[
            pltpu.VMEM((images, SEQ, D), bf16),
            pltpu.VMEM((images, SEQ, STACK), bf16),
            pltpu.VMEM((3 * D, STACK), bf16),
            pltpu.VMEM((2, members, rows, 3 * width), bf16),
            pltpu.SemaphoreType.DMA((2,)),
            pltpu.SemaphoreType.DMA((len(moves),)),
        ],
    )
    return pl.pallas_call(
        partial(qkv_kernel, len(sources), moves),
        grid_spec=grid_spec,
        out_shape=[jax.ShapeDtypeStruct((images, SEQ, D), bf16)] * 3
        + [jax.ShapeDtypeStruct((images, SEQ, STACK), bf16)]
        + [jax.ShapeDtypeStruct(shape, bf16) for shape in STACK_SHAPES],
        compiler_params=params(),
        cost_estimate=cost(6 * images * SEQ * D * D, 20 << 20),
        name="qkv_project",
    )(table, places, who, tokens, *sources, *stacks, bias, vectors, vectors)


def attend_kernel(q_ref, k_ref, v_ref, o_ref, w_ref, scale_ref):
    q = q_ref[...]
    k = k_ref[...]
    v = v_ref[...]
    low = lax.broadcasted_iota(jnp.int32, q.shape, 1) < HEAD_DIM
    both = jnp.concatenate([v, jnp.ones_like(v)], axis=1)
    outs = []
    for head in range(2):
        own = low if head == 0 else jnp.logical_not(low)
        queries = jnp.where(own, q * HEAD_DIM**-0.5, jnp.zeros_like(q)).astype(bf16)
        scores = dot(queries, k, NT)
        raised = jnp.exp(scores - jnp.max(scores, axis=-1, keepdims=True)).astype(bf16)
        w_ref[head] = raised
        outs.append(dot(raised, both, NN))
    width = v.shape[-1]
    scale = 1.0 / jnp.where(low, outs[0][:, width:], outs[1][:, width:])
    scale_ref[...] = scale
    o_ref[...] = (jnp.where(low, outs[0][:, :width], outs[1][:, :width]) * scale).astype(bf16)


def pair_rows(image):
    return pl.BlockSpec((pl.Squeezed(), SEQ, 2 * HEAD_DIM), lambda h: (image, 0, h))


def pair_weights(image):
    return pl.BlockSpec((2, SEQ, SEQ), lambda h: (image * (HEADS // 2) + h, 0, 0))


def into(kernel, inputs):
    def body(*refs):
        kernel(*refs[:inputs], *refs[len(refs) - (len(refs) - inputs) // 2 :])

    return body


def per_image(kernel, name, image, inputs, in_specs, outs, out_specs, filled, flops, moved, exps):
    count = len(inputs)
    if filled is None:
        return pl.pallas_call(
            kernel, grid=(HEADS // 2,), in_specs=in_specs, out_specs=out_specs, out_shape=outs,
            compiler_params=params(), cost_estimate=cost(flops, moved, exps), name=name,
        )(*inputs)
    return pl.pallas_call(
        into(kernel, count), grid=(HEADS // 2,), in_specs=in_specs + [any_space()] * len(outs),
        out_specs=out_specs, out_shape=outs,
        input_output_aliases={count + n: n for n in range(len(outs))},
        compiler_params=params(), cost_estimate=cost(flops, moved, exps), name=name,
    )(*inputs, *filled)


def attend(q, k, v, image, filled):
    images = q.shape[0]
    outs = [
        jax.ShapeDtypeStruct((images, SEQ, D), bf16),
        jax.ShapeDtypeStruct((images * HEADS, SEQ, SEQ), bf16),
        jax.ShapeDtypeStruct((images, SEQ, D), f32),
    ]
    return per_image(
        attend_kernel, "attend", image, (q, k, v), [pair_rows(image)] * 3, outs,
        [pair_rows(image), pair_weights(image), pair_rows(image)], filled,
        16 * SEQ * SEQ * D, 20 << 20, HEADS * SEQ * SEQ,
    )


def attend_back_kernel(
    q_ref, k_ref, v_ref, do_ref, o_ref, w_ref, scale_ref, dq_ref, dk_ref, dv_ref
):
    q = q_ref[...]
    k = k_ref[...]
    v = v_ref[...]
    do = (do_ref[...].astype(f32) * scale_ref[...]).astype(bf16)
    products = do.astype(f32) * o_ref[...].astype(f32)
    low = lax.broadcasted_iota(jnp.int32, q.shape, 1) < HEAD_DIM
    grads = []
    for head in range(2):
        own = low if head == 0 else jnp.logical_not(low)
        mixed_grad = jnp.where(own, do, jnp.zeros_like(do))
        inner = jnp.sum(jnp.where(own, products, 0.0), axis=-1, keepdims=True)
        raised = w_ref[head]
        prob_grad = dot(mixed_grad, v, NT)
        score_grad = (raised.astype(f32) * (prob_grad - inner)).astype(bf16)
        grads.append((dot(score_grad, k, NN), dot(score_grad, q, TN), dot(raised, do, TN)))
    scale = HEAD_DIM**-0.5
    dq_ref[...] = (jnp.where(low, grads[0][0], grads[1][0]) * scale).astype(bf16)
    dk_ref[...] = (jnp.where(low, grads[0][1], grads[1][1]) * scale).astype(bf16)
    dv_ref[...] = jnp.where(low, grads[0][2], grads[1][2]).astype(bf16)


def attend_back(q, k, v, do, o, kept, image, filled):
    outs = [jax.ShapeDtypeStruct(q.shape, bf16)] * 3
    return per_image(
        attend_back_kernel, "attend_back", image, (q, k, v, do, o, *kept),
        [pair_rows(image)] * 5 + [pair_weights(image), pair_rows(image)], outs,
        [pair_rows(image)] * 3, filled, 32 * SEQ * SEQ * D, 24 << 20, 0,
    )


def out_kernel(count, lane, *refs):
    table_ref, index_ref, filled_ref, tokens_ref, o_ref = refs[:5]
    sources = refs[5 : 5 + count]
    down_ref, up_ref, bias_ref, h_ref, low_ref, weight_s, sems = refs[5 + count :]
    image = pl.program_id(0)

    @pl.when(image == 0)
    def _():
        for copy in spread_copies(sources, lane, 1, table_ref, weight_s, sems):
            copy.start()

    low = keep(dot(o_ref[...], down_ref[...], NN), index_ref[0, image])
    low_ref[...] = low

    @pl.when(image == 0)
    def _():
        for copy in spread_copies(sources, lane, 1, table_ref, weight_s, sems):
            copy.wait()

    value = dot(o_ref[...], flat(weight_s[...]), NT) + dot(low, up_ref[...], NT) + bias_ref[...]
    h_ref[...] = tokens_ref[...].astype(f32) + filled_ref[1, image].astype(f32) * value


def out_project(tokens, o, sources, lane, table, down, up, who, vectors):
    images = tokens.shape[0]
    return pl.pallas_call(
        partial(out_kernel, len(sources), lane),
        grid=(images,),
        in_specs=[smem(), smem(), smem(), image_rows(), image_rows()]
        + [any_space()] * len(sources)
        + [whole((D, STACK)), whole((D, STACK)), vector(OUT_BIAS)],
        out_specs=[image_rows(), image_rows(STACK)],
        out_shape=[
            jax.ShapeDtypeStruct((images, SEQ, D), f32),
            jax.ShapeDtypeStruct((images, SEQ, STACK), bf16),
        ],
        scratch_shapes=spread_scratch(sources, 1),
        compiler_params=params(),
        cost_estimate=cost(2 * images * SEQ * D * D, 12 << 20),
        name="out_project",
    )(table, who, who, tokens, o, *sources, down, up, vectors)


def out_back_kernel(count, lane, *refs):
    table_ref, index_ref, filled_ref, dh_ref, o_ref, low_ref = refs[:6]
    sources = refs[6 : 6 + count]
    down_ref, up_ref, do_ref, grad_up_ref, grad_down_ref = refs[6 + count : 11 + count]
    grad_up_s, grad_down_s, weight_s, sems = refs[11 + count :]
    image = pl.program_id(0)
    last = image == pl.num_programs(0) - 1

    @pl.when(image == 0)
    def _():
        for copy in spread_copies(sources, lane, 1, table_ref, weight_s, sems):
            copy.start()
        grad_up_s[...] = jnp.zeros_like(grad_up_s)
        grad_down_s[...] = jnp.zeros_like(grad_down_s)

    branch = (dh_ref[...] * filled_ref[1, image].astype(f32)).astype(bf16)
    low_grad = keep(dot(branch, up_ref[...], NN), index_ref[0, image])
    grad_up_s[...] += dot(low_ref[...], branch, TN)
    grad_down_s[...] += dot(low_grad, o_ref[...], TN)

    @pl.when(image == 0)
    def _():
        for copy in spread_copies(sources, lane, 1, table_ref, weight_s, sems):
            copy.wait()

    value = dot(branch, flat(weight_s[...]), NN) + dot(low_grad, down_ref[...], NT)
    do_ref[...] = value.astype(bf16)

    @pl.when(last)
    def _():
        grad_up_ref[...] = grad_up_s[...].T.astype(bf16)
        grad_down_ref[...] = grad_down_s[...].T.astype(bf16)


def out_back(dh, o, low, sources, lane, table, down, up, who):
    images = dh.shape[0]
    grad = pl.BlockSpec((D, STACK), lambda i: (0, 0))
    return pl.pallas_call(
        partial(out_back_kernel, len(sources), lane),
        grid=(images,),
        in_specs=[smem(), smem(), smem(), image_rows(), image_rows(), image_rows(STACK)]
        + [any_space()] * len(sources)
        + [whole((D, STACK)), whole((D, STACK))],
        out_specs=[image_rows(), grad, grad],
        out_shape=[jax.ShapeDtypeStruct((images, SEQ, D), bf16)]
        + [jax.ShapeDtypeStruct((D, STACK), bf16)] * 2,
        scratch_shapes=[pltpu.VMEM((STACK, D), f32)] * 2 + spread_scratch(sources, 1),
        compiler_params=params(),
        cost_estimate=cost(2 * images * SEQ * D * D, 12 << 20),
        name="out_back",
    )(table, who, who, dh, o, low, *sources, down, up)


def mlp_kernel(sides, *refs):
    index_ref, filled_ref, h_ref, cot_ref, first_ref, second_ref, down1_ref = refs[:7]
    up1_refs = refs[7 : 7 + sides]
    down2_refs = refs[7 + sides : 7 + 2 * sides]
    (
        up2_ref, bias1_ref, bias2_ref, gain_ref, shift_ref,
        out_ref, dh_ref, grad_up2_ref, grad_down2_ref, grad_up1_ref, grad_down1_ref,
        a_s, dz_s, low3_s, dlow4_s, z_s, da_s, low4_s, dlow3_s,
        grad_up2_s, grad_down2_s, grad_up1_s, grad_down1_s,
    ) = refs[7 + 2 * sides :]
    width = grad_up1_ref.shape[0]
    tall = lambda parts: jnp.concatenate([part[...] for part in parts], axis=2).reshape(
        width, STACK
    )
    up1 = tall(up1_refs)
    down2 = tall(down2_refs)
    tile = pl.program_id(0)
    image = pl.program_id(1)
    last = tile == pl.num_programs(0) - 1
    final = image == pl.num_programs(1) - 1
    adapter = index_ref[0, image]
    mask = filled_ref[1, image].astype(f32)

    @pl.when(image == 0)
    def _():
        grad_down2_s[...] = jnp.zeros_like(grad_down2_s)
        grad_up1_s[...] = jnp.zeros_like(grad_up1_s)

    @pl.when(tile == 0)
    def _():
        for ref in (z_s, da_s, low4_s, dlow3_s):
            ref[image] = jnp.zeros(ref.shape[1:], f32)
        normed, _ = normalize(h_ref[image])
        a = (normed * gain_ref[...] + shift_ref[...]).astype(bf16)
        a_s[image] = a
        dz = (cot_ref[image].astype(f32) * mask).astype(bf16)
        dz_s[image] = dz
        low3_s[image] = keep(dot(a, down1_ref[...], NN), adapter)
        dlow4_s[image] = keep(dot(dz, up2_ref[...], NN), adapter)

    a = a_s[image]
    dz = dz_s[image]
    low3 = low3_s[image]
    dlow4 = dlow4_s[image]
    first = flat(first_ref[...])
    second = flat(second_ref[...])
    before = dot(a, first, NN) + dot(low3, up1, NT) + bias1_ref[...]
    density = jnp.exp(before * before * -0.5) * 0.3989422804014327
    below = 0.5 * lax.erf(before * 0.7071067811865476) + 0.5
    g = (before * below).astype(bf16)
    slope = below + before * density
    dg = dot(dz, second, NN) + dot(dlow4, down2, NT)
    df = (dg * slope).astype(bf16)
    z_s[image] += dot(g, second, NT)
    da_s[image] += dot(df, first, NT)
    low4_s[image] += dot(g, down2, NN)
    dlow3_s[image] += dot(df, up1, NN)
    grad_down2_s[...] += dot(dlow4, g, TN)
    grad_up1_s[...] += dot(low3, df, TN)

    @pl.when(final)
    def _():
        grad_down2_ref[...] = grad_down2_s[...].T.astype(bf16)
        grad_up1_ref[...] = grad_up1_s[...].T.astype(bf16)

    @pl.when(last)
    def _():
        low4 = keep(low4_s[image], adapter)
        h = h_ref[image]
        z = z_s[image] + dot(low4, up2_ref[...], NT) + bias2_ref[...]
        outputs = (h + mask * z).astype(bf16)
        for number in range(out_ref.shape[1]):

            @pl.when(image == number)
            def _(number=number):
                out_ref[:, number, :] = outputs

        add_to(grad_up2_s, dot(low4, dz, TN), image == 0)
        dlow3 = keep(dlow3_s[image], adapter)
        da = da_s[image] + dot(dlow3, down1_ref[...], NT)
        add_to(grad_down1_s, dot(dlow3, a, TN), image == 0)
        normed, inverse = normalize(h)
        dh_ref[...] = cot_ref[image].astype(f32) + norm_back(
            da, normed, inverse, gain_ref[...]
        )

    @pl.when(jnp.logical_and(last, final))
    def _():
        grad_up2_ref[...] = grad_up2_s[...].T.astype(bf16)
        grad_down1_ref[...] = grad_down1_s[...].T.astype(bf16)


def mlp(h, cot, weights, down1, up1, down2, up2, who, vectors):
    images = h.shape[0]
    members, groups, rows, _ = weights.shape
    hidden = FF // groups
    width = min(TILE, hidden)
    per_group = hidden // width
    tiles = FF // width
    sq = pl.Squeezed()

    def weight(base):
        return pl.BlockSpec(
            (members, sq, rows, width),
            lambda j, i: (0, j // per_group, 0, base * per_group + j % per_group),
        )

    tall = pl.BlockSpec((width, STACK), lambda j, i: (j, 0))
    sides = up1 + down2

    def side_block(array, lane):
        shape = (16 * width // FF, 2, FF // 32 // len(up1), STACK)
        return pl.BlockSpec(shape, lambda j, i: (j, 0, 0, lane))

    short = pl.BlockSpec((D, STACK), lambda j, i: (0, 0))
    late = pl.BlockSpec((sq, SEQ, D), lambda j, i: (jnp.where(j == tiles - 1, i, 0), 0, 0))
    return pl.pallas_call(
        partial(mlp_kernel, len(up1)),
        grid=(tiles, images),
        in_specs=[
            smem(),
            smem(),
            whole((images, SEQ, D)),
            whole((images, SEQ, D)),
            weight(0),
            weight(1),
            whole((D, STACK)),
        ]
        + [side_block(*side) for side in sides]
        + [
            whole((D, STACK)),
            pl.BlockSpec((1, width), lambda j, i: (0, BIAS1 * D // width + j)),
            vector(BIAS2),
            vector(GAIN2),
            vector(SHIFT2),
        ],
        out_specs=[pl.BlockSpec((SEQ, images, D), lambda j, i: (0, 0, 0)), late, short, tall, tall, short],
        out_shape=[
            jax.ShapeDtypeStruct((SEQ, images, D), bf16),
            jax.ShapeDtypeStruct((images, SEQ, D), f32),
            jax.ShapeDtypeStruct((D, STACK), bf16),
            jax.ShapeDtypeStruct((FF, STACK), bf16),
            jax.ShapeDtypeStruct((FF, STACK), bf16),
            jax.ShapeDtypeStruct((D, STACK), bf16),
        ],
        scratch_shapes=[
            pltpu.VMEM((images, SEQ, D), bf16),
            pltpu.VMEM((images, SEQ, D), bf16),
            pltpu.VMEM((images, SEQ, STACK), bf16),
            pltpu.VMEM((images, SEQ, STACK), bf16),
            pltpu.VMEM((images, SEQ, D), f32),
            pltpu.VMEM((images, SEQ, D), f32),
            pltpu.VMEM((images, SEQ, STACK), f32),
            pltpu.VMEM((images, SEQ, STACK), f32),
            pltpu.VMEM((STACK, D), f32),
            pltpu.VMEM((STACK, width), f32),
            pltpu.VMEM((STACK, width), f32),
            pltpu.VMEM((STACK, D), f32),
        ],
        compiler_params=params(),
        cost_estimate=cost(8 * images * SEQ * D * FF, 40 << 20, 2 * images * SEQ * FF),
        name="mlp",
    )(
        who, who, h, cot, weights, weights, down1, *[array for array, _ in sides], up2,
        vectors, vectors, vectors, vectors,
    )


def qkv_grads_kernel(
    index_ref, tokens_ref, dq_ref, dk_ref, dv_ref, low_ref, up_ref, gain_ref, shift_ref,
    low_grad_ref, grad_up_ref, grad_down_ref, grad_up_s, grad_down_s,
):
    image = pl.program_id(0)
    parts = (dq_ref, dk_ref, dv_ref)

    @pl.when(image == 0)
    def _():
        grad_up_s[...] = jnp.zeros_like(grad_up_s)
        grad_down_s[...] = jnp.zeros_like(grad_down_s)

    low = low_ref[...]
    low_grad = dot(parts[0][...], up_ref[0:D, :], NN)
    for part in (1, 2):
        low_grad += dot(parts[part][...], up_ref[part * D : (part + 1) * D, :], NN)
    low_grad = keep(low_grad, index_ref[0, image])
    low_grad_ref[...] = low_grad
    for part in range(3):
        grad_up_s[part] += dot(low, parts[part][...], TN)
    normed, _ = normalize(tokens_ref[...].astype(f32))
    a = (normed * gain_ref[...] + shift_ref[...]).astype(bf16)
    grad_down_s[...] += dot(low_grad, a, TN)

    @pl.when(image == pl.num_programs(0) - 1)
    def _():
        for part in range(3):
            grad_up_ref[part * D : (part + 1) * D, :] = grad_up_s[part].T.astype(bf16)
        grad_down_ref[...] = grad_down_s[...].T.astype(bf16)


def qkv_grads(tokens, dq, dk, dv, low, up, who, vectors):
    images = tokens.shape[0]
    return pl.pallas_call(
        qkv_grads_kernel,
        grid=(images,),
        in_specs=[smem()]
        + [image_rows()] * 4
        + [image_rows(STACK), whole((3 * D, STACK)), vector(GAIN1), vector(SHIFT1)],
        out_specs=[
            image_rows(STACK),
            pl.BlockSpec((3 * D, STACK), lambda i: (0, 0)),
            pl.BlockSpec((D, STACK), lambda i: (0, 0)),
        ],
        out_shape=[
            jax.ShapeDtypeStruct((images, SEQ, STACK), bf16),
            jax.ShapeDtypeStruct((3 * D, STACK), bf16),
            jax.ShapeDtypeStruct((D, STACK), bf16),
        ],
        scratch_shapes=[pltpu.VMEM((3, STACK, D), f32), pltpu.VMEM((STACK, D), f32)],
        compiler_params=params(),
        cost_estimate=cost(2 * images * SEQ * D * D, 12 << 20),
        name="qkv_grads",
    )(who, tokens, dq, dk, dv, low, up, vectors, vectors)


def qkv_back_kernel(count, image, *refs):
    table_ref = refs[0]
    arrays = refs[1:6]
    low_grad_ref = refs[6]
    sources = refs[7 : 7 + count]
    down_ref, gain_ref = refs[7 + count : 9 + count]
    grad_ref, dq_s, dk_s, dv_s, tokens_s, dh_s, earlier_s, row_sems, weight_s, sems = refs[-10:]
    earlier_refs = refs[9 + count : -10]
    weights = list(spread_copies(sources, 0, 3, table_ref, weight_s, sems))
    held = (tokens_s, dh_s, dq_s, dk_s, dv_s)
    rows = [
        pltpu.make_async_copy(array.at[image], into_ref, row_sems.at[number])
        for number, (array, into_ref) in enumerate(zip(arrays, held))
    ]
    before = [
        pltpu.make_async_copy(ref, earlier_s.at[number], row_sems.at[len(rows) + number])
        for number, ref in enumerate(earlier_refs)
    ]
    for part in range(3):
        rows[2 + part].start()
        for copy in weights[part::3]:
            copy.start()
    for copy in (rows[0], rows[1], *before):
        copy.start()
    da = dot(low_grad_ref[...], down_ref[...], NT)
    for part, part_s in enumerate((dq_s, dk_s, dv_s)):
        rows[2 + part].wait()
        for copy in weights[part::3]:
            copy.wait()
        da += dot(part_s[...], flat(weight_s[:, :, part * D : (part + 1) * D]), NT)
    rows[0].wait()
    normed, inverse = normalize(tokens_s[...].astype(f32))
    rows[1].wait()
    grad = dh_s[...] + norm_back(da, normed, inverse, gain_ref[...])
    if len(grad_ref.shape) == 2:
        grad_ref[...] = grad
    else:
        for number, copy in enumerate(before):
            copy.wait()
            grad_ref[:, number, :] = earlier_s[number]
        grad_ref[:, len(before), :] = grad


def qkv_back(tokens, dh, dq, dk, dv, low_grad, sources, table, down, vectors, earlier):
    images = tokens.shape[0]
    image = len(earlier)
    out = (SEQ, D) if image + 1 < images else (SEQ, images, D)
    return pl.pallas_call(
        partial(qkv_back_kernel, len(sources), image),
        grid=(1,),
        in_specs=[smem()]
        + [any_space()] * 5
        + [pl.BlockSpec((pl.Squeezed(), SEQ, STACK), lambda i: (image, 0, 0))]
        + [any_space()] * len(sources)
        + [whole((D, STACK)), vector(GAIN1)]
        + [any_space()] * image,
        out_specs=whole(out),
        out_shape=jax.ShapeDtypeStruct(out, f32),
        scratch_shapes=[pltpu.VMEM((SEQ, D), bf16)] * 4
        + [
            pltpu.VMEM((SEQ, D), f32),
            pltpu.VMEM((max(image, 1), SEQ, D), f32),
            pltpu.SemaphoreType.DMA((5 + max(image, 1),)),
        ]
        + spread_scratch(sources, 3),
        compiler_params=params(),
        cost_estimate=cost(6 * SEQ * D * D, 18 << 20),
        name="qkv_back",
    )(table, tokens, dh, dq, dk, dv, low_grad, *sources, down, vectors, *earlier)


STEPS = (16, 2, 2)


def along_x(array):
    return lax.ppermute(array, "fsdp", [(f, f ^ 1) for f in range(16)])


def along_y(array):
    return lax.ppermute(array, "fsdp", [(f, f ^ 2) for f in range(16)])


def along_z(array, shift):
    pairs = [(f, (f // 4 + shift) % 4 * 4 + f % 4) for f in range(16)]
    return lax.ppermute(array, "fsdp", pairs)


def other_core(array):
    return lax.ppermute(array, "tensor", [(0, 1), (1, 0)])


def positions():
    f = lax.axis_index("fsdp")
    t = lax.axis_index("tensor")
    z, y, x = f // 4, f // 2 % 2, f % 2
    places = [z, (z + 3) % 4, (z + 2) % 4, (z + 1) % 4, y, 1 - y, x, 1 - x, t, 1 - t]
    return jnp.stack(places).astype(jnp.int32)


def move(name, places, parts, outs, moves, room=None):
    room = room or (4 << 20) + sum(2 * math.prod(shape) for shape in outs)

    def kernel(places_ref, *refs):
        sems = refs[-1]
        copies = []
        for number, (part, out, source, target) in enumerate(moves):
            copies.append(
                pltpu.make_async_copy(
                    source(refs[part], places_ref),
                    target(refs[len(parts) + out], places_ref),
                    sems.at[number],
                )
            )
            copies[-1].start()
        for copy in copies:
            copy.wait()

    return pl.pallas_call(
        kernel,
        in_specs=[smem()] + [any_space()] * len(parts),
        out_specs=[pl.BlockSpec(memory_space=pltpu.VMEM)] * len(outs),
        out_shape=[jax.ShapeDtypeStruct(shape, bf16) for shape in outs],
        scratch_shapes=[pltpu.SemaphoreType.DMA((len(moves),))],
        compiler_params=pltpu.CompilerParams(vmem_limit_bytes=room),
        name=name,
    )(places, *parts)


def everything(ref, places):
    return ref


def after(value, *others):
    return lax.optimization_barrier((value, *others))[0]


class Piece:
    def __init__(self, shard, places, tag):
        self.shard, self.places, self.tag = shard, places, tag
        self.rows, self.half = shard.shape[0], shard.shape[1] // 2

    def send_z(self):
        self.parts = [self.shard] + [along_z(self.shard, shift) for shift in (1, 2, 3)]

    def wait_for(self, other):
        self.parts[0] = after(self.parts[0], other)

    def join_z(self):
        half = self.half
        self.a, self.b = move(
            "gather_z" + self.tag, self.places, self.parts, [(4, self.rows, half)] * 2,
            [
                (
                    shift, side,
                    lambda ref, p, side=side: ref.at[:, pl.ds(side * half, half)],
                    lambda ref, p, shift=shift: ref.at[p[shift]],
                )
                for shift in range(4)
                for side in range(2)
            ],
            room=60 << 20,
        )

    def send_half(self):
        self.parts = [self.a, along_y(self.a), self.b, along_x(self.b)]

    def join_half(self):
        self.a, self.b = move(
            "gather_yx" + self.tag, self.places, self.parts, [(4, 2, self.rows, self.half)] * 2,
            [
                (0, 0, everything, lambda ref, p: ref.at[:, p[4]]),
                (1, 0, everything, lambda ref, p: ref.at[:, p[5]]),
                (2, 1, everything, lambda ref, p: ref.at[:, p[6]]),
                (3, 1, everything, lambda ref, p: ref.at[:, p[7]]),
            ],
        )

    def send_rest(self):
        self.parts = [self.a, along_x(self.a), self.b, along_y(self.b)]

    def join_rest(self):
        (joined,) = move(
            "gather_xy" + self.tag, self.places, self.parts,
            [(2, 4, 2, 2, self.rows, self.half)],
            [
                (0, 0, everything, lambda ref, p: ref.at[0, :, :, p[6]]),
                (1, 0, everything, lambda ref, p: ref.at[0, :, :, p[7]]),
                (2, 0, everything, lambda ref, p: ref.at[1, :, p[4]]),
                (3, 0, everything, lambda ref, p: ref.at[1, :, p[5]]),
            ],
        )
        self.own = joined.reshape(2, 16, self.rows, self.half)
        self.sources = (self.own, other_core(self.own))


class SmallPiece(Piece):
    def join_z(self):
        (self.a,) = move(
            "gather_z" + self.tag, self.places, self.parts, [(4, self.rows, 2 * self.half)],
            [
                (shift, 0, everything, lambda ref, p, shift=shift: ref.at[p[shift]])
                for shift in range(4)
            ],
        )

    def send_layer(self):
        diagonal = lax.ppermute(self.a, "fsdp", [(f, f ^ 3) for f in range(16)])
        self.parts = [self.a, along_x(self.a), along_y(self.a), diagonal]

    def join_layer(self):
        half = self.half
        (joined,) = move(
            "gather_layer" + self.tag, self.places, self.parts,
            [(2, 4, 2, 2, self.rows, half)],
            [
                (
                    part, 0,
                    lambda ref, p, side=side: ref.at[:, :, pl.ds(side * half, half)],
                    lambda ref, p, side=side, y=y, x=x: ref.at[side, :, p[y], p[x]],
                )
                for part, (y, x) in enumerate(((4, 6), (4, 7), (5, 6), (5, 7)))
                for side in range(2)
            ],
        )
        self.own = joined.reshape(2, 16, self.rows, half)
        self.sources = (self.own, other_core(self.own))


def transposed(stacked):
    return stacked.reshape(STACK, -1).T


def halves(rows_by_lanes, pieces):
    rows = rows_by_lanes.shape[0]
    split = rows_by_lanes.reshape(rows, pieces, 2, -1)
    return [split[:, :, side].reshape(rows, -1) for side in range(2)]


class StepGather:
    def __init__(self, qkv_weight, out_weight, fc1_weight, fc2_weight, shards):
        rows, _, column = qkv_weight.shape
        qd, qu, od, ou, f1d, f1u, f2d, f2u = shards
        places = positions()
        t = lax.axis_index("tensor")
        qkv_a, qkv_b = halves(qkv_weight.reshape(rows, 3 * column), 3)
        out_a, out_b = halves(out_weight.T, 1)
        low1 = jnp.concatenate([qd, qu], axis=0)
        low2 = jnp.concatenate([od, ou], axis=0)
        low3 = jnp.concatenate([f1d, f2u], axis=0)
        self.piece1 = Piece(
            jnp.concatenate([qkv_a, low1[:64], qkv_b, low1[64:]], axis=1), places, "1"
        )
        self.piece2 = SmallPiece(jnp.concatenate([out_a, low2, out_b, low3], axis=1), places, "2")
        hidden = jnp.concatenate(
            [fc1_weight, fc2_weight.T, f1u[:64], f1u[64:], f2d[:64], f2d[64:]], axis=1
        )
        self.hidden = hidden
        self.places, self.column = places, column
        self.width = fc1_weight.shape[1]
        self.groups = jnp.stack([2 * t, 2 * t + 1, 2 - 2 * t, 3 - 2 * t]).astype(jnp.int32)
        self.lane = 0

    def first(self, tokens, *others):
        one, two = self.piece1, self.piece2
        one.send_z()
        one.join_z()
        hidden = after(self.hidden, one.a)
        two.shard = after(two.shard, one.a)
        self.hidden = lax.all_gather(hidden, BOTH, axis=0).reshape(16, 2, *hidden.shape)
        one.send_half()
        one.wait_for(tokens)
        one.join_half()
        one.send_rest()
        two.send_z()
        two.join_z()
        one.parts[0] = after(one.parts[0], two.a, *others)
        one.join_rest()
        lanes = pl.ds(3 * self.column // 2, STACK)
        moves = [
            m
            for source, core in ((0, 8), (1, 9))
            for m in (
                (source, 0, lambda ref, p: ref.at[0, :, pl.ds(0, 32), lanes],
                 lambda ref, p, core=core: ref.at[:, p[core]]),
                (source, 1, lambda ref, p: ref.at[0, :, pl.ds(32, 32), lanes],
                 lambda ref, p, core=core: ref.at[:, p[core], pl.ds(0, 32)]),
                (source, 1, lambda ref, p: ref.at[1, :, :, lanes],
                 lambda ref, p, core=core: ref.at[:, p[core], pl.ds(32, 64)]),
            )
        ]
        return one.sources, self.places, one.sources, moves

    def after_qkv(self, q):
        two = self.piece2
        two.a = after(two.a, q)
        two.send_layer()
        return q

    def between_images(self, o):
        return o

    def second(self, o):
        self.piece2.wait_for(o)
        self.piece2.join_layer()
        lanes = pl.ds(self.column // 2, STACK)
        stacks = move(
            "stacks2", self.places, self.piece2.sources, [(16, 2, 32, STACK)] * 4,
            [
                (source, out,
                 lambda ref, p, out=out: ref.at[out // 2, :, pl.ds(out % 2 * 32, 32), lanes],
                 lambda ref, p, core=core: ref.at[:, p[core]])
                for source, core in ((0, 8), (1, 9))
                for out in range(4)
            ],
            room=60 << 20,
        )
        od, ou, f1d, f2u = [stack.reshape(-1, STACK) for stack in stacks]
        self.stacks = (f1d, f2u)
        return self.piece2.sources, od, ou

    def third(self):
        f1d, f2u = self.stacks
        base = 2 * self.width // STACK
        sides = [[(self.hidden, base + 2 * out + side) for side in range(2)] for out in range(2)]
        return self.hidden, f1d, sides[0], sides[1], f2u


class WholeGather:
    def __init__(self, qkv_weight, out_weight, fc1_weight, fc2_weight, shards):
        rows, _, column = qkv_weight.shape
        piece = jnp.concatenate(
            [fc1_weight, fc2_weight.T, qkv_weight.reshape(rows, 3 * column), out_weight.T],
            axis=1,
        )
        groups = lax.axis_size("tensor")
        self.joined = lax.all_gather(piece, BOTH, axis=0).reshape(-1, groups, *piece.shape)
        stacked = lax.all_gather(jnp.concatenate(shards, axis=0), BOTH, axis=0)
        self.full = []
        offset = 0
        for shard in shards:
            part = stacked[:, offset : offset + shard.shape[0]]
            self.full.append(part.reshape(-1, STACK))
            offset += shard.shape[0]
        start = 2 * fc1_weight.shape[1]
        by_group = self.joined[..., start:].transpose(1, 0, 2, 3)
        self.qkv, self.out = by_group[..., : 3 * column], by_group[..., 3 * column :]
        self.groups = jnp.arange(groups, dtype=jnp.int32)
        self.lane = 0

    def first(self, tokens, *others):
        stacks = [part.reshape(shape) for part, shape in zip(self.full[:2], STACK_SHAPES)]
        moves = [(part, part, everything, everything) for part in range(2)]
        return (self.qkv,), jnp.zeros((1,), jnp.int32), stacks, moves

    def after_qkv(self, q):
        return q

    def between_images(self, o):
        return o

    def second(self, o):
        return (self.out,), self.full[2], self.full[3]

    def third(self):
        down1, up1, down2, up2 = self.full[4:]
        view = lambda stack: [(stack.reshape(16, 2, -1, STACK), 0)]
        return self.joined, down1, view(up1), view(down2), up2


def small_call(name, kernel, places, parts, outs):
    vmem = pl.BlockSpec(memory_space=pltpu.VMEM)
    return pl.pallas_call(
        kernel,
        in_specs=[smem()] + [vmem] * len(parts),
        out_specs=[vmem] * len(outs),
        out_shape=[jax.ShapeDtypeStruct(shape, dtype) for shape, dtype in outs],
        compiler_params=pltpu.CompilerParams(vmem_limit_bytes=24 << 20),
        name=name,
    )(places, *parts)


def add(*values):
    total = values[0].astype(f32)
    for value in values[1:]:
        total += value.astype(f32)
    return total


class StepScatter:
    def __init__(self, terms, tag):
        self.places, self.tag = positions(), tag
        self.widths = [term.shape[0] // 32 for term in terms]
        self.total = sum(self.widths)
        moves = []
        offset = 0
        for number, width in enumerate(self.widths):
            for out, core in enumerate((8, 9)):
                moves.append(
                    (number, out,
                     lambda ref, p, core=core: ref.at[:, :, :, p[core]],
                     lambda ref, p, offset=offset, width=width: ref.at[
                         :, :, :, pl.ds(offset, width)])
                )
            offset += width
        split = [
            term.reshape(4, 2, 2, 2, width, STACK) for term, width in zip(terms, self.widths)
        ]
        kept, sent = move(
            "scatter_core" + tag, self.places, split, [(4, 2, 2, self.total, STACK)] * 2, moves,
            room=60 << 20,
        )
        self.parts = [kept, other_core(sent)]
        self.mark = kept

    def wait_for(self, other):
        self.parts[0] = after(self.parts[0], other)

    def layer(self):
        def kernel(p, kept, came, *outs):
            for out, y, x in zip(outs, (4, 4, 5, 5), (6, 7, 6, 7)):
                out[...] = add(kept[:, p[y], p[x]], came[:, p[y], p[x]]).astype(bf16)

        shape = ((4, self.total, STACK), bf16)
        own, to_x, to_y, to_both = small_call(
            "scatter_layer" + self.tag, kernel, self.places, self.parts, [shape] * 4
        )
        diagonal = lax.ppermute(to_both, "fsdp", [(f, f ^ 3) for f in range(16)])
        self.parts = [own, along_x(to_x), along_y(to_y), diagonal]
        self.mark = own

    def layers(self):
        def kernel(p, one, two, three, four, *outs):
            for shift, out in enumerate(outs):
                z = (p[0] + shift) % 4
                out[...] = add(one[z], two[z], three[z], four[z]).astype(out.dtype)

        own, *sends = small_call(
            "scatter_layers" + self.tag, kernel, self.places, self.parts,
            [((self.total, STACK), f32)] + [((self.total, STACK), bf16)] * 3,
        )
        self.parts = [own] + [along_z(send, shift + 1) for shift, send in enumerate(sends)]
        self.mark = own

    def finish(self):
        def kernel(p, own, first, second, third, *outs):
            value = add(own[...], first[...], second[...], third[...])
            offset = 0
            for width, out in zip(self.widths, outs):
                out[...] = value[offset : offset + width].T
                offset += width

        return small_call(
            "scatter_sum" + self.tag, kernel, self.places, self.parts,
            [((STACK, width), f32) for width in self.widths],
        )


class WholeScatter:
    def __init__(self, terms, tag):
        members = lax.axis_size(BOTH)
        packed = jnp.concatenate(
            [term.reshape(members, -1, STACK).astype(f32) for term in terms], axis=1
        )
        self.widths = [term.shape[0] // members for term in terms]
        self.summed = lax.psum_scatter(packed, BOTH, scatter_dimension=0, tiled=False)
        self.mark = terms[0]

    def wait_for(self, other):
        pass

    def layer(self):
        pass

    def layers(self):
        pass

    def finish(self):
        grads = []
        offset = 0
        for width in self.widths:
            grads.append(self.summed[offset : offset + width].T)
            offset += width
        return grads


def on_device(
    tokens,
    cotangent,
    adapter_index,
    filled,
    ln1_gain,
    ln1_shift,
    qkv_weight,
    qv_bias,
    out_weight,
    out_bias,
    ln2_gain,
    ln2_shift,
    fc1_weight,
    fc1_bias,
    fc2_weight,
    fc2_bias,
    qkv_down,
    qkv_up,
    out_down,
    out_up,
    fc1_down,
    fc1_up,
    fc2_down,
    fc2_up,
):
    images = tokens.shape[0]
    own_start = lax.axis_index("tensor") * images
    who = lax.dynamic_slice_in_dim(
        jnp.stack([adapter_index, filled]), own_start, images, 1
    )
    vectors = jnp.concatenate(
        [ln1_gain, ln1_shift, out_bias, ln2_gain, ln2_shift, fc2_bias, fc1_bias]
    ).astype(f32)[None, :]
    stack_list = (qkv_down, qkv_up, out_down, out_up, fc1_down, fc1_up, fc2_down, fc2_up)
    steps = (lax.axis_size("fsdp"), lax.axis_size("tensor"), images) == STEPS
    shards = [transposed(stacked) for stacked in stack_list]
    gather = (StepGather if steps else WholeGather)(
        qkv_weight, out_weight, fc1_weight, fc2_weight, shards
    )
    scatter = StepScatter if steps else WholeScatter
    groups = gather.groups
    tokens = untangle(tokens)
    cotangent = untangle(cotangent)
    qkv_sources, places, stacks, moves = gather.first(tokens, cotangent, vectors, who)
    q, k, v, low_one, qkv_down_full, qkv_up_full = qkv_project(
        tokens, qkv_sources, groups, places, stacks, moves, who, qv_bias, vectors
    )
    qkv_down_full = qkv_down_full.reshape(D, STACK)
    qkv_up_full = qkv_up_full.reshape(3 * D, STACK)
    q = gather.after_qkv(q)
    mixed = None
    for image in range(images):
        mixed = attend(q, k, v, image, mixed)
        if image == 0 and images > 1:
            mixed = (gather.between_images(mixed[0]), *mixed[1:])
    o, *kept = mixed
    out_sources, out_down_full, out_up_full = gather.second(o)
    h, low_out = out_project(
        tokens, o, out_sources, gather.lane, groups, out_down_full, out_up_full, who, vectors
    )
    mlp_weights, *stacks = gather.third()
    outputs, dh, grad_up2, grad_down2, grad_up1, grad_down1 = mlp(
        h, cotangent, mlp_weights, *stacks, who, vectors
    )
    do, grad_out_up, grad_out_down = out_back(
        dh, o, low_out, out_sources, gather.lane, groups, out_down_full, out_up_full, who
    )
    early = scatter(
        [grad_out_down, grad_out_up, grad_down1, grad_up1, grad_down2, grad_up2], "1"
    )
    do = after(do, early.mark)
    grads = None
    for image in range(images):
        grads = attend_back(q, k, v, do, o, kept, image, grads)
        if image == 0:
            early.wait_for(grads[0])
            early.layer()
            grads = (after(grads[0], early.mark), *grads[1:])
    dq, dk, dv = grads
    early.wait_for(dq)
    early.layers()
    dq = after(dq, early.mark)
    low_grad, grad_qkv_up, grad_qkv_down = qkv_grads(
        tokens, dq, dk, dv, low_one, qkv_up_full, who, vectors
    )
    late = scatter([grad_qkv_down, grad_qkv_up], "2")
    early_grads = early.finish()
    low_grad = after(low_grad, late.mark, early_grads[0])
    rows_grads = []
    for image in range(images):
        rows_grads.append(
            qkv_back(
                tokens, dh, dq, dk, dv, low_grad, qkv_sources, groups, qkv_down_full,
                vectors, rows_grads,
            )
        )
        if image == 0:
            late.wait_for(rows_grads[0])
            late.layer()
            rows_grads[0] = after(rows_grads[0], late.mark)
    input_grad = rows_grads[-1].transpose(1, 0, 2)
    late.layers()
    grads = [grad.reshape(ADAPTERS, RANK, -1) for grad in (*late.finish(), *early_grads)]
    return (outputs.transpose(1, 0, 2), input_grad, *grads)


def solution(mesh):
    images = P(BOTH, None, None)
    stacked = P(None, None, BOTH)
    in_specs = (
        images, images, P("fsdp"), P("fsdp"), P(), P(), P("fsdp", None, "tensor"), P(),
        P("tensor", "fsdp"), P(), P(), P(), P("fsdp", "tensor"), P(), P("tensor", "fsdp"), P(),
    ) + (stacked,) * 8
    out_specs = (images, images) + (stacked,) * 8
    return jax.shard_map(
        on_device, mesh=mesh, in_specs=in_specs, out_specs=out_specs, check_vma=False
    )
```

```python
import math
from functools import partial

import jax
import jax.numpy as jnp
from jax import lax
from jax.experimental import pallas as pl
from jax.experimental.pallas import tpu as pltpu
from jax.sharding import PartitionSpec as P

D = 1024
HEADS = 16
HEAD_DIM = 64
FF = 4096
SEQ = 577
RANK = 16
ADAPTERS = 8
STACK = ADAPTERS * RANK
TILE = 1024
STACK_SHAPES = ((16, 2, 32, STACK), (16, 2, 96, STACK))

epsilon = 1e-05
bf16 = jnp.bfloat16
f32 = jnp.float32
NN = (((1,), (0,)), ((), ()))
NT = (((1,), (1,)), ((), ()))
TN = (((0,), (0,)), ((), ()))
BOTH = ("fsdp", "tensor")


def dot(left, right, dims):
    return lax.dot_general(left, right, dims, preferred_element_type=f32)


def params():
    return pltpu.CompilerParams(vmem_limit_bytes=60 << 20)


def cost(flops, moved, exps=0):
    return pl.CostEstimate(flops=flops, bytes_accessed=moved, transcendentals=exps)


def smem():
    return pl.BlockSpec(memory_space=pltpu.SMEM)


def whole(shape):
    return pl.BlockSpec(shape, lambda *_: (0,) * len(shape), pipeline_mode=pl.Buffered(1))


GAIN1, SHIFT1, OUT_BIAS, GAIN2, SHIFT2, BIAS2, BIAS1 = range(7)


def vector(place):
    return pl.BlockSpec((1, D), lambda *_: (0, place), pipeline_mode=pl.Buffered(1))


def image_rows(width=D):
    return pl.BlockSpec((pl.Squeezed(), SEQ, width), lambda i: (i, 0, 0))


def normalize(values):
    center = values - jnp.mean(values, axis=-1, keepdims=True)
    inverse = lax.rsqrt(jnp.mean(center * center, axis=-1, keepdims=True) + epsilon)
    return center * inverse, inverse


def norm_back(upstream, normed, inverse, gain_row):
    scaled = upstream * gain_row
    return inverse * (
        scaled
        - jnp.mean(scaled, axis=-1, keepdims=True)
        - normed * jnp.mean(scaled * normed, axis=-1, keepdims=True)
    )


def chosen_lanes(adapter):
    lanes = lax.broadcasted_iota(jnp.int32, (1, STACK), 1)
    return (lanes // RANK) == adapter


def keep(product, adapter):
    return jnp.where(chosen_lanes(adapter), product, 0.0).astype(bf16)


def add_to(ref, value, first):
    @pl.when(first)
    def _():
        ref[...] = value

    @pl.when(jnp.logical_not(first))
    def _():
        ref[...] += value


def flat(block):
    return block.reshape(D, block.shape[-1])


def any_space():
    return pl.BlockSpec(memory_space=pl.ANY)


def untangle_kernel(mixed_ref, out_ref):
    for image in range(out_ref.shape[0]):
        out_ref[image] = mixed_ref[:, image, :]


def untangle(array):
    images = array.shape[0]
    return pl.pallas_call(
        untangle_kernel,
        grid=(1,),
        in_specs=[whole((SEQ, images, D))],
        out_specs=whole((images, SEQ, D)),
        out_shape=jax.ShapeDtypeStruct((images, SEQ, D), array.dtype),
        compiler_params=pltpu.CompilerParams(vmem_limit_bytes=32 << 20),
        name="untangle",
    )(array.transpose(1, 0, 2))


class Stream:
    def __init__(self, sources, lane, width, slots, sems):
        self.sources, self.lane, self.width = sources, lane, width
        self.slots, self.sems = slots, sems

    def copy(self, source, inner, slot):
        lanes = pl.ds(self.lane, self.width)
        return pltpu.make_async_copy(
            source.at[inner, :, :, lanes], self.slots.at[slot], self.sems.at[slot]
        )

    def start(self, group, slot):
        offset = 0
        for source in self.sources:
            count = source.shape[0]

            @pl.when(jnp.logical_and(group >= offset, group < offset + count))
            def _(source=source, offset=offset):
                self.copy(source, group - offset, slot).start()

            offset += count

    def wait(self, slot):
        self.copy(self.sources[0], 0, slot).wait()


def spread_copies(sources, lane, parts, table_ref, weight_ref, sem):
    members, rows, total = weight_ref.shape
    groups = group_count(sources)
    width = total // parts // groups
    group = 0
    for source in sources:
        for inner in range(source.shape[0]):
            start = pl.multiple_of(table_ref[group] * width, width)
            for part in range(parts):
                yield pltpu.make_async_copy(
                    source.at[inner, :, :, pl.ds(lane + part * width, width)],
                    weight_ref.at[:, :, pl.ds(part * width * groups + start, width)],
                    sem.at[group * parts + part],
                )
            group += 1


def spread_scratch(sources, parts):
    members, rows = sources[0].shape[1:3]
    return [
        pltpu.VMEM((members, rows, parts * D), bf16),
        pltpu.SemaphoreType.DMA((group_count(sources) * parts,)),
    ]


def qkv_kernel(count, moves, *refs):
    table_ref, places_ref, index_ref, tokens_ref = refs[:4]
    sources = refs[4 : 4 + count]
    stacks = refs[4 + count : 6 + count]
    bias_ref, gain_ref, shift_ref = refs[6 + count : 9 + count]
    (
        q_ref, k_ref, v_ref, low_ref, down_ref, up_ref,
        a_s, low_s, up_s, slots, sems, stack_sems,
    ) = refs[9 + count :]
    copies = [
        pltpu.make_async_copy(
            source(stacks[part], places_ref),
            target((down_ref, up_ref)[out], places_ref),
            stack_sems.at[number],
        )
        for number, (part, out, source, target) in enumerate(moves)
    ]
    group = pl.program_id(0)
    image = pl.program_id(1)
    width = q_ref.shape[-1]
    stream = Stream(sources, 0, 3 * width, slots, sems)
    slot = group % 2

    @pl.when(jnp.logical_and(group == 0, image == 0))
    def _():
        for copy in copies:
            copy.start()
        stream.start(group, 0)

    @pl.when(group == 0)
    def _():
        normed, _ = normalize(tokens_ref[...].astype(f32))
        a_s[image] = (normed * gain_ref[...] + shift_ref[...]).astype(bf16)

    @pl.when(jnp.logical_and(group == 0, image == 0))
    def _():
        for copy in copies:
            copy.wait()
        up_s[...] = up_ref[...].reshape(3 * D, STACK)

    @pl.when(group == 0)
    def _():
        down = down_ref[...].reshape(D, STACK)
        low_s[image] = keep(dot(a_s[image], down, NN), index_ref[0, image])

    @pl.when(image == 0)
    def _():
        stream.wait(slot)

        @pl.when(group + 1 < pl.num_programs(0))
        def _():
            stream.start(group + 1, 1 - slot)

    a = a_s[image]
    low = low_s[image]
    low_ref[...] = low
    weight = flat(slots[slot])
    start = pl.multiple_of(table_ref[group] * width, width)
    bias = bias_ref[...].astype(f32)
    for part, out_ref in enumerate((q_ref, k_ref, v_ref)):
        value = dot(a, weight[:, part * width : (part + 1) * width], NN)
        value += dot(low, up_s[pl.ds(part * D + start, width), :], NT)
        if part != 1:
            value += bias[part // 2 : part // 2 + 1]
        out_ref[...] = value.astype(bf16)


def group_count(sources):
    return sum(source.shape[0] for source in sources)


def qkv_project(tokens, sources, table, places, stacks, moves, who, bias, vectors):
    images = tokens.shape[0]
    members, rows = sources[0].shape[1:3]
    groups = group_count(sources)
    width = D // groups
    sq = pl.Squeezed()
    out = pl.BlockSpec((sq, SEQ, width), lambda g, i, t: (i, 0, t[g]))
    grid_spec = pltpu.PrefetchScalarGridSpec(
        num_scalar_prefetch=1,
        grid=(groups, images),
        in_specs=[smem(), smem(), pl.BlockSpec((sq, SEQ, D), lambda g, i, t: (i, 0, 0))]
        + [any_space()] * (len(sources) + 2)
        + [pl.BlockSpec((2, width), lambda g, i, t: (0, t[g])), vector(GAIN1), vector(SHIFT1)],
        out_specs=[out, out, out, pl.BlockSpec((sq, SEQ, STACK), lambda g, i, t: (i, 0, 0))]
        + [pl.BlockSpec(shape, lambda g, i, t: (0, 0, 0, 0)) for shape in STACK_SHAPES],
        scratch_shapes=[
            pltpu.VMEM((images, SEQ, D), bf16),
            pltpu.VMEM((images, SEQ, STACK), bf16),
            pltpu.VMEM((3 * D, STACK), bf16),
            pltpu.VMEM((2, members, rows, 3 * width), bf16),
            pltpu.SemaphoreType.DMA((2,)),
            pltpu.SemaphoreType.DMA((len(moves),)),
        ],
    )
    return pl.pallas_call(
        partial(qkv_kernel, len(sources), moves),
        grid_spec=grid_spec,
        out_shape=[jax.ShapeDtypeStruct((images, SEQ, D), bf16)] * 3
        + [jax.ShapeDtypeStruct((images, SEQ, STACK), bf16)]
        + [jax.ShapeDtypeStruct(shape, bf16) for shape in STACK_SHAPES],
        compiler_params=params(),
        cost_estimate=cost(6 * images * SEQ * D * D, 20 << 20),
        name="qkv_project",
    )(table, places, who, tokens, *sources, *stacks, bias, vectors, vectors)


def attend_kernel(q_ref, k_ref, v_ref, o_ref, w_ref, scale_ref):
    q = q_ref[...]
    k = k_ref[...]
    v = v_ref[...]
    low = lax.broadcasted_iota(jnp.int32, q.shape, 1) < HEAD_DIM
    both = jnp.concatenate([v, jnp.ones_like(v)], axis=1)
    outs = []
    for head in range(2):
        own = low if head == 0 else jnp.logical_not(low)
        queries = jnp.where(own, q * HEAD_DIM**-0.5, jnp.zeros_like(q)).astype(bf16)
        scores = dot(queries, k, NT)
        raised = jnp.exp(scores - jnp.max(scores, axis=-1, keepdims=True)).astype(bf16)
        w_ref[head] = raised
        outs.append(dot(raised, both, NN))
    width = v.shape[-1]
    scale = 1.0 / jnp.where(low, outs[0][:, width:], outs[1][:, width:])
    scale_ref[...] = scale
    o_ref[...] = (jnp.where(low, outs[0][:, :width], outs[1][:, :width]) * scale).astype(bf16)


def pair_rows(image):
    return pl.BlockSpec((pl.Squeezed(), SEQ, 2 * HEAD_DIM), lambda h: (image, 0, h))


def pair_weights(image):
    return pl.BlockSpec((2, SEQ, SEQ), lambda h: (image * (HEADS // 2) + h, 0, 0))


def into(kernel, inputs):
    def body(*refs):
        kernel(*refs[:inputs], *refs[len(refs) - (len(refs) - inputs) // 2 :])

    return body


def per_image(kernel, name, image, inputs, in_specs, outs, out_specs, filled, flops, moved, exps):
    count = len(inputs)
    if filled is None:
        return pl.pallas_call(
            kernel, grid=(HEADS // 2,), in_specs=in_specs, out_specs=out_specs, out_shape=outs,
            compiler_params=params(), cost_estimate=cost(flops, moved, exps), name=name,
        )(*inputs)
    return pl.pallas_call(
        into(kernel, count), grid=(HEADS // 2,), in_specs=in_specs + [any_space()] * len(outs),
        out_specs=out_specs, out_shape=outs,
        input_output_aliases={count + n: n for n in range(len(outs))},
        compiler_params=params(), cost_estimate=cost(flops, moved, exps), name=name,
    )(*inputs, *filled)


def attend(q, k, v, image, filled):
    images = q.shape[0]
    outs = [
        jax.ShapeDtypeStruct((images, SEQ, D), bf16),
        jax.ShapeDtypeStruct((images * HEADS, SEQ, SEQ), bf16),
        jax.ShapeDtypeStruct((images, SEQ, D), f32),
    ]
    return per_image(
        attend_kernel, "attend", image, (q, k, v), [pair_rows(image)] * 3, outs,
        [pair_rows(image), pair_weights(image), pair_rows(image)], filled,
        16 * SEQ * SEQ * D, 20 << 20, HEADS * SEQ * SEQ,
    )


def attend_back_kernel(
    q_ref, k_ref, v_ref, do_ref, o_ref, w_ref, scale_ref, dq_ref, dk_ref, dv_ref
):
    q = q_ref[...]
    k = k_ref[...]
    v = v_ref[...]
    do = (do_ref[...].astype(f32) * scale_ref[...]).astype(bf16)
    products = do.astype(f32) * o_ref[...].astype(f32)
    low = lax.broadcasted_iota(jnp.int32, q.shape, 1) < HEAD_DIM
    grads = []
    for head in range(2):
        own = low if head == 0 else jnp.logical_not(low)
        mixed_grad = jnp.where(own, do, jnp.zeros_like(do))
        inner = jnp.sum(jnp.where(own, products, 0.0), axis=-1, keepdims=True)
        raised = w_ref[head]
        prob_grad = dot(mixed_grad, v, NT)
        score_grad = (raised.astype(f32) * (prob_grad - inner)).astype(bf16)
        grads.append((dot(score_grad, k, NN), dot(score_grad, q, TN), dot(raised, do, TN)))
    scale = HEAD_DIM**-0.5
    dq_ref[...] = (jnp.where(low, grads[0][0], grads[1][0]) * scale).astype(bf16)
    dk_ref[...] = (jnp.where(low, grads[0][1], grads[1][1]) * scale).astype(bf16)
    dv_ref[...] = jnp.where(low, grads[0][2], grads[1][2]).astype(bf16)


def attend_back(q, k, v, do, o, kept, image, filled):
    outs = [jax.ShapeDtypeStruct(q.shape, bf16)] * 3
    return per_image(
        attend_back_kernel, "attend_back", image, (q, k, v, do, o, *kept),
        [pair_rows(image)] * 5 + [pair_weights(image), pair_rows(image)], outs,
        [pair_rows(image)] * 3, filled, 32 * SEQ * SEQ * D, 24 << 20, 0,
    )


def out_kernel(count, lane, *refs):
    table_ref, index_ref, filled_ref, tokens_ref, o_ref = refs[:5]
    sources = refs[5 : 5 + count]
    down_ref, up_ref, bias_ref, h_ref, low_ref, weight_s, sems = refs[5 + count :]
    image = pl.program_id(0)

    @pl.when(image == 0)
    def _():
        for copy in spread_copies(sources, lane, 1, table_ref, weight_s, sems):
            copy.start()

    low = keep(dot(o_ref[...], down_ref[...], NN), index_ref[0, image])
    low_ref[...] = low

    @pl.when(image == 0)
    def _():
        for copy in spread_copies(sources, lane, 1, table_ref, weight_s, sems):
            copy.wait()

    value = dot(o_ref[...], flat(weight_s[...]), NT) + dot(low, up_ref[...], NT) + bias_ref[...]
    h_ref[...] = tokens_ref[...].astype(f32) + filled_ref[1, image].astype(f32) * value


def out_project(tokens, o, sources, lane, table, down, up, who, vectors):
    images = tokens.shape[0]
    return pl.pallas_call(
        partial(out_kernel, len(sources), lane),
        grid=(images,),
        in_specs=[smem(), smem(), smem(), image_rows(), image_rows()]
        + [any_space()] * len(sources)
        + [whole((D, STACK)), whole((D, STACK)), vector(OUT_BIAS)],
        out_specs=[image_rows(), image_rows(STACK)],
        out_shape=[
            jax.ShapeDtypeStruct((images, SEQ, D), f32),
            jax.ShapeDtypeStruct((images, SEQ, STACK), bf16),
        ],
        scratch_shapes=spread_scratch(sources, 1),
        compiler_params=params(),
        cost_estimate=cost(2 * images * SEQ * D * D, 12 << 20),
        name="out_project",
    )(table, who, who, tokens, o, *sources, down, up, vectors)


def out_back_kernel(count, lane, *refs):
    table_ref, index_ref, filled_ref, dh_ref, o_ref, low_ref = refs[:6]
    sources = refs[6 : 6 + count]
    down_ref, up_ref, do_ref, grad_up_ref, grad_down_ref = refs[6 + count : 11 + count]
    grad_up_s, grad_down_s, weight_s, sems = refs[11 + count :]
    image = pl.program_id(0)
    last = image == pl.num_programs(0) - 1

    @pl.when(image == 0)
    def _():
        for copy in spread_copies(sources, lane, 1, table_ref, weight_s, sems):
            copy.start()
        grad_up_s[...] = jnp.zeros_like(grad_up_s)
        grad_down_s[...] = jnp.zeros_like(grad_down_s)

    branch = (dh_ref[...] * filled_ref[1, image].astype(f32)).astype(bf16)
    low_grad = keep(dot(branch, up_ref[...], NN), index_ref[0, image])
    grad_up_s[...] += dot(low_ref[...], branch, TN)
    grad_down_s[...] += dot(low_grad, o_ref[...], TN)

    @pl.when(image == 0)
    def _():
        for copy in spread_copies(sources, lane, 1, table_ref, weight_s, sems):
            copy.wait()

    value = dot(branch, flat(weight_s[...]), NN) + dot(low_grad, down_ref[...], NT)
    do_ref[...] = value.astype(bf16)

    @pl.when(last)
    def _():
        grad_up_ref[...] = grad_up_s[...].T.astype(bf16)
        grad_down_ref[...] = grad_down_s[...].T.astype(bf16)


def out_back(dh, o, low, sources, lane, table, down, up, who):
    images = dh.shape[0]
    grad = pl.BlockSpec((D, STACK), lambda i: (0, 0))
    return pl.pallas_call(
        partial(out_back_kernel, len(sources), lane),
        grid=(images,),
        in_specs=[smem(), smem(), smem(), image_rows(), image_rows(), image_rows(STACK)]
        + [any_space()] * len(sources)
        + [whole((D, STACK)), whole((D, STACK))],
        out_specs=[image_rows(), grad, grad],
        out_shape=[jax.ShapeDtypeStruct((images, SEQ, D), bf16)]
        + [jax.ShapeDtypeStruct((D, STACK), bf16)] * 2,
        scratch_shapes=[pltpu.VMEM((STACK, D), f32)] * 2 + spread_scratch(sources, 1),
        compiler_params=params(),
        cost_estimate=cost(2 * images * SEQ * D * D, 12 << 20),
        name="out_back",
    )(table, who, who, dh, o, low, *sources, down, up)


def mlp_kernel(sides, *refs):
    index_ref, filled_ref, h_ref, cot_ref, first_ref, second_ref, down1_ref = refs[:7]
    up1_refs = refs[7 : 7 + sides]
    down2_refs = refs[7 + sides : 7 + 2 * sides]
    (
        up2_ref, bias1_ref, bias2_ref, gain_ref, shift_ref,
        out_ref, dh_ref, grad_up2_ref, grad_down2_ref, grad_up1_ref, grad_down1_ref,
        a_s, dz_s, low3_s, dlow4_s, z_s, da_s, low4_s, dlow3_s,
        grad_up2_s, grad_down2_s, grad_up1_s, grad_down1_s,
    ) = refs[7 + 2 * sides :]
    width = grad_up1_ref.shape[0]
    tall = lambda parts: jnp.concatenate([part[...] for part in parts], axis=2).reshape(
        width, STACK
    )
    up1 = tall(up1_refs)
    down2 = tall(down2_refs)
    tile = pl.program_id(0)
    image = pl.program_id(1)
    last = tile == pl.num_programs(0) - 1
    final = image == pl.num_programs(1) - 1
    adapter = index_ref[0, image]
    mask = filled_ref[1, image].astype(f32)

    @pl.when(image == 0)
    def _():
        grad_down2_s[...] = jnp.zeros_like(grad_down2_s)
        grad_up1_s[...] = jnp.zeros_like(grad_up1_s)

    @pl.when(tile == 0)
    def _():
        for ref in (z_s, da_s, low4_s, dlow3_s):
            ref[image] = jnp.zeros(ref.shape[1:], f32)
        normed, _ = normalize(h_ref[image])
        a = (normed * gain_ref[...] + shift_ref[...]).astype(bf16)
        a_s[image] = a
        dz = (cot_ref[image].astype(f32) * mask).astype(bf16)
        dz_s[image] = dz
        low3_s[image] = keep(dot(a, down1_ref[...], NN), adapter)
        dlow4_s[image] = keep(dot(dz, up2_ref[...], NN), adapter)

    a = a_s[image]
    dz = dz_s[image]
    low3 = low3_s[image]
    dlow4 = dlow4_s[image]
    first = flat(first_ref[...])
    second = flat(second_ref[...])
    before = dot(a, first, NN) + dot(low3, up1, NT) + bias1_ref[...]
    density = jnp.exp(before * before * -0.5) * 0.3989422804014327
    below = 0.5 * lax.erf(before * 0.7071067811865476) + 0.5
    g = (before * below).astype(bf16)
    slope = below + before * density
    dg = dot(dz, second, NN) + dot(dlow4, down2, NT)
    df = (dg * slope).astype(bf16)
    z_s[image] += dot(g, second, NT)
    da_s[image] += dot(df, first, NT)
    low4_s[image] += dot(g, down2, NN)
    dlow3_s[image] += dot(df, up1, NN)
    grad_down2_s[...] += dot(dlow4, g, TN)
    grad_up1_s[...] += dot(low3, df, TN)

    @pl.when(final)
    def _():
        grad_down2_ref[...] = grad_down2_s[...].T.astype(bf16)
        grad_up1_ref[...] = grad_up1_s[...].T.astype(bf16)

    @pl.when(last)
    def _():
        low4 = keep(low4_s[image], adapter)
        h = h_ref[image]
        z = z_s[image] + dot(low4, up2_ref[...], NT) + bias2_ref[...]
        outputs = (h + mask * z).astype(bf16)
        for number in range(out_ref.shape[1]):

            @pl.when(image == number)
            def _(number=number):
                out_ref[:, number, :] = outputs

        add_to(grad_up2_s, dot(low4, dz, TN), image == 0)
        dlow3 = keep(dlow3_s[image], adapter)
        da = da_s[image] + dot(dlow3, down1_ref[...], NT)
        add_to(grad_down1_s, dot(dlow3, a, TN), image == 0)
        normed, inverse = normalize(h)
        dh_ref[...] = cot_ref[image].astype(f32) + norm_back(
            da, normed, inverse, gain_ref[...]
        )

    @pl.when(jnp.logical_and(last, final))
    def _():
        grad_up2_ref[...] = grad_up2_s[...].T.astype(bf16)
        grad_down1_ref[...] = grad_down1_s[...].T.astype(bf16)


def mlp(h, cot, weights, down1, up1, down2, up2, who, vectors):
    images = h.shape[0]
    members, groups, rows, _ = weights.shape
    hidden = FF // groups
    width = min(TILE, hidden)
    per_group = hidden // width
    tiles = FF // width
    sq = pl.Squeezed()

    def weight(base):
        return pl.BlockSpec(
            (members, sq, rows, width),
            lambda j, i: (0, j // per_group, 0, base * per_group + j % per_group),
        )

    tall = pl.BlockSpec((width, STACK), lambda j, i: (j, 0))
    sides = up1 + down2

    def side_block(array, lane):
        shape = (16 * width // FF, 2, FF // 32 // len(up1), STACK)
        return pl.BlockSpec(shape, lambda j, i: (j, 0, 0, lane))

    short = pl.BlockSpec((D, STACK), lambda j, i: (0, 0))
    late = pl.BlockSpec((sq, SEQ, D), lambda j, i: (jnp.where(j == tiles - 1, i, 0), 0, 0))
    return pl.pallas_call(
        partial(mlp_kernel, len(up1)),
        grid=(tiles, images),
        in_specs=[
            smem(),
            smem(),
            whole((images, SEQ, D)),
            whole((images, SEQ, D)),
            weight(0),
            weight(1),
            whole((D, STACK)),
        ]
        + [side_block(*side) for side in sides]
        + [
            whole((D, STACK)),
            pl.BlockSpec((1, width), lambda j, i: (0, BIAS1 * D // width + j)),
            vector(BIAS2),
            vector(GAIN2),
            vector(SHIFT2),
        ],
        out_specs=[pl.BlockSpec((SEQ, images, D), lambda j, i: (0, 0, 0)), late, short, tall, tall, short],
        out_shape=[
            jax.ShapeDtypeStruct((SEQ, images, D), bf16),
            jax.ShapeDtypeStruct((images, SEQ, D), f32),
            jax.ShapeDtypeStruct((D, STACK), bf16),
            jax.ShapeDtypeStruct((FF, STACK), bf16),
            jax.ShapeDtypeStruct((FF, STACK), bf16),
            jax.ShapeDtypeStruct((D, STACK), bf16),
        ],
        scratch_shapes=[
            pltpu.VMEM((images, SEQ, D), bf16),
            pltpu.VMEM((images, SEQ, D), bf16),
            pltpu.VMEM((images, SEQ, STACK), bf16),
            pltpu.VMEM((images, SEQ, STACK), bf16),
            pltpu.VMEM((images, SEQ, D), f32),
            pltpu.VMEM((images, SEQ, D), f32),
            pltpu.VMEM((images, SEQ, STACK), f32),
            pltpu.VMEM((images, SEQ, STACK), f32),
            pltpu.VMEM((STACK, D), f32),
            pltpu.VMEM((STACK, width), f32),
            pltpu.VMEM((STACK, width), f32),
            pltpu.VMEM((STACK, D), f32),
        ],
        compiler_params=params(),
        cost_estimate=cost(8 * images * SEQ * D * FF, 40 << 20, 2 * images * SEQ * FF),
        name="mlp",
    )(
        who, who, h, cot, weights, weights, down1, *[array for array, _ in sides], up2,
        vectors, vectors, vectors, vectors,
    )


def qkv_grads_kernel(
    index_ref, tokens_ref, dq_ref, dk_ref, dv_ref, low_ref, up_ref, gain_ref, shift_ref,
    low_grad_ref, grad_up_ref, grad_down_ref, grad_up_s, grad_down_s,
):
    image = pl.program_id(0)
    parts = (dq_ref, dk_ref, dv_ref)

    @pl.when(image == 0)
    def _():
        grad_up_s[...] = jnp.zeros_like(grad_up_s)
        grad_down_s[...] = jnp.zeros_like(grad_down_s)

    low = low_ref[...]
    low_grad = dot(parts[0][...], up_ref[0:D, :], NN)
    for part in (1, 2):
        low_grad += dot(parts[part][...], up_ref[part * D : (part + 1) * D, :], NN)
    low_grad = keep(low_grad, index_ref[0, image])
    low_grad_ref[...] = low_grad
    for part in range(3):
        grad_up_s[part] += dot(low, parts[part][...], TN)
    normed, _ = normalize(tokens_ref[...].astype(f32))
    a = (normed * gain_ref[...] + shift_ref[...]).astype(bf16)
    grad_down_s[...] += dot(low_grad, a, TN)

    @pl.when(image == pl.num_programs(0) - 1)
    def _():
        for part in range(3):
            grad_up_ref[part * D : (part + 1) * D, :] = grad_up_s[part].T.astype(bf16)
        grad_down_ref[...] = grad_down_s[...].T.astype(bf16)


def qkv_grads(tokens, dq, dk, dv, low, up, who, vectors):
    images = tokens.shape[0]
    return pl.pallas_call(
        qkv_grads_kernel,
        grid=(images,),
        in_specs=[smem()]
        + [image_rows()] * 4
        + [image_rows(STACK), whole((3 * D, STACK)), vector(GAIN1), vector(SHIFT1)],
        out_specs=[
            image_rows(STACK),
            pl.BlockSpec((3 * D, STACK), lambda i: (0, 0)),
            pl.BlockSpec((D, STACK), lambda i: (0, 0)),
        ],
        out_shape=[
            jax.ShapeDtypeStruct((images, SEQ, STACK), bf16),
            jax.ShapeDtypeStruct((3 * D, STACK), bf16),
            jax.ShapeDtypeStruct((D, STACK), bf16),
        ],
        scratch_shapes=[pltpu.VMEM((3, STACK, D), f32), pltpu.VMEM((STACK, D), f32)],
        compiler_params=params(),
        cost_estimate=cost(2 * images * SEQ * D * D, 12 << 20),
        name="qkv_grads",
    )(who, tokens, dq, dk, dv, low, up, vectors, vectors)


def qkv_back_kernel(count, image, *refs):
    table_ref = refs[0]
    arrays = refs[1:6]
    low_grad_ref = refs[6]
    sources = refs[7 : 7 + count]
    down_ref, gain_ref = refs[7 + count : 9 + count]
    grad_ref, dq_s, dk_s, dv_s, tokens_s, dh_s, earlier_s, row_sems, weight_s, sems = refs[-10:]
    earlier_refs = refs[9 + count : -10]
    weights = list(spread_copies(sources, 0, 3, table_ref, weight_s, sems))
    held = (tokens_s, dh_s, dq_s, dk_s, dv_s)
    rows = [
        pltpu.make_async_copy(array.at[image], into_ref, row_sems.at[number])
        for number, (array, into_ref) in enumerate(zip(arrays, held))
    ]
    before = [
        pltpu.make_async_copy(ref, earlier_s.at[number], row_sems.at[len(rows) + number])
        for number, ref in enumerate(earlier_refs)
    ]
    for part in range(3):
        rows[2 + part].start()
        for copy in weights[part::3]:
            copy.start()
    for copy in (rows[0], rows[1], *before):
        copy.start()
    da = dot(low_grad_ref[...], down_ref[...], NT)
    for part, part_s in enumerate((dq_s, dk_s, dv_s)):
        rows[2 + part].wait()
        for copy in weights[part::3]:
            copy.wait()
        da += dot(part_s[...], flat(weight_s[:, :, part * D : (part + 1) * D]), NT)
    rows[0].wait()
    normed, inverse = normalize(tokens_s[...].astype(f32))
    rows[1].wait()
    grad = dh_s[...] + norm_back(da, normed, inverse, gain_ref[...])
    if len(grad_ref.shape) == 2:
        grad_ref[...] = grad
    else:
        for number, copy in enumerate(before):
            copy.wait()
            grad_ref[:, number, :] = earlier_s[number]
        grad_ref[:, len(before), :] = grad


def qkv_back(tokens, dh, dq, dk, dv, low_grad, sources, table, down, vectors, earlier):
    images = tokens.shape[0]
    image = len(earlier)
    out = (SEQ, D) if image + 1 < images else (SEQ, images, D)
    return pl.pallas_call(
        partial(qkv_back_kernel, len(sources), image),
        grid=(1,),
        in_specs=[smem()]
        + [any_space()] * 5
        + [pl.BlockSpec((pl.Squeezed(), SEQ, STACK), lambda i: (image, 0, 0))]
        + [any_space()] * len(sources)
        + [whole((D, STACK)), vector(GAIN1)]
        + [any_space()] * image,
        out_specs=whole(out),
        out_shape=jax.ShapeDtypeStruct(out, f32),
        scratch_shapes=[pltpu.VMEM((SEQ, D), bf16)] * 4
        + [
            pltpu.VMEM((SEQ, D), f32),
            pltpu.VMEM((max(image, 1), SEQ, D), f32),
            pltpu.SemaphoreType.DMA((5 + max(image, 1),)),
        ]
        + spread_scratch(sources, 3),
        compiler_params=params(),
        cost_estimate=cost(6 * SEQ * D * D, 18 << 20),
        name="qkv_back",
    )(table, tokens, dh, dq, dk, dv, low_grad, *sources, down, vectors, *earlier)


STEPS = (16, 2, 2)


def along_x(array):
    return lax.ppermute(array, "fsdp", [(f, f ^ 1) for f in range(16)])


def along_y(array):
    return lax.ppermute(array, "fsdp", [(f, f ^ 2) for f in range(16)])


def along_z(array, shift):
    pairs = [(f, (f // 4 + shift) % 4 * 4 + f % 4) for f in range(16)]
    return lax.ppermute(array, "fsdp", pairs)


def other_core(array):
    return lax.ppermute(array, "tensor", [(0, 1), (1, 0)])


def positions():
    f = lax.axis_index("fsdp")
    t = lax.axis_index("tensor")
    z, y, x = f // 4, f // 2 % 2, f % 2
    places = [z, (z + 3) % 4, (z + 2) % 4, (z + 1) % 4, y, 1 - y, x, 1 - x, t, 1 - t]
    return jnp.stack(places).astype(jnp.int32)


def move(name, places, parts, outs, moves, room=None):
    room = room or (4 << 20) + sum(2 * math.prod(shape) for shape in outs)

    def kernel(places_ref, *refs):
        sems = refs[-1]
        copies = []
        for number, (part, out, source, target) in enumerate(moves):
            copies.append(
                pltpu.make_async_copy(
                    source(refs[part], places_ref),
                    target(refs[len(parts) + out], places_ref),
                    sems.at[number],
                )
            )
            copies[-1].start()
        for copy in copies:
            copy.wait()

    return pl.pallas_call(
        kernel,
        in_specs=[smem()] + [any_space()] * len(parts),
        out_specs=[pl.BlockSpec(memory_space=pltpu.VMEM)] * len(outs),
        out_shape=[jax.ShapeDtypeStruct(shape, bf16) for shape in outs],
        scratch_shapes=[pltpu.SemaphoreType.DMA((len(moves),))],
        compiler_params=pltpu.CompilerParams(vmem_limit_bytes=room),
        name=name,
    )(places, *parts)


def everything(ref, places):
    return ref


def after(value, *others):
    return lax.optimization_barrier((value, *others))[0]


class Piece:
    def __init__(self, shard, places, tag):
        self.shard, self.places, self.tag = shard, places, tag
        self.rows, self.half = shard.shape[0], shard.shape[1] // 2

    def send_z(self):
        self.parts = [self.shard] + [along_z(self.shard, shift) for shift in (1, 2, 3)]

    def wait_for(self, other):
        self.parts[0] = after(self.parts[0], other)

    def join_z(self):
        half = self.half
        self.a, self.b = move(
            "gather_z" + self.tag, self.places, self.parts, [(4, self.rows, half)] * 2,
            [
                (
                    shift, side,
                    lambda ref, p, side=side: ref.at[:, pl.ds(side * half, half)],
                    lambda ref, p, shift=shift: ref.at[p[shift]],
                )
                for shift in range(4)
                for side in range(2)
            ],
            room=60 << 20,
        )

    def send_half(self):
        self.parts = [self.a, along_y(self.a), self.b, along_x(self.b)]

    def join_half(self):
        self.a, self.b = move(
            "gather_yx" + self.tag, self.places, self.parts, [(4, 2, self.rows, self.half)] * 2,
            [
                (0, 0, everything, lambda ref, p: ref.at[:, p[4]]),
                (1, 0, everything, lambda ref, p: ref.at[:, p[5]]),
                (2, 1, everything, lambda ref, p: ref.at[:, p[6]]),
                (3, 1, everything, lambda ref, p: ref.at[:, p[7]]),
            ],
        )

    def send_rest(self):
        self.parts = [self.a, along_x(self.a), self.b, along_y(self.b)]

    def join_rest(self):
        (joined,) = move(
            "gather_xy" + self.tag, self.places, self.parts,
            [(2, 4, 2, 2, self.rows, self.half)],
            [
                (0, 0, everything, lambda ref, p: ref.at[0, :, :, p[6]]),
                (1, 0, everything, lambda ref, p: ref.at[0, :, :, p[7]]),
                (2, 0, everything, lambda ref, p: ref.at[1, :, p[4]]),
                (3, 0, everything, lambda ref, p: ref.at[1, :, p[5]]),
            ],
        )
        self.own = joined.reshape(2, 16, self.rows, self.half)
        self.sources = (self.own, other_core(self.own))


class SmallPiece(Piece):
    def join_z(self):
        (self.a,) = move(
            "gather_z" + self.tag, self.places, self.parts, [(4, self.rows, 2 * self.half)],
            [
                (shift, 0, everything, lambda ref, p, shift=shift: ref.at[p[shift]])
                for shift in range(4)
            ],
        )

    def send_layer(self):
        diagonal = lax.ppermute(self.a, "fsdp", [(f, f ^ 3) for f in range(16)])
        self.parts = [self.a, along_x(self.a), along_y(self.a), diagonal]

    def join_layer(self):
        half = self.half
        (joined,) = move(
            "gather_layer" + self.tag, self.places, self.parts,
            [(2, 4, 2, 2, self.rows, half)],
            [
                (
                    part, 0,
                    lambda ref, p, side=side: ref.at[:, :, pl.ds(side * half, half)],
                    lambda ref, p, side=side, y=y, x=x: ref.at[side, :, p[y], p[x]],
                )
                for part, (y, x) in enumerate(((4, 6), (4, 7), (5, 6), (5, 7)))
                for side in range(2)
            ],
        )
        self.own = joined.reshape(2, 16, self.rows, half)
        self.sources = (self.own, other_core(self.own))


def transposed(stacked):
    return stacked.reshape(STACK, -1).T


def halves(rows_by_lanes, pieces):
    rows = rows_by_lanes.shape[0]
    split = rows_by_lanes.reshape(rows, pieces, 2, -1)
    return [split[:, :, side].reshape(rows, -1) for side in range(2)]


class StepGather:
    def __init__(self, qkv_weight, out_weight, fc1_weight, fc2_weight, shards):
        rows, _, column = qkv_weight.shape
        qd, qu, od, ou, f1d, f1u, f2d, f2u = shards
        places = positions()
        t = lax.axis_index("tensor")
        qkv_a, qkv_b = halves(qkv_weight.reshape(rows, 3 * column), 3)
        out_a, out_b = halves(out_weight.T, 1)
        low1 = jnp.concatenate([qd, qu], axis=0)
        low2 = jnp.concatenate([od, ou], axis=0)
        low3 = jnp.concatenate([f1d, f2u], axis=0)
        self.piece1 = Piece(
            jnp.concatenate([qkv_a, low1[:64], qkv_b, low1[64:]], axis=1), places, "1"
        )
        self.piece2 = SmallPiece(jnp.concatenate([out_a, low2, out_b, low3], axis=1), places, "2")
        hidden = jnp.concatenate(
            [fc1_weight, fc2_weight.T, f1u[:64], f1u[64:], f2d[:64], f2d[64:]], axis=1
        )
        self.hidden = hidden
        self.places, self.column = places, column
        self.width = fc1_weight.shape[1]
        self.groups = jnp.stack([2 * t, 2 * t + 1, 2 - 2 * t, 3 - 2 * t]).astype(jnp.int32)
        self.lane = 0

    def first(self, tokens, *others):
        one, two = self.piece1, self.piece2
        one.send_z()
        one.join_z()
        hidden = after(self.hidden, one.a)
        two.shard = after(two.shard, one.a)
        self.hidden = lax.all_gather(hidden, BOTH, axis=0).reshape(16, 2, *hidden.shape)
        one.send_half()
        one.wait_for(tokens)
        one.join_half()
        one.send_rest()
        one.parts[0] = after(one.parts[0], *others)
        one.join_rest()
        two.shard = after(two.shard, one.own)
        two.send_z()
        lanes = pl.ds(3 * self.column // 2, STACK)
        moves = [
            m
            for source, core in ((0, 8), (1, 9))
            for m in (
                (source, 0, lambda ref, p: ref.at[0, :, pl.ds(0, 32), lanes],
                 lambda ref, p, core=core: ref.at[:, p[core]]),
                (source, 1, lambda ref, p: ref.at[0, :, pl.ds(32, 32), lanes],
                 lambda ref, p, core=core: ref.at[:, p[core], pl.ds(0, 32)]),
                (source, 1, lambda ref, p: ref.at[1, :, :, lanes],
                 lambda ref, p, core=core: ref.at[:, p[core], pl.ds(32, 64)]),
            )
        ]
        return one.sources, self.places, one.sources, moves

    def after_qkv(self, q):
        return q

    def between_images(self, o):
        two = self.piece2
        two.wait_for(o)
        two.join_z()
        two.send_layer()
        return after(o, two.a)

    def second(self, o):
        self.piece2.wait_for(o)
        self.piece2.join_layer()
        lanes = pl.ds(self.column // 2, STACK)
        stacks = move(
            "stacks2", self.places, self.piece2.sources, [(16, 2, 32, STACK)] * 4,
            [
                (source, out,
                 lambda ref, p, out=out: ref.at[out // 2, :, pl.ds(out % 2 * 32, 32), lanes],
                 lambda ref, p, core=core: ref.at[:, p[core]])
                for source, core in ((0, 8), (1, 9))
                for out in range(4)
            ],
            room=60 << 20,
        )
        od, ou, f1d, f2u = [stack.reshape(-1, STACK) for stack in stacks]
        self.stacks = (f1d, f2u)
        return self.piece2.sources, od, ou

    def third(self):
        f1d, f2u = self.stacks
        base = 2 * self.width // STACK
        sides = [[(self.hidden, base + 2 * out + side) for side in range(2)] for out in range(2)]
        return self.hidden, f1d, sides[0], sides[1], f2u


class WholeGather:
    def __init__(self, qkv_weight, out_weight, fc1_weight, fc2_weight, shards):
        rows, _, column = qkv_weight.shape
        piece = jnp.concatenate(
            [fc1_weight, fc2_weight.T, qkv_weight.reshape(rows, 3 * column), out_weight.T],
            axis=1,
        )
        groups = lax.axis_size("tensor")
        self.joined = lax.all_gather(piece, BOTH, axis=0).reshape(-1, groups, *piece.shape)
        stacked = lax.all_gather(jnp.concatenate(shards, axis=0), BOTH, axis=0)
        self.full = []
        offset = 0
        for shard in shards:
            part = stacked[:, offset : offset + shard.shape[0]]
            self.full.append(part.reshape(-1, STACK))
            offset += shard.shape[0]
        start = 2 * fc1_weight.shape[1]
        by_group = self.joined[..., start:].transpose(1, 0, 2, 3)
        self.qkv, self.out = by_group[..., : 3 * column], by_group[..., 3 * column :]
        self.groups = jnp.arange(groups, dtype=jnp.int32)
        self.lane = 0

    def first(self, tokens, *others):
        stacks = [part.reshape(shape) for part, shape in zip(self.full[:2], STACK_SHAPES)]
        moves = [(part, part, everything, everything) for part in range(2)]
        return (self.qkv,), jnp.zeros((1,), jnp.int32), stacks, moves

    def after_qkv(self, q):
        return q

    def between_images(self, o):
        return o

    def second(self, o):
        return (self.out,), self.full[2], self.full[3]

    def third(self):
        down1, up1, down2, up2 = self.full[4:]
        view = lambda stack: [(stack.reshape(16, 2, -1, STACK), 0)]
        return self.joined, down1, view(up1), view(down2), up2


def small_call(name, kernel, places, parts, outs):
    vmem = pl.BlockSpec(memory_space=pltpu.VMEM)
    return pl.pallas_call(
        kernel,
        in_specs=[smem()] + [vmem] * len(parts),
        out_specs=[vmem] * len(outs),
        out_shape=[jax.ShapeDtypeStruct(shape, dtype) for shape, dtype in outs],
        compiler_params=pltpu.CompilerParams(vmem_limit_bytes=24 << 20),
        name=name,
    )(places, *parts)


def add(*values):
    total = values[0].astype(f32)
    for value in values[1:]:
        total += value.astype(f32)
    return total


class StepScatter:
    def __init__(self, terms, tag):
        self.places, self.tag = positions(), tag
        self.widths = [term.shape[0] // 32 for term in terms]
        self.total = sum(self.widths)
        moves = []
        offset = 0
        for number, width in enumerate(self.widths):
            for out, core in enumerate((8, 9)):
                moves.append(
                    (number, out,
                     lambda ref, p, core=core: ref.at[:, :, :, p[core]],
                     lambda ref, p, offset=offset, width=width: ref.at[
                         :, :, :, pl.ds(offset, width)])
                )
            offset += width
        split = [
            term.reshape(4, 2, 2, 2, width, STACK) for term, width in zip(terms, self.widths)
        ]
        kept, sent = move(
            "scatter_core" + tag, self.places, split, [(4, 2, 2, self.total, STACK)] * 2, moves,
            room=60 << 20,
        )
        self.parts = [kept, other_core(sent)]
        self.mark = kept

    def wait_for(self, other):
        self.parts[0] = after(self.parts[0], other)

    def layer(self):
        def kernel(p, kept, came, *outs):
            for out, y, x in zip(outs, (4, 4, 5, 5), (6, 7, 6, 7)):
                out[...] = add(kept[:, p[y], p[x]], came[:, p[y], p[x]]).astype(bf16)

        shape = ((4, self.total, STACK), bf16)
        own, to_x, to_y, to_both = small_call(
            "scatter_layer" + self.tag, kernel, self.places, self.parts, [shape] * 4
        )
        diagonal = lax.ppermute(to_both, "fsdp", [(f, f ^ 3) for f in range(16)])
        self.parts = [own, along_x(to_x), along_y(to_y), diagonal]
        self.mark = own

    def layers(self):
        def kernel(p, one, two, three, four, *outs):
            for shift, out in enumerate(outs):
                z = (p[0] + shift) % 4
                out[...] = add(one[z], two[z], three[z], four[z]).astype(out.dtype)

        own, *sends = small_call(
            "scatter_layers" + self.tag, kernel, self.places, self.parts,
            [((self.total, STACK), f32)] + [((self.total, STACK), bf16)] * 3,
        )
        self.parts = [own] + [along_z(send, shift + 1) for shift, send in enumerate(sends)]
        self.mark = own

    def finish(self):
        def kernel(p, own, first, second, third, *outs):
            value = add(own[...], first[...], second[...], third[...])
            offset = 0
            for width, out in zip(self.widths, outs):
                out[...] = value[offset : offset + width].T
                offset += width

        return small_call(
            "scatter_sum" + self.tag, kernel, self.places, self.parts,
            [((STACK, width), f32) for width in self.widths],
        )


class WholeScatter:
    def __init__(self, terms, tag):
        members = lax.axis_size(BOTH)
        packed = jnp.concatenate(
            [term.reshape(members, -1, STACK).astype(f32) for term in terms], axis=1
        )
        self.widths = [term.shape[0] // members for term in terms]
        self.summed = lax.psum_scatter(packed, BOTH, scatter_dimension=0, tiled=False)
        self.mark = terms[0]

    def wait_for(self, other):
        pass

    def layer(self):
        pass

    def layers(self):
        pass

    def finish(self):
        grads = []
        offset = 0
        for width in self.widths:
            grads.append(self.summed[offset : offset + width].T)
            offset += width
        return grads


def on_device(
    tokens,
    cotangent,
    adapter_index,
    filled,
    ln1_gain,
    ln1_shift,
    qkv_weight,
    qv_bias,
    out_weight,
    out_bias,
    ln2_gain,
    ln2_shift,
    fc1_weight,
    fc1_bias,
    fc2_weight,
    fc2_bias,
    qkv_down,
    qkv_up,
    out_down,
    out_up,
    fc1_down,
    fc1_up,
    fc2_down,
    fc2_up,
):
    images = tokens.shape[0]
    own_start = lax.axis_index("tensor") * images
    who = lax.dynamic_slice_in_dim(
        jnp.stack([adapter_index, filled]), own_start, images, 1
    )
    vectors = jnp.concatenate(
        [ln1_gain, ln1_shift, out_bias, ln2_gain, ln2_shift, fc2_bias, fc1_bias]
    ).astype(f32)[None, :]
    stack_list = (qkv_down, qkv_up, out_down, out_up, fc1_down, fc1_up, fc2_down, fc2_up)
    steps = (lax.axis_size("fsdp"), lax.axis_size("tensor"), images) == STEPS
    shards = [transposed(stacked) for stacked in stack_list]
    gather = (StepGather if steps else WholeGather)(
        qkv_weight, out_weight, fc1_weight, fc2_weight, shards
    )
    scatter = StepScatter if steps else WholeScatter
    groups = gather.groups
    tokens = untangle(tokens)
    cotangent = untangle(cotangent)
    qkv_sources, places, stacks, moves = gather.first(tokens, cotangent, vectors, who)
    q, k, v, low_one, qkv_down_full, qkv_up_full = qkv_project(
        tokens, qkv_sources, groups, places, stacks, moves, who, qv_bias, vectors
    )
    qkv_down_full = qkv_down_full.reshape(D, STACK)
    qkv_up_full = qkv_up_full.reshape(3 * D, STACK)
    q = gather.after_qkv(q)
    mixed = None
    for image in range(images):
        mixed = attend(q, k, v, image, mixed)
        if image == 0 and images > 1:
            mixed = (gather.between_images(mixed[0]), *mixed[1:])
    o, *kept = mixed
    out_sources, out_down_full, out_up_full = gather.second(o)
    h, low_out = out_project(
        tokens, o, out_sources, gather.lane, groups, out_down_full, out_up_full, who, vectors
    )
    mlp_weights, *stacks = gather.third()
    outputs, dh, grad_up2, grad_down2, grad_up1, grad_down1 = mlp(
        h, cotangent, mlp_weights, *stacks, who, vectors
    )
    do, grad_out_up, grad_out_down = out_back(
        dh, o, low_out, out_sources, gather.lane, groups, out_down_full, out_up_full, who
    )
    early = scatter(
        [grad_out_down, grad_out_up, grad_down1, grad_up1, grad_down2, grad_up2], "1"
    )
    do = after(do, early.mark)
    grads = None
    for image in range(images):
        grads = attend_back(q, k, v, do, o, kept, image, grads)
        if image == 0:
            early.wait_for(grads[0])
            early.layer()
            grads = (after(grads[0], early.mark), *grads[1:])
    dq, dk, dv = grads
    early.wait_for(dq)
    early.layers()
    dq = after(dq, early.mark)
    low_grad, grad_qkv_up, grad_qkv_down = qkv_grads(
        tokens, dq, dk, dv, low_one, qkv_up_full, who, vectors
    )
    late = scatter([grad_qkv_down, grad_qkv_up], "2")
    early_grads = early.finish()
    low_grad = after(low_grad, late.mark, early_grads[0])
    rows_grads = []
    for image in range(images):
        rows_grads.append(
            qkv_back(
                tokens, dh, dq, dk, dv, low_grad, qkv_sources, groups, qkv_down_full,
                vectors, rows_grads,
            )
        )
        if image == 0:
            late.wait_for(rows_grads[0])
            late.layer()
            rows_grads[0] = after(rows_grads[0], late.mark)
    input_grad = rows_grads[-1].transpose(1, 0, 2)
    late.layers()
    grads = [grad.reshape(ADAPTERS, RANK, -1) for grad in (*late.finish(), *early_grads)]
    return (outputs.transpose(1, 0, 2), input_grad, *grads)


def solution(mesh):
    images = P(BOTH, None, None)
    stacked = P(None, None, BOTH)
    in_specs = (
        images, images, P("fsdp"), P("fsdp"), P(), P(), P("fsdp", None, "tensor"), P(),
        P("tensor", "fsdp"), P(), P(), P(), P("fsdp", "tensor"), P(), P("tensor", "fsdp"), P(),
    ) + (stacked,) * 8
    out_specs = (images, images) + (stacked,) * 8
    return jax.shard_map(
        on_device, mesh=mesh, in_specs=in_specs, out_specs=out_specs, check_vma=False
    )
```
